256 devices in a mesh: pb: 16 (over x, z_hi), sa: 16 (over z_lo, y, core).
Axes of the slice: x: 4, y: 4, z: 8 (z_hi: 4, z_lo: 2; z = z_hi * 2 + z_lo), core: 2. Of those that a mesh axis runs over, the one named last changes fastest.
Arguments:
- question_states: bfloat16 [16, 16, 256, 768], P('pb', 'sa'), may hold values from -16 to 16
- question_ids: int32 [16, 16, 256], P('pb'), may hold values from 0 to 30521, as said below
- q_inner_weight: bfloat16 [768, 3072], P(None, 'sa'), may hold values from -0.21875 to 0.21875
- q_outer_weight: bfloat16 [3072, 768], P('sa'), may hold values from -0.109375 to 0.109375
- q_norm_gain: float32 [768], replicated, may hold values from 0.1 to 1.9
- sql_states: bfloat16 [16, 16, 256, 768], P('sa', 'pb'), may hold values from -16 to 16
- sql_ids: int32 [16, 16, 256], P('sa'), may hold values from 0 to 32099, as said below
- s_inner_weight: bfloat16 [768, 3072], P(None, 'pb'), may hold values from -0.21875 to 0.21875
- s_outer_weight: bfloat16 [3072, 768], P('pb'), may hold values from -0.109375 to 0.109375
- s_norm_gain: float32 [768], replicated, may hold values from 0.1 to 1.9
- positive_column: int32 [256], P('pb'), may hold values from 0 to 255, each once
Outputs:
- loss: float32 [], replicated
- q_inner_grad: float32 [768, 3072], P(None, 'sa')
- q_outer_grad: float32 [3072, 768], P('sa')
- q_gain_grad: float32 [768], replicated
- s_inner_grad: float32 [768, 3072], P(None, 'pb')
- s_outer_grad: float32 [3072, 768], P('pb')
- s_gain_grad: float32 [768], replicated
The draws below stay inside these ranges and needn't reach their ends.
Inputs may be any that keep to these rules, and one draw needn't show every extreme that they name: `question_ids`: each sequence is a run of nonzero ids followed by padding zeros, the run 3 * 64 long or longer. `sql_ids`: each sequence is a run of nonzero ids followed by padding zeros, the run 3 * 64 long or longer.
All inputs are finite; a program needn't handle non-finite values.
Results may differ from the reference program's by a relative error of at most 0.0051.
Values may be sent and summed in bfloat16 or wider, within the bound.
A program may use at most 128 MiB of HBM per device.

```python
import math
import jax
import jax.numpy as jnp
from jax import lax

D = 768
FF = 3072
VOCAB_Q = 30522
VOCAB_S = 32100
SEQ = 256
G_Q = 16
G_S = 16
BATCH = 256
N_PB = 16
N_SA = 16


def rough_states(key, first, shape):
    values = jax.random.normal(jax.random.fold_in(key, first), shape, jnp.float32)
    return jnp.clip(values, -6.0, 6.0)


def draw_question_states(key, part):
    shape = (N_PB, G_Q, SEQ, D)
    states = rough_states(key, 1, shape)
    return states.astype(jnp.bfloat16)


def draw_sql_states(key, part):
    shape = (N_SA, G_S, SEQ, D)
    states = rough_states(key, 7, shape)
    return states.astype(jnp.bfloat16)


def padded_ids(key, first, shape, vocab):
    shortest = 3 * SEQ // 4
    lengths = jax.random.randint(jax.random.fold_in(key, first), shape[:2] + (1,), shortest, SEQ + 1)
    lengths = lengths.at[:, 0, :].set(SEQ)
    lengths = lengths.at[:, 1, :].set(shortest)
    tokens = jax.random.randint(jax.random.fold_in(key, first + 1), shape, 1, vocab)
    tokens = tokens.at[:, 0, 0].set(vocab - 1)
    places = jnp.arange(SEQ, dtype=jnp.int32)[None, None, :]
    return jnp.where(places < lengths, tokens, 0).astype(jnp.int32)


def draw_question_ids(key, part):
    return padded_ids(key, 3, (N_PB, G_Q, SEQ), VOCAB_Q)


def draw_sql_ids(key, part):
    return padded_ids(key, 5, (N_SA, G_S, SEQ), VOCAB_S)


def levels(rng, dims, split, smallest, high):
    level = 1.0
    for axis_at, blocks in split:
        draws = jax.random.uniform(jax.random.fold_in(jax.random.fold_in(rng, 6), axis_at), (blocks,), jnp.float32, smallest / len(split), high / len(split))
        level = level * jnp.repeat(jnp.exp(draws), dims[axis_at] // blocks).reshape((-1,) + (1,) * (len(dims) - 1 - axis_at))
    return level


def bell_draw(key, dims, scale, bound, pieces=(), kind=jnp.bfloat16):
    result = scale * jax.random.normal(key, dims, jnp.float32)
    if pieces:
        result = result * levels(key, dims, pieces, -0.22, 0.18)
    return jnp.clip(result, -bound, bound).astype(kind)


def setup_inputs(seed: int = 0) -> dict:
    key_of = jax.random.split(jax.random.key(seed), 12)
    question_states = draw_question_states(jax.random.fold_in(key_of[11], 71), 0)
    question_ids = draw_question_ids(jax.random.fold_in(key_of[11], 71), 0)
    q_inner_weight = bell_draw(key_of[2], (D, FF), D ** -0.5, 0.21875, ((1, 16),))
    q_outer_weight = bell_draw(key_of[3], (FF, D), FF ** -0.5, 0.109375, ((0, 16),))
    q_norm_gain = jnp.clip(1.0 + 0.18 * jax.random.normal(key_of[4], (D,), jnp.float32), 0.1, 1.9)
    sql_states = draw_sql_states(jax.random.fold_in(key_of[11], 71), 0)
    sql_ids = draw_sql_ids(jax.random.fold_in(key_of[11], 71), 0)
    s_inner_weight = bell_draw(key_of[7], (D, FF), D ** -0.5, 0.21875, ((1, 16),))
    s_outer_weight = bell_draw(key_of[8], (FF, D), FF ** -0.5, 0.109375, ((0, 16),))
    s_norm_gain = jnp.clip(1.0 + 0.18 * jax.random.normal(key_of[9], (D,), jnp.float32), 0.1, 1.9)
    positive_column = jax.random.permutation(key_of[10], BATCH).astype(jnp.int32)
    return dict(question_states=question_states, question_ids=question_ids, q_inner_weight=q_inner_weight, q_outer_weight=q_outer_weight, q_norm_gain=q_norm_gain, sql_states=sql_states, sql_ids=sql_ids, s_inner_weight=s_inner_weight, s_outer_weight=s_outer_weight, s_norm_gain=s_norm_gain, positive_column=positive_column)


HIGH = lax.Precision.HIGHEST

def apply_rms_norm(input_float, norm_gain_vector, root_mean_square):
    if root_mean_square:
        input_normalized = input_float * lax.rsqrt(lax.optimization_barrier(jnp.mean(input_float * input_float, axis=-1, keepdims=True)) + 1e-06)
    else:
        mean_removed = input_float - lax.optimization_barrier(jnp.mean(input_float, axis=-1, keepdims=True))
        input_normalized = mean_removed * lax.rsqrt(lax.optimization_barrier(jnp.mean(mean_removed * mean_removed, axis=-1, keepdims=True)) + 1e-05)
    return (input_normalized, (input_normalized * norm_gain_vector).astype(jnp.bfloat16))

def gelu_value(v):
    return 0.5 * v * (1.0 + lax.erf(v / math.sqrt(2.0)))

def gelu_slope(v):
    return 0.5 * (1.0 + lax.erf(v / math.sqrt(2.0))) + v * jnp.exp(-0.5 * v * v) / math.sqrt(2.0 * math.pi)

def pool_weights(ids):
    mask = (ids > 0).astype(jnp.float32)
    return mask / lax.optimization_barrier(jnp.sum(mask, axis=-1, keepdims=True))

def forward_block(states, ids, inner, norm_gain_vector, root_mean_square):
    count, length, width = states.shape
    input_float = states.astype(jnp.float32).reshape(count * length, width)
    input_normalized, normalized_rows = apply_rms_norm(input_float, norm_gain_vector, root_mean_square)
    pre = jnp.dot(normalized_rows, inner, preferred_element_type=jnp.float32)
    weights = pool_weights(ids)
    hidden = gelu_value(pre).reshape(count, length, -1)
    pooled = jnp.einsum('nt,ntf->nf', weights, hidden, precision=HIGH)
    resid = jnp.einsum('nt,ntd->nd', weights, input_float.reshape(count, length, width), precision=HIGH)
    return (pooled, resid)

def backward_block(states, ids, inner, norm_gain_vector, root_mean_square, hidden_grad):
    count, length, width = states.shape
    input_float = states.astype(jnp.float32).reshape(count * length, width)
    input_normalized, normalized_rows = apply_rms_norm(input_float, norm_gain_vector, root_mean_square)
    pre = jnp.dot(normalized_rows, inner, preferred_element_type=jnp.float32)
    weights = pool_weights(ids)
    slope = gelu_slope(pre).reshape(count, length, -1)
    dpre = (weights[:, :, None] * hidden_grad[:, None, :] * slope).reshape(count * length, -1).astype(jnp.bfloat16)
    inner_layer_grad = lax.dot_general(normalized_rows, dpre, (((0,), (0,)), ((), ())), preferred_element_type=jnp.float32)
    normalized_grad = lax.dot_general(dpre, inner, (((1,), (1,)), ((), ())), preferred_element_type=jnp.float32)
    return (inner_layer_grad, lax.optimization_barrier(jnp.sum(input_normalized * normalized_grad, axis=0)))

def tower_forward(states, ids, inner, outer, norm_gain_vector, root_mean_square):
    pooled, resid = lax.map(lambda pair: forward_block(pair[0], pair[1], inner, norm_gain_vector, root_mean_square), (states, ids))
    pooled = pooled.reshape(-1, pooled.shape[-1])
    embed = resid.reshape(-1, resid.shape[-1]) + jnp.dot(pooled, outer.astype(jnp.float32), precision=HIGH)
    return (pooled, embed)

def tower_backward(states, ids, inner, outer, norm_gain_vector, root_mean_square, pooled, embed_grad):
    outer_grad = lax.dot_general(pooled, embed_grad, (((0,), (0,)), ((), ())), precision=HIGH)
    hidden_grad = lax.dot_general(embed_grad, outer.astype(jnp.float32), (((1,), (1,)), ((), ())), precision=HIGH)
    hidden_grad = hidden_grad.reshape(states.shape[0], states.shape[1], -1)

    def step(carry, item):
        inner_layer_grad, gain_grad = backward_block(item[0], item[1], inner, norm_gain_vector, root_mean_square, item[2])
        return ((carry[0] + inner_layer_grad, carry[1] + gain_grad), None)
    start = (jnp.zeros(inner.shape, jnp.float32), jnp.zeros(norm_gain_vector.shape, jnp.float32))
    totals, _ = lax.scan(step, start, (states, ids, hidden_grad))
    return (totals[0], outer_grad, totals[1])

def reference(question_states, question_ids, q_inner_weight, q_outer_weight, q_norm_gain, sql_states, sql_ids, s_inner_weight, s_outer_weight, s_norm_gain, positive_column):
    scale = 1.0 / math.sqrt(D)
    q_pooled, q_embed = tower_forward(question_states, question_ids, q_inner_weight, q_outer_weight, q_norm_gain, False)
    s_pooled, s_embed = tower_forward(sql_states, sql_ids, s_inner_weight, s_outer_weight, s_norm_gain, True)
    score = scale * jnp.dot(q_embed, s_embed.T, precision=HIGH)
    count = score.shape[0]
    match = (positive_column[:, None] == jnp.arange(count, dtype=jnp.int32)[None, :]).astype(jnp.float32)
    row_max = lax.optimization_barrier(jnp.max(score, axis=1))
    row_lse = row_max + jnp.log(lax.optimization_barrier(jnp.sum(jnp.exp(score - row_max[:, None]), axis=1)))
    col_max = lax.optimization_barrier(jnp.max(score, axis=0))
    col_lse = col_max + jnp.log(lax.optimization_barrier(jnp.sum(jnp.exp(score - col_max[None, :]), axis=0)))
    row_pos = lax.optimization_barrier(jnp.sum(match * score, axis=1))
    col_pos = lax.optimization_barrier(jnp.sum(match * score, axis=0))
    loss = (jnp.sum(row_lse - row_pos) + jnp.sum(col_lse - col_pos)) / (2.0 * count)
    dscore = 0.5 * (jnp.exp(score - row_lse[:, None]) + jnp.exp(score - col_lse[None, :]) - 2.0 * match)
    q_grad = scale * jnp.dot(dscore, s_embed, precision=HIGH)
    s_grad = scale * jnp.dot(dscore.T, q_embed, precision=HIGH)
    q_inner, q_outer, q_gain = tower_backward(question_states, question_ids, q_inner_weight, q_outer_weight, q_norm_gain, False, q_pooled, q_grad)
    s_inner, s_outer, s_gain = tower_backward(sql_states, sql_ids, s_inner_weight, s_outer_weight, s_norm_gain, True, s_pooled, s_grad)
    return (loss, q_inner, q_outer, q_gain, s_inner, s_outer, s_gain)
```

```python
import math

import jax
import jax.numpy as jnp
from jax import lax
from jax.sharding import PartitionSpec as P

D = 768


HIGH = lax.Precision.HIGHEST


def apply_rms_norm(input_float, norm_gain_vector, root_mean_square):
    if root_mean_square:
        input_normalized = input_float * lax.rsqrt(
            jnp.mean(input_float * input_float, axis=-1, keepdims=True) + 1e-06
        )
    else:
        mean_removed = input_float - jnp.mean(input_float, axis=-1, keepdims=True)
        input_normalized = mean_removed * lax.rsqrt(
            jnp.mean(mean_removed * mean_removed, axis=-1, keepdims=True) + 1e-05
        )
    return (input_normalized, (input_normalized * norm_gain_vector).astype(jnp.bfloat16))


def gelu_value(v):
    return 0.5 * v * (1.0 + lax.erf(v / math.sqrt(2.0)))


def gelu_slope(v):
    return 0.5 * (1.0 + lax.erf(v / math.sqrt(2.0))) + v * jnp.exp(-0.5 * v * v) / math.sqrt(
        2.0 * math.pi
    )


def pool_weights(ids):
    mask = (ids > 0).astype(jnp.float32)
    return mask / jnp.sum(mask, axis=-1, keepdims=True)


def tower_forward(tokens, ids, inner, gain, root_mean_square):
    count, length, width = tokens.shape
    input_float = tokens.astype(jnp.float32).reshape(count * length, width)
    input_normalized, normalized_rows = apply_rms_norm(input_float, gain, root_mean_square)
    pre = jnp.dot(normalized_rows, inner, preferred_element_type=jnp.float32)
    weights = pool_weights(ids)
    hidden = gelu_value(pre).reshape(count, length, -1)
    pooled = jnp.einsum("nt,ntf->nf", weights, hidden, precision=HIGH)
    resid = jnp.einsum(
        "nt,ntd->nd", weights, input_float.reshape(count, length, width), precision=HIGH
    )
    return input_normalized, normalized_rows, pre, weights, pooled, resid


def tower_backward(input_normalized, normalized_rows, pre, weights, inner, hidden_grad):
    count, length = weights.shape
    slope = gelu_slope(pre).reshape(count, length, -1)
    dpre = (
        (weights[:, :, None] * hidden_grad[:, None, :] * slope)
        .reshape(count * length, -1)
        .astype(jnp.bfloat16)
    )
    inner_part = lax.dot_general(
        normalized_rows, dpre, (((0,), (0,)), ((), ())), preferred_element_type=jnp.float32
    )
    normalized_grad = lax.dot_general(
        dpre, inner, (((1,), (1,)), ((), ())), preferred_element_type=jnp.float32
    )
    return inner_part, jnp.sum(input_normalized * normalized_grad, axis=0)


def per_device(
    question_states,
    question_ids,
    q_inner_weight,
    q_outer_weight,
    q_norm_gain,
    sql_states,
    sql_ids,
    s_inner_weight,
    s_outer_weight,
    s_norm_gain,
    positive_column,
):
    scale = 1.0 / math.sqrt(D)
    q_place = lax.axis_index("sa")
    s_place = lax.axis_index("pb")
    q_tokens = lax.all_gather(question_states, "sa", axis=1, tiled=True)[0]
    s_tokens = lax.all_gather(sql_states, "pb", axis=1, tiled=True)[0]
    q_rows = q_tokens.shape[0]
    s_rows = s_tokens.shape[0]

    q_hat, q_normed, q_pre, q_weights, q_pooled, q_resid = tower_forward(
        q_tokens, question_ids[0], q_inner_weight, q_norm_gain, False
    )
    s_hat, s_normed, s_pre, s_weights, s_pooled, s_resid = tower_forward(
        s_tokens, sql_ids[0], s_inner_weight, s_norm_gain, True
    )
    q_outer_f = q_outer_weight.astype(jnp.float32)
    s_outer_f = s_outer_weight.astype(jnp.float32)
    q_block = lax.psum(jnp.dot(q_pooled, q_outer_f, precision=HIGH), "sa") + q_resid
    s_block = lax.psum(jnp.dot(s_pooled, s_outer_f, precision=HIGH), "pb") + s_resid
    q_embed = lax.all_gather(q_block, "pb", axis=0, tiled=True)
    s_embed = lax.all_gather(s_block, "sa", axis=0, tiled=True)
    q_pooled_all = lax.all_gather(q_pooled, "pb", axis=0, tiled=True)
    s_pooled_all = lax.all_gather(s_pooled, "sa", axis=0, tiled=True)
    positive_all = lax.all_gather(positive_column, "pb", axis=0, tiled=True)

    score = scale * lax.dot_general(q_embed, s_embed, (((1,), (1,)), ((), ())), precision=HIGH)
    count = score.shape[0]
    match = (positive_all[:, None] == jnp.arange(count, dtype=jnp.int32)[None, :]).astype(
        jnp.float32
    )
    row_max = jnp.max(score, axis=1)
    row_lse = row_max + jnp.log(jnp.sum(jnp.exp(score - row_max[:, None]), axis=1))
    col_max = jnp.max(score, axis=0)
    col_lse = col_max + jnp.log(jnp.sum(jnp.exp(score - col_max[None, :]), axis=0))
    row_pos = jnp.sum(match * score, axis=1)
    col_pos = jnp.sum(match * score, axis=0)
    loss = (jnp.sum(row_lse - row_pos) + jnp.sum(col_lse - col_pos)) / (2.0 * count)
    dscore = 0.5 * (
        jnp.exp(score - row_lse[:, None]) + jnp.exp(score - col_lse[None, :]) - 2.0 * match
    )
    q_grad = scale * jnp.dot(dscore, s_embed, precision=HIGH)
    s_grad = scale * lax.dot_general(dscore, q_embed, (((0,), (0,)), ((), ())), precision=HIGH)

    q_outer_grad = lax.dot_general(q_pooled_all, q_grad, (((0,), (0,)), ((), ())), precision=HIGH)
    s_outer_grad = lax.dot_general(s_pooled_all, s_grad, (((0,), (0,)), ((), ())), precision=HIGH)
    q_grad_own = lax.dynamic_slice_in_dim(q_grad, s_place * q_rows, q_rows, 0)
    s_grad_own = lax.dynamic_slice_in_dim(s_grad, q_place * s_rows, s_rows, 0)
    q_hidden_grad = lax.dot_general(
        q_grad_own, q_outer_f, (((1,), (1,)), ((), ())), precision=HIGH
    )
    s_hidden_grad = lax.dot_general(
        s_grad_own, s_outer_f, (((1,), (1,)), ((), ())), precision=HIGH
    )
    q_inner_part, q_gain_part = tower_backward(
        q_hat, q_normed, q_pre, q_weights, q_inner_weight, q_hidden_grad
    )
    s_inner_part, s_gain_part = tower_backward(
        s_hat, s_normed, s_pre, s_weights, s_inner_weight, s_hidden_grad
    )
    q_inner_grad = lax.psum(q_inner_part, "pb")
    s_inner_grad = lax.psum(s_inner_part, "sa")
    q_gain_grad, s_gain_grad = lax.psum((q_gain_part, s_gain_part), ("pb", "sa"))
    return (loss, q_inner_grad, q_outer_grad, q_gain_grad, s_inner_grad, s_outer_grad, s_gain_grad)


def solution(mesh):
    placed = (
        P("pb", "sa", None, None),
        P("pb", None, None),
        P(None, "sa"),
        P("sa", None),
        P(),
        P("sa", "pb", None, None),
        P("sa", None, None),
        P(None, "pb"),
        P("pb", None),
        P(),
        P("pb"),
    )
    return jax.shard_map(
        per_device,
        mesh=mesh,
        in_specs=placed,
        out_specs=(P(), P(None, "sa"), P("sa", None), P(), P(None, "pb"), P("pb", None), P()),
        check_vma=False,
    )
```

```python
import functools
import math

import jax
import jax.numpy as jnp
from jax import lax
from jax.experimental import pallas as pl
from jax.experimental.pallas import tpu as pltpu
from jax.sharding import PartitionSpec as P

D = 768

MESH_AXES = ("pb", "sa")


def _peer(axis, p):
    return tuple(p if a == axis else lax.axis_index(a) for a in MESH_AXES)


def exchange(jobs, cid):
    arrays = [a for a, _, _ in jobs]
    kinds = [(ax, spread) for _, ax, spread in jobs]
    sizes = {ax: lax.axis_size(ax) for ax, _ in kinds}
    widest = max(sizes.values())
    count = len(jobs)

    def kernel(*refs):
        srcs, dsts = refs[:count], refs[count:2 * count]
        send, recv, local = refs[2 * count:]
        barrier = pltpu.get_barrier_semaphore()
        axes = list(dict.fromkeys(ax for ax, _ in kinds))
        total = 0
        for ax in axes:
            n = sizes[ax]
            me = lax.axis_index(ax)
            for s in range(1, n):
                pl.semaphore_signal(barrier, 1, device_id=_peer(ax, lax.rem(me + s, n)),
                                    device_id_type=pl.DeviceIdType.MESH)
            total += n - 1
        pl.semaphore_wait(barrier, total)
        started = []
        for t, (ax, spread) in enumerate(kinds):
            n = sizes[ax]
            me = lax.axis_index(ax)
            for s in range(1, n):
                p = lax.rem(me + s, n)
                src = srcs[t].at[p] if spread else srcs[t]
                c = pltpu.make_async_remote_copy(
                    src_ref=src, dst_ref=dsts[t].at[me], send_sem=send.at[t, s],
                    recv_sem=recv.at[t, s], device_id=_peer(ax, p),
                    device_id_type=pl.DeviceIdType.MESH)
                c.start()
                started.append(c)
            src = srcs[t].at[me] if spread else srcs[t]
            c = pltpu.make_async_copy(src, dsts[t].at[me], local.at[t])
            c.start()
            started.append(c)
        for c in started:
            c.wait()

    out_shape = []
    for a, (ax, spread) in zip(arrays, kinds):
        shape = a.shape if spread else (sizes[ax],) + a.shape
        out_shape.append(jax.ShapeDtypeStruct(shape, a.dtype))
    anywhere = pl.BlockSpec(memory_space=pl.ANY)
    return pl.pallas_call(
        kernel,
        out_shape=out_shape,
        in_specs=[anywhere] * count,
        out_specs=[anywhere] * count,
        scratch_shapes=[
            pltpu.SemaphoreType.DMA((count, widest)),
            pltpu.SemaphoreType.DMA((count, widest)),
            pltpu.SemaphoreType.DMA((count,)),
        ],
        compiler_params=pltpu.CompilerParams(collective_id=cid, has_side_effects=True),
    )(*arrays)


HIGH = lax.Precision.HIGHEST


def apply_rms_norm(input_float, norm_gain_vector, root_mean_square):
    if root_mean_square:
        input_normalized = input_float * lax.rsqrt(
            jnp.mean(input_float * input_float, axis=-1, keepdims=True) + 1e-06
        )
    else:
        mean_removed = input_float - jnp.mean(input_float, axis=-1, keepdims=True)
        input_normalized = mean_removed * lax.rsqrt(
            jnp.mean(mean_removed * mean_removed, axis=-1, keepdims=True) + 1e-05
        )
    return (input_normalized, (input_normalized * norm_gain_vector).astype(jnp.bfloat16))


def gelu_value(v):
    return 0.5 * v * (1.0 + lax.erf(v / math.sqrt(2.0)))


def gelu_slope(v):
    return 0.5 * (1.0 + lax.erf(v / math.sqrt(2.0))) + v * jnp.exp(-0.5 * v * v) / math.sqrt(
        2.0 * math.pi
    )


def pool_weights(ids):
    mask = (ids > 0).astype(jnp.float32)
    return mask / jnp.sum(mask, axis=-1, keepdims=True)


def tower_forward(tokens, ids, inner, gain, root_mean_square):
    count, length, width = tokens.shape
    input_float = tokens.astype(jnp.float32).reshape(count * length, width)
    input_normalized, normalized_rows = apply_rms_norm(input_float, gain, root_mean_square)
    pre = jnp.dot(normalized_rows, inner, preferred_element_type=jnp.float32)
    weights = pool_weights(ids)
    hidden = gelu_value(pre).reshape(count, length, -1)
    pooled = jnp.einsum("nt,ntf->nf", weights, hidden, precision=HIGH)
    resid = jnp.einsum(
        "nt,ntd->nd", weights, input_float.reshape(count, length, width), precision=HIGH
    )
    return input_normalized, normalized_rows, pre, weights, pooled, resid


def tower_backward(input_normalized, normalized_rows, pre, weights, inner, hidden_grad):
    count, length = weights.shape
    slope = gelu_slope(pre).reshape(count, length, -1)
    dpre = (
        (weights[:, :, None] * hidden_grad[:, None, :] * slope)
        .reshape(count * length, -1)
        .astype(jnp.bfloat16)
    )
    inner_part = lax.dot_general(
        normalized_rows, dpre, (((0,), (0,)), ((), ())), preferred_element_type=jnp.float32
    )
    normalized_grad = lax.dot_general(
        dpre, inner, (((1,), (1,)), ((), ())), preferred_element_type=jnp.float32
    )
    return inner_part, jnp.sum(input_normalized * normalized_grad, axis=0)


def per_device(
    question_states,
    question_ids,
    q_inner_weight,
    q_outer_weight,
    q_norm_gain,
    sql_states,
    sql_ids,
    s_inner_weight,
    s_outer_weight,
    s_norm_gain,
    positive_column,
):
    scale = 1.0 / math.sqrt(D)
    q_place = lax.axis_index("sa")
    s_place = lax.axis_index("pb")
    q_tokens, s_tokens, positive_all = exchange(
        [
            (question_states[0, 0], "sa", False),
            (sql_states[0, 0], "pb", False),
            (positive_column.reshape(1, -1), "pb", False),
        ],
        0,
    )
    positive_all = positive_all.reshape(-1)
    q_rows = q_tokens.shape[0]
    s_rows = s_tokens.shape[0]

    q_hat, q_normed, q_pre, q_weights, q_pooled, q_resid = tower_forward(
        q_tokens, question_ids[0], q_inner_weight, q_norm_gain, False
    )
    s_hat, s_normed, s_pre, s_weights, s_pooled, s_resid = tower_forward(
        s_tokens, sql_ids[0], s_inner_weight, s_norm_gain, True
    )
    q_outer_f = q_outer_weight.astype(jnp.float32)
    s_outer_f = s_outer_weight.astype(jnp.float32)
    q_terms, s_terms = exchange(
        [
            (jnp.dot(q_pooled, q_outer_f, precision=HIGH), "sa", False),
            (jnp.dot(s_pooled, s_outer_f, precision=HIGH), "pb", False),
        ],
        1,
    )
    q_block = jnp.sum(q_terms, axis=0) + q_resid
    s_block = jnp.sum(s_terms, axis=0) + s_resid
    q_embed, q_pooled_all, s_embed, s_pooled_all = exchange(
        [
            (q_block, "pb", False),
            (q_pooled, "pb", False),
            (s_block, "sa", False),
            (s_pooled, "sa", False),
        ],
        2,
    )
    q_embed = q_embed.reshape(-1, D)
    s_embed = s_embed.reshape(-1, D)
    q_pooled_all = q_pooled_all.reshape(-1, q_pooled.shape[-1])
    s_pooled_all = s_pooled_all.reshape(-1, s_pooled.shape[-1])
    score = scale * lax.dot_general(q_embed, s_embed, (((1,), (1,)), ((), ())), precision=HIGH)
    count = score.shape[0]
    match = (positive_all[:, None] == jnp.arange(count, dtype=jnp.int32)[None, :]).astype(
        jnp.float32
    )
    row_max = jnp.max(score, axis=1)
    row_lse = row_max + jnp.log(jnp.sum(jnp.exp(score - row_max[:, None]), axis=1))
    col_max = jnp.max(score, axis=0)
    col_lse = col_max + jnp.log(jnp.sum(jnp.exp(score - col_max[None, :]), axis=0))
    row_pos = jnp.sum(match * score, axis=1)
    col_pos = jnp.sum(match * score, axis=0)
    loss = (jnp.sum(row_lse - row_pos) + jnp.sum(col_lse - col_pos)) / (2.0 * count)
    dscore = 0.5 * (
        jnp.exp(score - row_lse[:, None]) + jnp.exp(score - col_lse[None, :]) - 2.0 * match
    )
    q_grad = scale * jnp.dot(dscore, s_embed, precision=HIGH)
    s_grad = scale * lax.dot_general(dscore, q_embed, (((0,), (0,)), ((), ())), precision=HIGH)

    q_outer_grad = lax.dot_general(q_pooled_all, q_grad, (((0,), (0,)), ((), ())), precision=HIGH)
    s_outer_grad = lax.dot_general(s_pooled_all, s_grad, (((0,), (0,)), ((), ())), precision=HIGH)
    q_grad_own = lax.dynamic_slice_in_dim(q_grad, s_place * q_rows, q_rows, 0)
    s_grad_own = lax.dynamic_slice_in_dim(s_grad, q_place * s_rows, s_rows, 0)
    q_hidden_grad = lax.dot_general(
        q_grad_own, q_outer_f, (((1,), (1,)), ((), ())), precision=HIGH
    )
    s_hidden_grad = lax.dot_general(
        s_grad_own, s_outer_f, (((1,), (1,)), ((), ())), precision=HIGH
    )
    q_inner_part, q_gain_part = tower_backward(
        q_hat, q_normed, q_pre, q_weights, q_inner_weight, q_hidden_grad
    )
    s_inner_part, s_gain_part = tower_backward(
        s_hat, s_normed, s_pre, s_weights, s_inner_weight, s_hidden_grad
    )
    q_pieces = q_inner_part.reshape(lax.axis_size("pb"), -1, q_inner_part.shape[-1])
    s_pieces = s_inner_part.reshape(lax.axis_size("sa"), -1, s_inner_part.shape[-1])
    gains = jnp.stack([q_gain_part, s_gain_part])
    q_pieces, s_pieces, gains = exchange(
        [(q_pieces, "pb", True), (s_pieces, "sa", True), (gains, "sa", False)], 3
    )
    q_inner_grad, s_inner_grad, gains = exchange(
        [
            (jnp.sum(q_pieces, axis=0), "pb", False),
            (jnp.sum(s_pieces, axis=0), "sa", False),
            (jnp.sum(gains, axis=0), "pb", False),
        ],
        4,
    )
    q_inner_grad = q_inner_grad.reshape(q_inner_part.shape)
    s_inner_grad = s_inner_grad.reshape(s_inner_part.shape)
    gains = jnp.sum(gains, axis=0)
    q_gain_grad, s_gain_grad = gains[0], gains[1]
    return (loss, q_inner_grad, q_outer_grad, q_gain_grad, s_inner_grad, s_outer_grad, s_gain_grad)


def solution(mesh):
    placed = (
        P("pb", "sa", None, None),
        P("pb", None, None),
        P(None, "sa"),
        P("sa", None),
        P(),
        P("sa", "pb", None, None),
        P("sa", None, None),
        P(None, "pb"),
        P("pb", None),
        P(),
        P("pb"),
    )
    return jax.shard_map(
        per_device,
        mesh=mesh,
        in_specs=placed,
        out_specs=(P(), P(None, "sa"), P("sa", None), P(), P(None, "pb"), P("pb", None), P()),
        check_vma=False,
    )
```

```python
import functools
import math

import jax
import jax.numpy as jnp
from jax import lax
from jax.experimental import pallas as pl
from jax.experimental.pallas import tpu as pltpu
from jax.sharding import PartitionSpec as P

D = 768

MESH_AXES = ("pb", "sa")


def _peer(axis, p):
    return tuple(p if a == axis else lax.axis_index(a) for a in MESH_AXES)


def exchange(jobs, cid):
    arrays = [a for a, _, _ in jobs]
    kinds = [(ax, spread) for _, ax, spread in jobs]
    sizes = {ax: lax.axis_size(ax) for ax, _ in kinds}
    widest = max(sizes.values())
    count = len(jobs)

    def kernel(*refs):
        srcs, dsts = refs[:count], refs[count:2 * count]
        send, recv, local = refs[2 * count:]
        barrier = pltpu.get_barrier_semaphore()
        axes = list(dict.fromkeys(ax for ax, _ in kinds))
        total = 0
        for ax in axes:
            n = sizes[ax]
            me = lax.axis_index(ax)
            for s in range(1, n):
                pl.semaphore_signal(barrier, 1, device_id=_peer(ax, lax.rem(me + s, n)),
                                    device_id_type=pl.DeviceIdType.MESH)
            total += n - 1
        pl.semaphore_wait(barrier, total)
        started = []
        for t, (ax, spread) in enumerate(kinds):
            n = sizes[ax]
            me = lax.axis_index(ax)
            for s in range(1, n):
                p = lax.rem(me + s, n)
                src = srcs[t].at[p] if spread else srcs[t]
                c = pltpu.make_async_remote_copy(
                    src_ref=src, dst_ref=dsts[t].at[me], send_sem=send.at[t, s],
                    recv_sem=recv.at[t, s], device_id=_peer(ax, p),
                    device_id_type=pl.DeviceIdType.MESH)
                c.start()
                started.append(c)
            src = srcs[t].at[me] if spread else srcs[t]
            c = pltpu.make_async_copy(src, dsts[t].at[me], local.at[t])
            c.start()
            started.append(c)
        for c in started:
            c.wait()

    out_shape = []
    for a, (ax, spread) in zip(arrays, kinds):
        shape = a.shape if spread else (sizes[ax],) + a.shape
        out_shape.append(jax.ShapeDtypeStruct(shape, a.dtype))
    anywhere = pl.BlockSpec(memory_space=pl.ANY)
    return pl.pallas_call(
        kernel,
        out_shape=out_shape,
        in_specs=[anywhere] * count,
        out_specs=[anywhere] * count,
        scratch_shapes=[
            pltpu.SemaphoreType.DMA((count, widest)),
            pltpu.SemaphoreType.DMA((count, widest)),
            pltpu.SemaphoreType.DMA((count,)),
        ],
        compiler_params=pltpu.CompilerParams(collective_id=cid, has_side_effects=True),
    )(*arrays)


HIGH = lax.Precision.HIGHEST


def apply_rms_norm(input_float, norm_gain_vector, root_mean_square):
    if root_mean_square:
        input_normalized = input_float * lax.rsqrt(
            jnp.mean(input_float * input_float, axis=-1, keepdims=True) + 1e-06
        )
    else:
        mean_removed = input_float - jnp.mean(input_float, axis=-1, keepdims=True)
        input_normalized = mean_removed * lax.rsqrt(
            jnp.mean(mean_removed * mean_removed, axis=-1, keepdims=True) + 1e-05
        )
    return (input_normalized, (input_normalized * norm_gain_vector).astype(jnp.bfloat16))


def gelu_value(v):
    return 0.5 * v * (1.0 + lax.erf(v / math.sqrt(2.0)))


def gelu_slope(v):
    return 0.5 * (1.0 + lax.erf(v / math.sqrt(2.0))) + v * jnp.exp(-0.5 * v * v) / math.sqrt(
        2.0 * math.pi
    )


def pool_weights(ids):
    mask = (ids > 0).astype(jnp.float32)
    return mask / jnp.sum(mask, axis=-1, keepdims=True)


def tower_forward(tokens, ids, inner, gain, root_mean_square):
    count, length, width = tokens.shape
    input_float = tokens.astype(jnp.float32).reshape(count * length, width)
    input_normalized, normalized_rows = apply_rms_norm(input_float, gain, root_mean_square)
    pre = jnp.dot(normalized_rows, inner, preferred_element_type=jnp.float32)
    weights = pool_weights(ids)
    hidden = gelu_value(pre).reshape(count, length, -1)
    pooled = jnp.einsum("nt,ntf->nf", weights, hidden, precision=HIGH)
    resid = jnp.einsum(
        "nt,ntd->nd", weights, input_float.reshape(count, length, width), precision=HIGH
    )
    return input_normalized, normalized_rows, pre, weights, pooled, resid


def tower_backward(input_normalized, normalized_rows, pre, weights, inner, hidden_grad):
    count, length = weights.shape
    slope = gelu_slope(pre).reshape(count, length, -1)
    dpre = (
        (weights[:, :, None] * hidden_grad[:, None, :] * slope)
        .reshape(count * length, -1)
        .astype(jnp.bfloat16)
    )
    inner_part = lax.dot_general(
        normalized_rows, dpre, (((0,), (0,)), ((), ())), preferred_element_type=jnp.float32
    )
    normalized_grad = lax.dot_general(
        dpre, inner, (((1,), (1,)), ((), ())), preferred_element_type=jnp.float32
    )
    return inner_part, jnp.sum(input_normalized * normalized_grad, axis=0)


def per_device(
    question_states,
    question_ids,
    q_inner_weight,
    q_outer_weight,
    q_norm_gain,
    sql_states,
    sql_ids,
    s_inner_weight,
    s_outer_weight,
    s_norm_gain,
    positive_column,
):
    scale = 1.0 / math.sqrt(D)
    q_place = lax.axis_index("sa")
    s_place = lax.axis_index("pb")
    q_tokens = lax.all_gather(question_states, "sa", axis=1, tiled=True)[0]
    s_tokens = lax.all_gather(sql_states, "pb", axis=1, tiled=True)[0]
    (positive_all,) = exchange([(positive_column.reshape(1, -1), "pb", False)], 0)
    positive_all = positive_all.reshape(-1)
    q_rows = q_tokens.shape[0]
    s_rows = s_tokens.shape[0]

    q_hat, q_normed, q_pre, q_weights, q_pooled, q_resid = tower_forward(
        q_tokens, question_ids[0], q_inner_weight, q_norm_gain, False
    )
    s_hat, s_normed, s_pre, s_weights, s_pooled, s_resid = tower_forward(
        s_tokens, sql_ids[0], s_inner_weight, s_norm_gain, True
    )
    q_outer_f = q_outer_weight.astype(jnp.float32)
    s_outer_f = s_outer_weight.astype(jnp.float32)
    q_terms, s_terms = exchange(
        [
            (jnp.dot(q_pooled, q_outer_f, precision=HIGH), "sa", False),
            (jnp.dot(s_pooled, s_outer_f, precision=HIGH), "pb", False),
        ],
        1,
    )
    q_block = jnp.sum(q_terms, axis=0) + q_resid
    s_block = jnp.sum(s_terms, axis=0) + s_resid
    q_embed, q_pooled_all, s_embed, s_pooled_all = exchange(
        [
            (q_block, "pb", False),
            (q_pooled, "pb", False),
            (s_block, "sa", False),
            (s_pooled, "sa", False),
        ],
        2,
    )
    q_embed = q_embed.reshape(-1, D)
    s_embed = s_embed.reshape(-1, D)
    q_pooled_all = q_pooled_all.reshape(-1, q_pooled.shape[-1])
    s_pooled_all = s_pooled_all.reshape(-1, s_pooled.shape[-1])
    score = scale * lax.dot_general(q_embed, s_embed, (((1,), (1,)), ((), ())), precision=HIGH)
    count = score.shape[0]
    match = (positive_all[:, None] == jnp.arange(count, dtype=jnp.int32)[None, :]).astype(
        jnp.float32
    )
    row_max = jnp.max(score, axis=1)
    row_lse = row_max + jnp.log(jnp.sum(jnp.exp(score - row_max[:, None]), axis=1))
    col_max = jnp.max(score, axis=0)
    col_lse = col_max + jnp.log(jnp.sum(jnp.exp(score - col_max[None, :]), axis=0))
    row_pos = jnp.sum(match * score, axis=1)
    col_pos = jnp.sum(match * score, axis=0)
    loss = (jnp.sum(row_lse - row_pos) + jnp.sum(col_lse - col_pos)) / (2.0 * count)
    dscore = 0.5 * (
        jnp.exp(score - row_lse[:, None]) + jnp.exp(score - col_lse[None, :]) - 2.0 * match
    )
    q_grad = scale * jnp.dot(dscore, s_embed, precision=HIGH)
    s_grad = scale * lax.dot_general(dscore, q_embed, (((0,), (0,)), ((), ())), precision=HIGH)

    q_outer_grad = lax.dot_general(q_pooled_all, q_grad, (((0,), (0,)), ((), ())), precision=HIGH)
    s_outer_grad = lax.dot_general(s_pooled_all, s_grad, (((0,), (0,)), ((), ())), precision=HIGH)
    q_grad_own = lax.dynamic_slice_in_dim(q_grad, s_place * q_rows, q_rows, 0)
    s_grad_own = lax.dynamic_slice_in_dim(s_grad, q_place * s_rows, s_rows, 0)
    q_hidden_grad = lax.dot_general(
        q_grad_own, q_outer_f, (((1,), (1,)), ((), ())), precision=HIGH
    )
    s_hidden_grad = lax.dot_general(
        s_grad_own, s_outer_f, (((1,), (1,)), ((), ())), precision=HIGH
    )
    q_inner_part, q_gain_part = tower_backward(
        q_hat, q_normed, q_pre, q_weights, q_inner_weight, q_hidden_grad
    )
    s_inner_part, s_gain_part = tower_backward(
        s_hat, s_normed, s_pre, s_weights, s_inner_weight, s_hidden_grad
    )
    q_pieces = q_inner_part.reshape(lax.axis_size("pb"), -1, q_inner_part.shape[-1])
    s_pieces = s_inner_part.reshape(lax.axis_size("sa"), -1, s_inner_part.shape[-1])
    gains = jnp.stack([q_gain_part, s_gain_part])
    q_pieces, s_pieces, gains = exchange(
        [(q_pieces, "pb", True), (s_pieces, "sa", True), (gains, "sa", False)], 3
    )
    q_inner_grad, s_inner_grad, gains = exchange(
        [
            (jnp.sum(q_pieces, axis=0), "pb", False),
            (jnp.sum(s_pieces, axis=0), "sa", False),
            (jnp.sum(gains, axis=0), "pb", False),
        ],
        4,
    )
    q_inner_grad = q_inner_grad.reshape(q_inner_part.shape)
    s_inner_grad = s_inner_grad.reshape(s_inner_part.shape)
    gains = jnp.sum(gains, axis=0)
    q_gain_grad, s_gain_grad = gains[0], gains[1]
    return (loss, q_inner_grad, q_outer_grad, q_gain_grad, s_inner_grad, s_outer_grad, s_gain_grad)


def solution(mesh):
    placed = (
        P("pb", "sa", None, None),
        P("pb", None, None),
        P(None, "sa"),
        P("sa", None),
        P(),
        P("sa", "pb", None, None),
        P("sa", None, None),
        P(None, "pb"),
        P("pb", None),
        P(),
        P("pb"),
    )
    return jax.shard_map(
        per_device,
        mesh=mesh,
        in_specs=placed,
        out_specs=(P(), P(None, "sa"), P("sa", None), P(), P(None, "pb"), P("pb", None), P()),
        check_vma=False,
    )
```

```python
import functools
import math

import jax
import jax.numpy as jnp
from jax import lax
from jax.experimental import pallas as pl
from jax.experimental.pallas import tpu as pltpu
from jax.sharding import PartitionSpec as P

D = 768

MESH_AXES = ("pb", "sa")


def _peer(axis, p):
    return tuple(p if a == axis else lax.axis_index(a) for a in MESH_AXES)


def exchange(jobs, cid):
    arrays = [a for a, _, _ in jobs]
    kinds = [(ax, spread) for _, ax, spread in jobs]
    sizes = {ax: lax.axis_size(ax) for ax, _ in kinds}
    widest = max(sizes.values())
    count = len(jobs)

    def kernel(*refs):
        srcs, dsts = refs[:count], refs[count:2 * count]
        send, recv, local = refs[2 * count:]
        barrier = pltpu.get_barrier_semaphore()
        axes = list(dict.fromkeys(ax for ax, _ in kinds))
        total = 0
        for ax in axes:
            n = sizes[ax]
            me = lax.axis_index(ax)
            for s in range(1, n):
                pl.semaphore_signal(barrier, 1, device_id=_peer(ax, lax.rem(me + s, n)),
                                    device_id_type=pl.DeviceIdType.MESH)
            total += n - 1
        pl.semaphore_wait(barrier, total)
        started = []
        for t, (ax, spread) in enumerate(kinds):
            n = sizes[ax]
            me = lax.axis_index(ax)
            for s in range(1, n):
                p = lax.rem(me + s, n)
                src = srcs[t].at[p] if spread else srcs[t]
                c = pltpu.make_async_remote_copy(
                    src_ref=src, dst_ref=dsts[t].at[me], send_sem=send.at[t, s],
                    recv_sem=recv.at[t, s], device_id=_peer(ax, p),
                    device_id_type=pl.DeviceIdType.MESH)
                c.start()
                started.append(c)
            src = srcs[t].at[me] if spread else srcs[t]
            c = pltpu.make_async_copy(src, dsts[t].at[me], local.at[t])
            c.start()
            started.append(c)
        for c in started:
            c.wait()

    out_shape = []
    for a, (ax, spread) in zip(arrays, kinds):
        shape = a.shape if spread else (sizes[ax],) + a.shape
        out_shape.append(jax.ShapeDtypeStruct(shape, a.dtype))
    anywhere = pl.BlockSpec(memory_space=pl.ANY)
    return pl.pallas_call(
        kernel,
        out_shape=out_shape,
        in_specs=[anywhere] * count,
        out_specs=[anywhere] * count,
        scratch_shapes=[
            pltpu.SemaphoreType.DMA((count, widest)),
            pltpu.SemaphoreType.DMA((count, widest)),
            pltpu.SemaphoreType.DMA((count,)),
        ],
        compiler_params=pltpu.CompilerParams(collective_id=cid, has_side_effects=True),
    )(*arrays)


HIGH = lax.Precision.HIGHEST


def apply_rms_norm(input_float, norm_gain_vector, root_mean_square):
    if root_mean_square:
        input_normalized = input_float * lax.rsqrt(
            jnp.mean(input_float * input_float, axis=-1, keepdims=True) + 1e-06
        )
    else:
        mean_removed = input_float - jnp.mean(input_float, axis=-1, keepdims=True)
        input_normalized = mean_removed * lax.rsqrt(
            jnp.mean(mean_removed * mean_removed, axis=-1, keepdims=True) + 1e-05
        )
    return (input_normalized, (input_normalized * norm_gain_vector).astype(jnp.bfloat16))


def gelu_value(v):
    return 0.5 * v * (1.0 + lax.erf(v / math.sqrt(2.0)))


def gelu_slope(v):
    return 0.5 * (1.0 + lax.erf(v / math.sqrt(2.0))) + v * jnp.exp(-0.5 * v * v) / math.sqrt(
        2.0 * math.pi
    )


def pool_weights(ids):
    mask = (ids > 0).astype(jnp.float32)
    return mask / jnp.sum(mask, axis=-1, keepdims=True)


def tower_forward(tokens, ids, inner, gain, root_mean_square):
    count, length, width = tokens.shape
    input_float = tokens.astype(jnp.float32).reshape(count * length, width)
    input_normalized, normalized_rows = apply_rms_norm(input_float, gain, root_mean_square)
    pre = jnp.dot(normalized_rows, inner, preferred_element_type=jnp.float32)
    weights = pool_weights(ids)
    hidden = gelu_value(pre).reshape(count, length, -1)
    pooled = jnp.einsum("nt,ntf->nf", weights, hidden, precision=HIGH)
    resid = jnp.einsum(
        "nt,ntd->nd", weights, input_float.reshape(count, length, width), precision=HIGH
    )
    return input_normalized, normalized_rows, pre, weights, pooled, resid


def tower_backward(input_normalized, normalized_rows, pre, weights, inner, hidden_grad):
    count, length = weights.shape
    width = normalized_rows.shape[-1]
    slope = gelu_slope(pre).reshape(count, length, -1)
    dpre = (
        (weights[:, :, None] * hidden_grad[:, None, :] * slope)
        .reshape(count * length, -1)
        .astype(jnp.bfloat16)
    )
    high = input_normalized.astype(jnp.bfloat16)
    low = (input_normalized - high.astype(jnp.float32)).astype(jnp.bfloat16)
    rows = jnp.concatenate([normalized_rows, high, low], axis=1)
    both = lax.dot_general(
        dpre, rows, (((0,), (0,)), ((), ())), preferred_element_type=jnp.float32
    )
    inner_part = both[:, :width].T
    moment = both[:, width : 2 * width] + both[:, 2 * width :]
    gain_part = jnp.sum(inner.astype(jnp.float32).T * moment, axis=0)
    return inner_part, gain_part


def per_device(
    question_states,
    question_ids,
    q_inner_weight,
    q_outer_weight,
    q_norm_gain,
    sql_states,
    sql_ids,
    s_inner_weight,
    s_outer_weight,
    s_norm_gain,
    positive_column,
):
    scale = 1.0 / math.sqrt(D)
    q_place = lax.axis_index("sa")
    s_place = lax.axis_index("pb")
    q_tokens = lax.all_gather(question_states, "sa", axis=1, tiled=True)[0]
    s_tokens = lax.all_gather(sql_states, "pb", axis=1, tiled=True)[0]
    (positive_all,) = exchange([(positive_column.reshape(1, -1), "pb", False)], 0)
    positive_all = positive_all.reshape(-1)
    q_rows = q_tokens.shape[0]
    s_rows = s_tokens.shape[0]

    q_hat, q_normed, q_pre, q_weights, q_pooled, q_resid = tower_forward(
        q_tokens, question_ids[0], q_inner_weight, q_norm_gain, False
    )
    s_hat, s_normed, s_pre, s_weights, s_pooled, s_resid = tower_forward(
        s_tokens, sql_ids[0], s_inner_weight, s_norm_gain, True
    )
    q_outer_f = q_outer_weight.astype(jnp.float32)
    s_outer_f = s_outer_weight.astype(jnp.float32)
    q_terms, s_terms = exchange(
        [
            (jnp.dot(q_pooled, q_outer_f, precision=HIGH), "sa", False),
            (jnp.dot(s_pooled, s_outer_f, precision=HIGH), "pb", False),
        ],
        1,
    )
    q_block = jnp.sum(q_terms, axis=0) + q_resid
    s_block = jnp.sum(s_terms, axis=0) + s_resid
    q_embed, q_pooled_all, s_embed, s_pooled_all = exchange(
        [
            (q_block, "pb", False),
            (q_pooled, "pb", False),
            (s_block, "sa", False),
            (s_pooled, "sa", False),
        ],
        2,
    )
    q_embed = q_embed.reshape(-1, D)
    s_embed = s_embed.reshape(-1, D)
    q_pooled_all = q_pooled_all.reshape(-1, q_pooled.shape[-1])
    s_pooled_all = s_pooled_all.reshape(-1, s_pooled.shape[-1])
    score = scale * lax.dot_general(q_embed, s_embed, (((1,), (1,)), ((), ())), precision=HIGH)
    count = score.shape[0]
    match = (positive_all[:, None] == jnp.arange(count, dtype=jnp.int32)[None, :]).astype(
        jnp.float32
    )
    row_max = jnp.max(score, axis=1)
    row_lse = row_max + jnp.log(jnp.sum(jnp.exp(score - row_max[:, None]), axis=1))
    col_max = jnp.max(score, axis=0)
    col_lse = col_max + jnp.log(jnp.sum(jnp.exp(score - col_max[None, :]), axis=0))
    row_pos = jnp.sum(match * score, axis=1)
    col_pos = jnp.sum(match * score, axis=0)
    loss = (jnp.sum(row_lse - row_pos) + jnp.sum(col_lse - col_pos)) / (2.0 * count)
    dscore = 0.5 * (
        jnp.exp(score - row_lse[:, None]) + jnp.exp(score - col_lse[None, :]) - 2.0 * match
    )
    q_grad = scale * jnp.dot(dscore, s_embed, precision=HIGH)
    s_grad = scale * lax.dot_general(dscore, q_embed, (((0,), (0,)), ((), ())), precision=HIGH)

    q_outer_grad = lax.dot_general(q_pooled_all, q_grad, (((0,), (0,)), ((), ())), precision=HIGH)
    s_outer_grad = lax.dot_general(s_pooled_all, s_grad, (((0,), (0,)), ((), ())), precision=HIGH)
    q_grad_own = lax.dynamic_slice_in_dim(q_grad, s_place * q_rows, q_rows, 0)
    s_grad_own = lax.dynamic_slice_in_dim(s_grad, q_place * s_rows, s_rows, 0)
    q_hidden_grad = lax.dot_general(
        q_grad_own, q_outer_f, (((1,), (1,)), ((), ())), precision=HIGH
    )
    s_hidden_grad = lax.dot_general(
        s_grad_own, s_outer_f, (((1,), (1,)), ((), ())), precision=HIGH
    )
    q_inner_part, q_gain_part = tower_backward(
        q_hat, q_normed, q_pre, q_weights, q_inner_weight, q_hidden_grad
    )
    s_inner_part, s_gain_part = tower_backward(
        s_hat, s_normed, s_pre, s_weights, s_inner_weight, s_hidden_grad
    )
    q_pieces = q_inner_part.reshape(lax.axis_size("pb"), -1, q_inner_part.shape[-1])
    s_pieces = s_inner_part.reshape(lax.axis_size("sa"), -1, s_inner_part.shape[-1])
    gains = jnp.stack([q_gain_part, s_gain_part])
    q_pieces, s_pieces, gains = exchange(
        [(q_pieces, "pb", True), (s_pieces, "sa", True), (gains, "sa", False)], 3
    )
    q_inner_grad, s_inner_grad, gains = exchange(
        [
            (jnp.sum(q_pieces, axis=0), "pb", False),
            (jnp.sum(s_pieces, axis=0), "sa", False),
            (jnp.sum(gains, axis=0), "pb", False),
        ],
        4,
    )
    q_inner_grad = q_inner_grad.reshape(q_inner_part.shape)
    s_inner_grad = s_inner_grad.reshape(s_inner_part.shape)
    gains = jnp.sum(gains, axis=0)
    q_gain_grad, s_gain_grad = gains[0], gains[1]
    return (loss, q_inner_grad, q_outer_grad, q_gain_grad, s_inner_grad, s_outer_grad, s_gain_grad)


def solution(mesh):
    placed = (
        P("pb", "sa", None, None),
        P("pb", None, None),
        P(None, "sa"),
        P("sa", None),
        P(),
        P("sa", "pb", None, None),
        P("sa", None, None),
        P(None, "pb"),
        P("pb", None),
        P(),
        P("pb"),
    )
    return jax.shard_map(
        per_device,
        mesh=mesh,
        in_specs=placed,
        out_specs=(P(), P(None, "sa"), P("sa", None), P(), P(None, "pb"), P("pb", None), P()),
        check_vma=False,
    )
```

```python
import functools
import math

import jax
import jax.numpy as jnp
from jax import lax
from jax.experimental import pallas as pl
from jax.experimental.pallas import tpu as pltpu
from jax.sharding import PartitionSpec as P

D = 768

MESH_AXES = ("pb", "sa")


def _peer(axis, p):
    return tuple(p if a == axis else lax.axis_index(a) for a in MESH_AXES)


def exchange(jobs, cid):
    arrays = [a for a, _, _ in jobs]
    kinds = [(ax, spread) for _, ax, spread in jobs]
    sizes = {ax: lax.axis_size(ax) for ax, _ in kinds}
    widest = max(sizes.values())
    count = len(jobs)

    def kernel(*refs):
        srcs, dsts = refs[:count], refs[count:2 * count]
        send, recv, local = refs[2 * count:]
        barrier = pltpu.get_barrier_semaphore()
        axes = list(dict.fromkeys(ax for ax, _ in kinds))
        total = 0
        for ax in axes:
            n = sizes[ax]
            me = lax.axis_index(ax)
            for s in range(1, n):
                pl.semaphore_signal(barrier, 1, device_id=_peer(ax, lax.rem(me + s, n)),
                                    device_id_type=pl.DeviceIdType.MESH)
            total += n - 1
        pl.semaphore_wait(barrier, total)
        started = []
        for t, (ax, spread) in enumerate(kinds):
            n = sizes[ax]
            me = lax.axis_index(ax)
            for s in range(1, n):
                p = lax.rem(me + s, n)
                src = srcs[t].at[p] if spread else srcs[t]
                c = pltpu.make_async_remote_copy(
                    src_ref=src, dst_ref=dsts[t].at[me], send_sem=send.at[t, s],
                    recv_sem=recv.at[t, s], device_id=_peer(ax, p),
                    device_id_type=pl.DeviceIdType.MESH)
                c.start()
                started.append(c)
            src = srcs[t].at[me] if spread else srcs[t]
            c = pltpu.make_async_copy(src, dsts[t].at[me], local.at[t])
            c.start()
            started.append(c)
        for c in started:
            c.wait()

    out_shape = []
    for a, (ax, spread) in zip(arrays, kinds):
        shape = a.shape if spread else (sizes[ax],) + a.shape
        out_shape.append(jax.ShapeDtypeStruct(shape, a.dtype))
    anywhere = pl.BlockSpec(memory_space=pl.ANY)
    return pl.pallas_call(
        kernel,
        out_shape=out_shape,
        in_specs=[anywhere] * count,
        out_specs=[anywhere] * count,
        scratch_shapes=[
            pltpu.SemaphoreType.DMA((count, widest)),
            pltpu.SemaphoreType.DMA((count, widest)),
            pltpu.SemaphoreType.DMA((count,)),
        ],
        compiler_params=pltpu.CompilerParams(collective_id=cid, has_side_effects=True),
    )(*arrays)


HIGH = lax.Precision.HIGHEST


def apply_rms_norm(input_float, norm_gain_vector, root_mean_square):
    if root_mean_square:
        input_normalized = input_float * lax.rsqrt(
            jnp.mean(input_float * input_float, axis=-1, keepdims=True) + 1e-06
        )
    else:
        mean_removed = input_float - jnp.mean(input_float, axis=-1, keepdims=True)
        input_normalized = mean_removed * lax.rsqrt(
            jnp.mean(mean_removed * mean_removed, axis=-1, keepdims=True) + 1e-05
        )
    return (input_normalized, (input_normalized * norm_gain_vector).astype(jnp.bfloat16))


def gelu_value(v):
    return 0.5 * v * (1.0 + lax.erf(v / math.sqrt(2.0)))


def gelu_slope(v):
    return 0.5 * (1.0 + lax.erf(v / math.sqrt(2.0))) + v * jnp.exp(-0.5 * v * v) / math.sqrt(
        2.0 * math.pi
    )


def pool_weights(ids):
    mask = (ids > 0).astype(jnp.float32)
    return mask / jnp.sum(mask, axis=-1, keepdims=True)


def tower_forward(tokens, ids, inner, gain, root_mean_square):
    count, length, width = tokens.shape
    input_float = tokens.astype(jnp.float32).reshape(count * length, width)
    input_normalized, normalized_rows = apply_rms_norm(input_float, gain, root_mean_square)
    pre = jnp.dot(normalized_rows, inner, preferred_element_type=jnp.float32)
    weights = pool_weights(ids)
    hidden = gelu_value(pre).reshape(count, length, -1)
    pooled = jnp.einsum("nt,ntf->nf", weights, hidden, precision=HIGH)
    resid = jnp.einsum(
        "nt,ntd->nd", weights, input_float.reshape(count, length, width), precision=HIGH
    )
    return input_normalized, normalized_rows, pre, weights, pooled, resid


def tower_backward(input_normalized, normalized_rows, pre, weights, inner, hidden_grad):
    count, length = weights.shape
    width = normalized_rows.shape[-1]
    slope = gelu_slope(pre).reshape(count, length, -1)
    dpre = (
        (weights[:, :, None] * hidden_grad[:, None, :] * slope)
        .reshape(count * length, -1)
        .astype(jnp.bfloat16)
    )
    high = lax.reduce_precision(input_normalized, exponent_bits=8, mantissa_bits=7)
    low = input_normalized - high
    rows = jnp.concatenate(
        [normalized_rows, high.astype(jnp.bfloat16), low.astype(jnp.bfloat16)], axis=1
    )
    both = lax.dot_general(
        dpre, rows, (((0,), (0,)), ((), ())), preferred_element_type=jnp.float32
    )
    inner_part = both[:, :width].T
    moment = both[:, width : 2 * width] + both[:, 2 * width :]
    gain_part = jnp.sum(inner.astype(jnp.float32).T * moment, axis=0)
    return inner_part, gain_part


def per_device(
    question_states,
    question_ids,
    q_inner_weight,
    q_outer_weight,
    q_norm_gain,
    sql_states,
    sql_ids,
    s_inner_weight,
    s_outer_weight,
    s_norm_gain,
    positive_column,
):
    scale = 1.0 / math.sqrt(D)
    q_place = lax.axis_index("sa")
    s_place = lax.axis_index("pb")
    q_tokens = lax.all_gather(question_states, "sa", axis=1, tiled=True)[0]
    q_tokens, sql_states = lax.optimization_barrier((q_tokens, sql_states))
    s_tokens = lax.all_gather(sql_states, "pb", axis=1, tiled=True)[0]
    (positive_all,) = exchange([(positive_column.reshape(1, -1), "pb", False)], 0)
    positive_all = positive_all.reshape(-1)
    q_rows = q_tokens.shape[0]
    s_rows = s_tokens.shape[0]

    q_hat, q_normed, q_pre, q_weights, q_pooled, q_resid = tower_forward(
        q_tokens, question_ids[0], q_inner_weight, q_norm_gain, False
    )
    s_hat, s_normed, s_pre, s_weights, s_pooled, s_resid = tower_forward(
        s_tokens, sql_ids[0], s_inner_weight, s_norm_gain, True
    )
    q_outer_f = q_outer_weight.astype(jnp.float32)
    s_outer_f = s_outer_weight.astype(jnp.float32)
    q_terms, s_terms = exchange(
        [
            (jnp.dot(q_pooled, q_outer_f, precision=HIGH), "sa", False),
            (jnp.dot(s_pooled, s_outer_f, precision=HIGH), "pb", False),
        ],
        1,
    )
    q_block = jnp.sum(q_terms, axis=0) + q_resid
    s_block = jnp.sum(s_terms, axis=0) + s_resid
    q_embed, q_pooled_all, s_embed, s_pooled_all = exchange(
        [
            (q_block, "pb", False),
            (q_pooled, "pb", False),
            (s_block, "sa", False),
            (s_pooled, "sa", False),
        ],
        2,
    )
    q_embed = q_embed.reshape(-1, D)
    s_embed = s_embed.reshape(-1, D)
    q_pooled_all = q_pooled_all.reshape(-1, q_pooled.shape[-1])
    s_pooled_all = s_pooled_all.reshape(-1, s_pooled.shape[-1])
    score = scale * lax.dot_general(q_embed, s_embed, (((1,), (1,)), ((), ())), precision=HIGH)
    count = score.shape[0]
    match = (positive_all[:, None] == jnp.arange(count, dtype=jnp.int32)[None, :]).astype(
        jnp.float32
    )
    row_max = jnp.max(score, axis=1)
    row_lse = row_max + jnp.log(jnp.sum(jnp.exp(score - row_max[:, None]), axis=1))
    col_max = jnp.max(score, axis=0)
    col_lse = col_max + jnp.log(jnp.sum(jnp.exp(score - col_max[None, :]), axis=0))
    row_pos = jnp.sum(match * score, axis=1)
    col_pos = jnp.sum(match * score, axis=0)
    loss = (jnp.sum(row_lse - row_pos) + jnp.sum(col_lse - col_pos)) / (2.0 * count)
    dscore = 0.5 * (
        jnp.exp(score - row_lse[:, None]) + jnp.exp(score - col_lse[None, :]) - 2.0 * match
    )
    q_grad = scale * jnp.dot(dscore, s_embed, precision=HIGH)
    s_grad = scale * lax.dot_general(dscore, q_embed, (((0,), (0,)), ((), ())), precision=HIGH)

    q_outer_grad = lax.dot_general(q_pooled_all, q_grad, (((0,), (0,)), ((), ())), precision=HIGH)
    s_outer_grad = lax.dot_general(s_pooled_all, s_grad, (((0,), (0,)), ((), ())), precision=HIGH)
    q_grad_own = lax.dynamic_slice_in_dim(q_grad, s_place * q_rows, q_rows, 0)
    s_grad_own = lax.dynamic_slice_in_dim(s_grad, q_place * s_rows, s_rows, 0)
    q_hidden_grad = lax.dot_general(
        q_grad_own, q_outer_f, (((1,), (1,)), ((), ())), precision=HIGH
    )
    s_hidden_grad = lax.dot_general(
        s_grad_own, s_outer_f, (((1,), (1,)), ((), ())), precision=HIGH
    )
    q_inner_part, q_gain_part = tower_backward(
        q_hat, q_normed, q_pre, q_weights, q_inner_weight, q_hidden_grad
    )
    s_inner_part, s_gain_part = tower_backward(
        s_hat, s_normed, s_pre, s_weights, s_inner_weight, s_hidden_grad
    )
    q_pieces = q_inner_part.reshape(lax.axis_size("pb"), -1, q_inner_part.shape[-1])
    s_pieces = s_inner_part.reshape(lax.axis_size("sa"), -1, s_inner_part.shape[-1])
    gains = jnp.stack([q_gain_part, s_gain_part])
    q_pieces, s_pieces, gains = exchange(
        [(q_pieces, "pb", True), (s_pieces, "sa", True), (gains, "sa", False)], 3
    )
    q_inner_grad, s_inner_grad, gains = exchange(
        [
            (jnp.sum(q_pieces, axis=0), "pb", False),
            (jnp.sum(s_pieces, axis=0), "sa", False),
            (jnp.sum(gains, axis=0), "pb", False),
        ],
        4,
    )
    q_inner_grad = q_inner_grad.reshape(q_inner_part.shape)
    s_inner_grad = s_inner_grad.reshape(s_inner_part.shape)
    gains = jnp.sum(gains, axis=0)
    q_gain_grad, s_gain_grad = gains[0], gains[1]
    return (loss, q_inner_grad, q_outer_grad, q_gain_grad, s_inner_grad, s_outer_grad, s_gain_grad)


def solution(mesh):
    placed = (
        P("pb", "sa", None, None),
        P("pb", None, None),
        P(None, "sa"),
        P("sa", None),
        P(),
        P("sa", "pb", None, None),
        P("sa", None, None),
        P(None, "pb"),
        P("pb", None),
        P(),
        P("pb"),
    )
    return jax.shard_map(
        per_device,
        mesh=mesh,
        in_specs=placed,
        out_specs=(P(), P(None, "sa"), P("sa", None), P(), P(None, "pb"), P("pb", None), P()),
        check_vma=False,
    )
```

```python
import functools
import math

import jax
import jax.numpy as jnp
from jax import lax
from jax.experimental import pallas as pl
from jax.experimental.pallas import tpu as pltpu
from jax.sharding import PartitionSpec as P

D = 768

MESH_AXES = ("pb", "sa")


def _peer(axis, p):
    return tuple(p if a == axis else lax.axis_index(a) for a in MESH_AXES)


def exchange(jobs, cid):
    arrays = [a for a, _, _ in jobs]
    kinds = [(ax, spread) for _, ax, spread in jobs]
    sizes = {ax: lax.axis_size(ax) for ax, _ in kinds}
    widest = max(sizes.values())
    count = len(jobs)

    def kernel(*refs):
        srcs, dsts = refs[:count], refs[count:2 * count]
        send, recv, local = refs[2 * count:]
        barrier = pltpu.get_barrier_semaphore()
        axes = list(dict.fromkeys(ax for ax, _ in kinds))
        total = 0
        for ax in axes:
            n = sizes[ax]
            me = lax.axis_index(ax)
            for s in range(1, n):
                pl.semaphore_signal(barrier, 1, device_id=_peer(ax, lax.rem(me + s, n)),
                                    device_id_type=pl.DeviceIdType.MESH)
            total += n - 1
        pl.semaphore_wait(barrier, total)
        started = []
        for t, (ax, spread) in enumerate(kinds):
            n = sizes[ax]
            me = lax.axis_index(ax)
            for s in range(1, n):
                p = lax.rem(me + s, n)
                src = srcs[t].at[p] if spread else srcs[t]
                c = pltpu.make_async_remote_copy(
                    src_ref=src, dst_ref=dsts[t].at[me], send_sem=send.at[t, s],
                    recv_sem=recv.at[t, s], device_id=_peer(ax, p),
                    device_id_type=pl.DeviceIdType.MESH)
                c.start()
                started.append(c)
            src = srcs[t].at[me] if spread else srcs[t]
            c = pltpu.make_async_copy(src, dsts[t].at[me], local.at[t])
            c.start()
            started.append(c)
        for c in started:
            c.wait()

    out_shape = []
    for a, (ax, spread) in zip(arrays, kinds):
        shape = a.shape if spread else (sizes[ax],) + a.shape
        out_shape.append(jax.ShapeDtypeStruct(shape, a.dtype))
    anywhere = pl.BlockSpec(memory_space=pl.ANY)
    return pl.pallas_call(
        kernel,
        out_shape=out_shape,
        in_specs=[anywhere] * count,
        out_specs=[anywhere] * count,
        scratch_shapes=[
            pltpu.SemaphoreType.DMA((count, widest)),
            pltpu.SemaphoreType.DMA((count, widest)),
            pltpu.SemaphoreType.DMA((count,)),
        ],
        compiler_params=pltpu.CompilerParams(collective_id=cid, has_side_effects=True),
    )(*arrays)


def pair_gather(block, cid):
    n = lax.axis_size("sa")
    half = n // 2

    def kernel(src, dst, send, recv, relay_send, relay_recv, pair_send, pair_recv, local):
        me = lax.axis_index("sa")
        partner = me + 1 - 2 * lax.rem(me, 2)
        barrier = pltpu.get_barrier_semaphore()
        for s in range(1, half):
            pl.semaphore_signal(barrier, 1, device_id=_peer("sa", lax.rem(me + 2 * s, n)),
                                device_id_type=pl.DeviceIdType.MESH)
        pl.semaphore_signal(barrier, 1, device_id=_peer("sa", partner),
                            device_id_type=pl.DeviceIdType.MESH)
        pl.semaphore_wait(barrier, half)
        own = pltpu.make_async_copy(src, dst.at[me], local.at[0])
        own.start()
        pair = pltpu.make_async_remote_copy(
            src_ref=src, dst_ref=dst.at[me], send_sem=pair_send.at[0], recv_sem=pair_recv.at[0],
            device_id=_peer("sa", partner), device_id_type=pl.DeviceIdType.MESH)
        pair.start()
        outgoing = []
        for s in range(1, half):
            c = pltpu.make_async_remote_copy(
                src_ref=src, dst_ref=dst.at[me], send_sem=send.at[s], recv_sem=recv.at[s],
                device_id=_peer("sa", lax.rem(me + 2 * s, n)), device_id_type=pl.DeviceIdType.MESH)
            c.start()
            outgoing.append(c)
        relays = []
        for s in range(1, half):
            outgoing[s - 1].wait_recv()
            slot = lax.rem(me + n - 2 * s, n)
            r = pltpu.make_async_remote_copy(
                src_ref=dst.at[slot], dst_ref=dst.at[slot], send_sem=relay_send.at[s],
                recv_sem=relay_recv.at[s], device_id=_peer("sa", partner),
                device_id_type=pl.DeviceIdType.MESH)
            r.start()
            relays.append(r)
        for c in outgoing:
            c.wait_send()
        for r in relays:
            r.wait()
        pair.wait()
        own.wait()

    anywhere = pl.BlockSpec(memory_space=pl.ANY)
    return pl.pallas_call(
        kernel,
        out_shape=jax.ShapeDtypeStruct((n,) + block.shape, block.dtype),
        in_specs=[anywhere],
        out_specs=anywhere,
        scratch_shapes=[
            pltpu.SemaphoreType.DMA((half,)),
            pltpu.SemaphoreType.DMA((half,)),
            pltpu.SemaphoreType.DMA((half,)),
            pltpu.SemaphoreType.DMA((half,)),
            pltpu.SemaphoreType.DMA((1,)),
            pltpu.SemaphoreType.DMA((1,)),
            pltpu.SemaphoreType.DMA((1,)),
        ],
        compiler_params=pltpu.CompilerParams(collective_id=cid, has_side_effects=True),
    )(block)


HIGH = lax.Precision.HIGHEST


def apply_rms_norm(input_float, norm_gain_vector, root_mean_square):
    if root_mean_square:
        input_normalized = input_float * lax.rsqrt(
            jnp.mean(input_float * input_float, axis=-1, keepdims=True) + 1e-06
        )
    else:
        mean_removed = input_float - jnp.mean(input_float, axis=-1, keepdims=True)
        input_normalized = mean_removed * lax.rsqrt(
            jnp.mean(mean_removed * mean_removed, axis=-1, keepdims=True) + 1e-05
        )
    return (input_normalized, (input_normalized * norm_gain_vector).astype(jnp.bfloat16))


def gelu_value(v):
    return 0.5 * v * (1.0 + lax.erf(v / math.sqrt(2.0)))


def gelu_slope(v):
    return 0.5 * (1.0 + lax.erf(v / math.sqrt(2.0))) + v * jnp.exp(-0.5 * v * v) / math.sqrt(
        2.0 * math.pi
    )


def pool_weights(ids):
    mask = (ids > 0).astype(jnp.float32)
    return mask / jnp.sum(mask, axis=-1, keepdims=True)


def tower_forward(tokens, ids, inner, gain, root_mean_square):
    count, length, width = tokens.shape
    input_float = tokens.astype(jnp.float32).reshape(count * length, width)
    input_normalized, normalized_rows = apply_rms_norm(input_float, gain, root_mean_square)
    pre = jnp.dot(normalized_rows, inner, preferred_element_type=jnp.float32)
    weights = pool_weights(ids)
    hidden = gelu_value(pre).reshape(count, length, -1)
    pooled = jnp.einsum("nt,ntf->nf", weights, hidden, precision=HIGH)
    resid = jnp.einsum(
        "nt,ntd->nd", weights, input_float.reshape(count, length, width), precision=HIGH
    )
    return input_normalized, normalized_rows, pre, weights, pooled, resid


def tower_backward(input_normalized, normalized_rows, pre, weights, inner, hidden_grad):
    count, length = weights.shape
    width = normalized_rows.shape[-1]
    slope = gelu_slope(pre).reshape(count, length, -1)
    dpre = (
        (weights[:, :, None] * hidden_grad[:, None, :] * slope)
        .reshape(count * length, -1)
        .astype(jnp.bfloat16)
    )
    high = lax.reduce_precision(input_normalized, exponent_bits=8, mantissa_bits=7)
    low = input_normalized - high
    rows = jnp.concatenate(
        [normalized_rows, high.astype(jnp.bfloat16), low.astype(jnp.bfloat16)], axis=1
    )
    both = lax.dot_general(
        dpre, rows, (((0,), (0,)), ((), ())), preferred_element_type=jnp.float32
    )
    inner_part = both[:, :width].T
    moment = both[:, width : 2 * width] + both[:, 2 * width :]
    gain_part = jnp.sum(inner.astype(jnp.float32).T * moment, axis=0)
    return inner_part, gain_part


def per_device(
    question_states,
    question_ids,
    q_inner_weight,
    q_outer_weight,
    q_norm_gain,
    sql_states,
    sql_ids,
    s_inner_weight,
    s_outer_weight,
    s_norm_gain,
    positive_column,
):
    scale = 1.0 / math.sqrt(D)
    q_place = lax.axis_index("sa")
    s_place = lax.axis_index("pb")
    q_tokens = pair_gather(question_states[0, 0], 5)
    s_tokens = lax.all_gather(sql_states, "pb", axis=1, tiled=True)[0]
    (positive_all,) = exchange([(positive_column.reshape(1, -1), "pb", False)], 0)
    positive_all = positive_all.reshape(-1)
    q_rows = q_tokens.shape[0]
    s_rows = s_tokens.shape[0]

    q_hat, q_normed, q_pre, q_weights, q_pooled, q_resid = tower_forward(
        q_tokens, question_ids[0], q_inner_weight, q_norm_gain, False
    )
    s_hat, s_normed, s_pre, s_weights, s_pooled, s_resid = tower_forward(
        s_tokens, sql_ids[0], s_inner_weight, s_norm_gain, True
    )
    q_outer_f = q_outer_weight.astype(jnp.float32)
    s_outer_f = s_outer_weight.astype(jnp.float32)
    q_terms, s_terms = exchange(
        [
            (jnp.dot(q_pooled, q_outer_f, precision=HIGH), "sa", False),
            (jnp.dot(s_pooled, s_outer_f, precision=HIGH), "pb", False),
        ],
        1,
    )
    q_block = jnp.sum(q_terms, axis=0) + q_resid
    s_block = jnp.sum(s_terms, axis=0) + s_resid
    q_embed, q_pooled_all, s_embed, s_pooled_all = exchange(
        [
            (q_block, "pb", False),
            (q_pooled, "pb", False),
            (s_block, "sa", False),
            (s_pooled, "sa", False),
        ],
        2,
    )
    q_embed = q_embed.reshape(-1, D)
    s_embed = s_embed.reshape(-1, D)
    q_pooled_all = q_pooled_all.reshape(-1, q_pooled.shape[-1])
    s_pooled_all = s_pooled_all.reshape(-1, s_pooled.shape[-1])
    score = scale * lax.dot_general(q_embed, s_embed, (((1,), (1,)), ((), ())), precision=HIGH)
    count = score.shape[0]
    match = (positive_all[:, None] == jnp.arange(count, dtype=jnp.int32)[None, :]).astype(
        jnp.float32
    )
    row_max = jnp.max(score, axis=1)
    row_lse = row_max + jnp.log(jnp.sum(jnp.exp(score - row_max[:, None]), axis=1))
    col_max = jnp.max(score, axis=0)
    col_lse = col_max + jnp.log(jnp.sum(jnp.exp(score - col_max[None, :]), axis=0))
    row_pos = jnp.sum(match * score, axis=1)
    col_pos = jnp.sum(match * score, axis=0)
    loss = (jnp.sum(row_lse - row_pos) + jnp.sum(col_lse - col_pos)) / (2.0 * count)
    dscore = 0.5 * (
        jnp.exp(score - row_lse[:, None]) + jnp.exp(score - col_lse[None, :]) - 2.0 * match
    )
    q_grad = scale * jnp.dot(dscore, s_embed, precision=HIGH)
    s_grad = scale * lax.dot_general(dscore, q_embed, (((0,), (0,)), ((), ())), precision=HIGH)

    q_outer_grad = lax.dot_general(q_pooled_all, q_grad, (((0,), (0,)), ((), ())), precision=HIGH)
    s_outer_grad = lax.dot_general(s_pooled_all, s_grad, (((0,), (0,)), ((), ())), precision=HIGH)
    q_grad_own = lax.dynamic_slice_in_dim(q_grad, s_place * q_rows, q_rows, 0)
    s_grad_own = lax.dynamic_slice_in_dim(s_grad, q_place * s_rows, s_rows, 0)
    q_hidden_grad = lax.dot_general(
        q_grad_own, q_outer_f, (((1,), (1,)), ((), ())), precision=HIGH
    )
    s_hidden_grad = lax.dot_general(
        s_grad_own, s_outer_f, (((1,), (1,)), ((), ())), precision=HIGH
    )
    q_inner_part, q_gain_part = tower_backward(
        q_hat, q_normed, q_pre, q_weights, q_inner_weight, q_hidden_grad
    )
    s_inner_part, s_gain_part = tower_backward(
        s_hat, s_normed, s_pre, s_weights, s_inner_weight, s_hidden_grad
    )
    q_pieces = q_inner_part.reshape(lax.axis_size("pb"), -1, q_inner_part.shape[-1])
    s_pieces = s_inner_part.reshape(lax.axis_size("sa"), -1, s_inner_part.shape[-1])
    gains = jnp.stack([q_gain_part, s_gain_part])
    q_pieces, s_pieces, gains = exchange(
        [(q_pieces, "pb", True), (s_pieces, "sa", True), (gains, "sa", False)], 3
    )
    q_inner_grad, s_inner_grad, gains = exchange(
        [
            (jnp.sum(q_pieces, axis=0), "pb", False),
            (jnp.sum(s_pieces, axis=0), "sa", False),
            (jnp.sum(gains, axis=0), "pb", False),
        ],
        4,
    )
    q_inner_grad = q_inner_grad.reshape(q_inner_part.shape)
    s_inner_grad = s_inner_grad.reshape(s_inner_part.shape)
    gains = jnp.sum(gains, axis=0)
    q_gain_grad, s_gain_grad = gains[0], gains[1]
    return (loss, q_inner_grad, q_outer_grad, q_gain_grad, s_inner_grad, s_outer_grad, s_gain_grad)


def solution(mesh):
    placed = (
        P("pb", "sa", None, None),
        P("pb", None, None),
        P(None, "sa"),
        P("sa", None),
        P(),
        P("sa", "pb", None, None),
        P("sa", None, None),
        P(None, "pb"),
        P("pb", None),
        P(),
        P("pb"),
    )
    return jax.shard_map(
        per_device,
        mesh=mesh,
        in_specs=placed,
        out_specs=(P(), P(None, "sa"), P("sa", None), P(), P(None, "pb"), P("pb", None), P()),
        check_vma=False,
    )
```

```python
import functools
import math

import jax
import jax.numpy as jnp
from jax import lax
from jax.experimental import pallas as pl
from jax.experimental.pallas import tpu as pltpu
from jax.sharding import PartitionSpec as P

D = 768

MESH_AXES = ("pb", "sa")


def _peer(axis, p):
    return tuple(p if a == axis else lax.axis_index(a) for a in MESH_AXES)


def exchange(jobs, cid):
    arrays = [a for a, _, _ in jobs]
    kinds = [(ax, spread) for _, ax, spread in jobs]
    sizes = {ax: lax.axis_size(ax) for ax, _ in kinds}
    widest = max(sizes.values())
    count = len(jobs)

    def kernel(*refs):
        srcs, dsts = refs[:count], refs[count:2 * count]
        send, recv, local = refs[2 * count:]
        barrier = pltpu.get_barrier_semaphore()
        axes = list(dict.fromkeys(ax for ax, _ in kinds))
        total = 0
        for ax in axes:
            n = sizes[ax]
            me = lax.axis_index(ax)
            for s in range(1, n):
                pl.semaphore_signal(barrier, 1, device_id=_peer(ax, lax.rem(me + s, n)),
                                    device_id_type=pl.DeviceIdType.MESH)
            total += n - 1
        pl.semaphore_wait(barrier, total)
        started = []
        for t, (ax, spread) in enumerate(kinds):
            n = sizes[ax]
            me = lax.axis_index(ax)
            for s in range(1, n):
                p = lax.rem(me + s, n)
                src = srcs[t].at[p] if spread else srcs[t]
                c = pltpu.make_async_remote_copy(
                    src_ref=src, dst_ref=dsts[t].at[me], send_sem=send.at[t, s],
                    recv_sem=recv.at[t, s], device_id=_peer(ax, p),
                    device_id_type=pl.DeviceIdType.MESH)
                c.start()
                started.append(c)
            src = srcs[t].at[me] if spread else srcs[t]
            c = pltpu.make_async_copy(src, dsts[t].at[me], local.at[t])
            c.start()
            started.append(c)
        for c in started:
            c.wait()

    out_shape = []
    for a, (ax, spread) in zip(arrays, kinds):
        shape = a.shape if spread else (sizes[ax],) + a.shape
        out_shape.append(jax.ShapeDtypeStruct(shape, a.dtype))
    anywhere = pl.BlockSpec(memory_space=pl.ANY)
    return pl.pallas_call(
        kernel,
        out_shape=out_shape,
        in_specs=[anywhere] * count,
        out_specs=[anywhere] * count,
        scratch_shapes=[
            pltpu.SemaphoreType.DMA((count, widest)),
            pltpu.SemaphoreType.DMA((count, widest)),
            pltpu.SemaphoreType.DMA((count,)),
        ],
        compiler_params=pltpu.CompilerParams(collective_id=cid, has_side_effects=True),
    )(*arrays)


def plane_gather(block, cid):
    n = lax.axis_size("sa")
    rows = n // 4
    mesh_kind = pl.DeviceIdType.MESH

    def kernel(src, dst, ysend, yrecv, fsend, frecv, rsend, rrecv, zsend, zrecv, psend, precv, local):
        me = lax.axis_index("sa")
        core = lax.rem(me, 2)
        row = lax.rem(me // 2, rows)
        plane = me // (2 * rows)
        partner = me + 1 - 2 * core
        across = lax.rem(me + 2 * rows, n)

        def along(d):
            return plane * 2 * rows + lax.rem(row + d, rows) * 2 + core

        barrier = pltpu.get_barrier_semaphore()
        for peer in [partner, across] + [along(d) for d in range(1, rows)]:
            pl.semaphore_signal(barrier, 1, device_id=_peer("sa", peer), device_id_type=mesh_kind)
        pl.semaphore_wait(barrier, rows + 1)

        def send(source, slot, peer, s, r):
            c = pltpu.make_async_remote_copy(
                src_ref=source, dst_ref=dst.at[slot], send_sem=s, recv_sem=r,
                device_id=_peer("sa", peer), device_id_type=mesh_kind)
            c.start()
            return c

        own = pltpu.make_async_copy(src, dst.at[me], local.at[0])
        own.start()
        z_copy = send(src, me, across, zsend.at[0], zrecv.at[0])
        pair = send(src, me, partner, psend.at[0], precv.at[0])
        direct = [send(src, me, along(d), ysend.at[d], yrecv.at[d]) for d in range(1, rows)]
        z_copy.wait_recv()
        far = lax.rem(me + 2 * rows, n)
        relayed = [send(dst.at[far], far, along(d), fsend.at[d], frecv.at[d]) for d in range(1, rows)]
        handed = [send(dst.at[far], far, partner, rsend.at[0], rrecv.at[0])]
        for d in range(1, rows):
            direct[d - 1].wait_recv()
            slot = along(rows - d)
            handed.append(send(dst.at[slot], slot, partner, rsend.at[d], rrecv.at[d]))
        for d in range(1, rows):
            relayed[d - 1].wait_recv()
            slot = lax.rem(along(rows - d) + 2 * rows, n)
            handed.append(send(dst.at[slot], slot, partner, rsend.at[rows - 1 + d],
                               rrecv.at[rows - 1 + d]))
        for c in direct + relayed + [z_copy]:
            c.wait_send()
        for c in handed:
            c.wait()
        pair.wait()
        own.wait()

    anywhere = pl.BlockSpec(memory_space=pl.ANY)
    return pl.pallas_call(
        kernel,
        out_shape=jax.ShapeDtypeStruct((n,) + block.shape, block.dtype),
        in_specs=[anywhere],
        out_specs=anywhere,
        scratch_shapes=[
            pltpu.SemaphoreType.DMA((rows,)),
            pltpu.SemaphoreType.DMA((rows,)),
            pltpu.SemaphoreType.DMA((rows,)),
            pltpu.SemaphoreType.DMA((rows,)),
            pltpu.SemaphoreType.DMA((2 * rows - 1,)),
            pltpu.SemaphoreType.DMA((2 * rows - 1,)),
            pltpu.SemaphoreType.DMA((1,)),
            pltpu.SemaphoreType.DMA((1,)),
            pltpu.SemaphoreType.DMA((1,)),
            pltpu.SemaphoreType.DMA((1,)),
            pltpu.SemaphoreType.DMA((1,)),
        ],
        compiler_params=pltpu.CompilerParams(collective_id=cid, has_side_effects=True),
    )(block)


HIGH = lax.Precision.HIGHEST


def apply_rms_norm(input_float, norm_gain_vector, root_mean_square):
    if root_mean_square:
        input_normalized = input_float * lax.rsqrt(
            jnp.mean(input_float * input_float, axis=-1, keepdims=True) + 1e-06
        )
    else:
        mean_removed = input_float - jnp.mean(input_float, axis=-1, keepdims=True)
        input_normalized = mean_removed * lax.rsqrt(
            jnp.mean(mean_removed * mean_removed, axis=-1, keepdims=True) + 1e-05
        )
    return (input_normalized, (input_normalized * norm_gain_vector).astype(jnp.bfloat16))


def gelu_value(v):
    return 0.5 * v * (1.0 + lax.erf(v / math.sqrt(2.0)))


def gelu_slope(v):
    return 0.5 * (1.0 + lax.erf(v / math.sqrt(2.0))) + v * jnp.exp(-0.5 * v * v) / math.sqrt(
        2.0 * math.pi
    )


def pool_weights(ids):
    mask = (ids > 0).astype(jnp.float32)
    return mask / jnp.sum(mask, axis=-1, keepdims=True)


def tower_forward(tokens, ids, inner, gain, root_mean_square):
    count, length, width = tokens.shape
    input_float = tokens.astype(jnp.float32).reshape(count * length, width)
    input_normalized, normalized_rows = apply_rms_norm(input_float, gain, root_mean_square)
    pre = jnp.dot(normalized_rows, inner, preferred_element_type=jnp.float32)
    weights = pool_weights(ids)
    hidden = gelu_value(pre).reshape(count, length, -1)
    pooled = jnp.einsum("nt,ntf->nf", weights, hidden, precision=HIGH)
    resid = jnp.einsum(
        "nt,ntd->nd", weights, input_float.reshape(count, length, width), precision=HIGH
    )
    return input_normalized, normalized_rows, pre, weights, pooled, resid


def tower_backward(input_normalized, normalized_rows, pre, weights, inner, hidden_grad):
    count, length = weights.shape
    width = normalized_rows.shape[-1]
    slope = gelu_slope(pre).reshape(count, length, -1)
    dpre = (
        (weights[:, :, None] * hidden_grad[:, None, :] * slope)
        .reshape(count * length, -1)
        .astype(jnp.bfloat16)
    )
    high = lax.reduce_precision(input_normalized, exponent_bits=8, mantissa_bits=7)
    low = input_normalized - high
    rows = jnp.concatenate(
        [normalized_rows, high.astype(jnp.bfloat16), low.astype(jnp.bfloat16)], axis=1
    )
    both = lax.dot_general(
        dpre, rows, (((0,), (0,)), ((), ())), preferred_element_type=jnp.float32
    )
    inner_part = both[:, :width].T
    moment = both[:, width : 2 * width] + both[:, 2 * width :]
    gain_part = jnp.sum(inner.astype(jnp.float32).T * moment, axis=0)
    return inner_part, gain_part


def per_device(
    question_states,
    question_ids,
    q_inner_weight,
    q_outer_weight,
    q_norm_gain,
    sql_states,
    sql_ids,
    s_inner_weight,
    s_outer_weight,
    s_norm_gain,
    positive_column,
):
    scale = 1.0 / math.sqrt(D)
    q_place = lax.axis_index("sa")
    s_place = lax.axis_index("pb")
    q_tokens = plane_gather(question_states[0, 0], 5)
    s_tokens = lax.all_gather(sql_states, "pb", axis=1, tiled=True)[0]
    q_rows = q_tokens.shape[0]
    s_rows = s_tokens.shape[0]

    q_hat, q_normed, q_pre, q_weights, q_pooled, q_resid = tower_forward(
        q_tokens, question_ids[0], q_inner_weight, q_norm_gain, False
    )
    s_hat, s_normed, s_pre, s_weights, s_pooled, s_resid = tower_forward(
        s_tokens, sql_ids[0], s_inner_weight, s_norm_gain, True
    )
    q_outer_f = q_outer_weight.astype(jnp.float32)
    s_outer_f = s_outer_weight.astype(jnp.float32)
    q_terms, s_terms = exchange(
        [
            (jnp.dot(q_pooled, q_outer_f, precision=HIGH), "sa", False),
            (jnp.dot(s_pooled, s_outer_f, precision=HIGH), "pb", False),
        ],
        1,
    )
    q_block = jnp.sum(q_terms, axis=0) + q_resid
    s_block = jnp.sum(s_terms, axis=0) + s_resid
    q_embed, q_pooled_all, s_embed, s_pooled_all, positive_all = exchange(
        [
            (q_block, "pb", False),
            (q_pooled, "pb", False),
            (s_block, "sa", False),
            (s_pooled, "sa", False),
            (positive_column.reshape(1, -1), "pb", False),
        ],
        2,
    )
    positive_all = positive_all.reshape(-1)
    q_embed = q_embed.reshape(-1, D)
    s_embed = s_embed.reshape(-1, D)
    q_pooled_all = q_pooled_all.reshape(-1, q_pooled.shape[-1])
    s_pooled_all = s_pooled_all.reshape(-1, s_pooled.shape[-1])
    score = scale * lax.dot_general(q_embed, s_embed, (((1,), (1,)), ((), ())), precision=HIGH)
    count = score.shape[0]
    match = (positive_all[:, None] == jnp.arange(count, dtype=jnp.int32)[None, :]).astype(
        jnp.float32
    )
    row_max = jnp.max(score, axis=1)
    row_lse = row_max + jnp.log(jnp.sum(jnp.exp(score - row_max[:, None]), axis=1))
    col_max = jnp.max(score, axis=0)
    col_lse = col_max + jnp.log(jnp.sum(jnp.exp(score - col_max[None, :]), axis=0))
    row_pos = jnp.sum(match * score, axis=1)
    col_pos = jnp.sum(match * score, axis=0)
    loss = (jnp.sum(row_lse - row_pos) + jnp.sum(col_lse - col_pos)) / (2.0 * count)
    dscore = 0.5 * (
        jnp.exp(score - row_lse[:, None]) + jnp.exp(score - col_lse[None, :]) - 2.0 * match
    )
    q_grad = scale * jnp.dot(dscore, s_embed, precision=HIGH)
    s_grad = scale * lax.dot_general(dscore, q_embed, (((0,), (0,)), ((), ())), precision=HIGH)

    q_outer_grad = lax.dot_general(q_pooled_all, q_grad, (((0,), (0,)), ((), ())), precision=HIGH)
    s_outer_grad = lax.dot_general(s_pooled_all, s_grad, (((0,), (0,)), ((), ())), precision=HIGH)
    q_grad_own = lax.dynamic_slice_in_dim(q_grad, s_place * q_rows, q_rows, 0)
    s_grad_own = lax.dynamic_slice_in_dim(s_grad, q_place * s_rows, s_rows, 0)
    q_hidden_grad = lax.dot_general(
        q_grad_own, q_outer_f, (((1,), (1,)), ((), ())), precision=HIGH
    )
    s_hidden_grad = lax.dot_general(
        s_grad_own, s_outer_f, (((1,), (1,)), ((), ())), precision=HIGH
    )
    q_inner_part, q_gain_part = tower_backward(
        q_hat, q_normed, q_pre, q_weights, q_inner_weight, q_hidden_grad
    )
    s_inner_part, s_gain_part = tower_backward(
        s_hat, s_normed, s_pre, s_weights, s_inner_weight, s_hidden_grad
    )
    q_pieces = q_inner_part.reshape(lax.axis_size("pb"), -1, q_inner_part.shape[-1])
    s_pieces = s_inner_part.reshape(lax.axis_size("sa"), -1, s_inner_part.shape[-1])
    gains = jnp.stack([q_gain_part, s_gain_part])
    q_pieces, s_pieces, gains = exchange(
        [(q_pieces, "pb", True), (s_pieces, "sa", True), (gains, "sa", False)], 3
    )
    q_inner_grad, s_inner_grad, gains = exchange(
        [
            (jnp.sum(q_pieces, axis=0), "pb", False),
            (jnp.sum(s_pieces, axis=0), "sa", False),
            (jnp.sum(gains, axis=0), "pb", False),
        ],
        4,
    )
    q_inner_grad = q_inner_grad.reshape(q_inner_part.shape)
    s_inner_grad = s_inner_grad.reshape(s_inner_part.shape)
    gains = jnp.sum(gains, axis=0)
    q_gain_grad, s_gain_grad = gains[0], gains[1]
    return (loss, q_inner_grad, q_outer_grad, q_gain_grad, s_inner_grad, s_outer_grad, s_gain_grad)


def solution(mesh):
    placed = (
        P("pb", "sa", None, None),
        P("pb", None, None),
        P(None, "sa"),
        P("sa", None),
        P(),
        P("sa", "pb", None, None),
        P("sa", None, None),
        P(None, "pb"),
        P("pb", None),
        P(),
        P("pb"),
    )
    return jax.shard_map(
        per_device,
        mesh=mesh,
        in_specs=placed,
        out_specs=(P(), P(None, "sa"), P("sa", None), P(), P(None, "pb"), P("pb", None), P()),
        check_vma=False,
    )
```

```python
import functools
import math

import jax
import jax.numpy as jnp
from jax import lax
from jax.experimental import pallas as pl
from jax.experimental.pallas import tpu as pltpu
from jax.sharding import PartitionSpec as P

D = 768

MESH_AXES = ("pb", "sa")


def _peer(axis, p):
    return tuple(p if a == axis else lax.axis_index(a) for a in MESH_AXES)


def exchange(jobs, cid):
    arrays = [a for a, _, _ in jobs]
    kinds = [(ax, spread) for _, ax, spread in jobs]
    sizes = {ax: lax.axis_size(ax) for ax, _ in kinds}
    widest = max(sizes.values())
    count = len(jobs)

    def kernel(*refs):
        srcs, dsts = refs[:count], refs[count:2 * count]
        send, recv, local = refs[2 * count:]
        barrier = pltpu.get_barrier_semaphore()
        axes = list(dict.fromkeys(ax for ax, _ in kinds))
        total = 0
        for ax in axes:
            n = sizes[ax]
            me = lax.axis_index(ax)
            for s in range(1, n):
                pl.semaphore_signal(barrier, 1, device_id=_peer(ax, lax.rem(me + s, n)),
                                    device_id_type=pl.DeviceIdType.MESH)
            total += n - 1
        pl.semaphore_wait(barrier, total)
        started = []
        for t, (ax, spread) in enumerate(kinds):
            n = sizes[ax]
            me = lax.axis_index(ax)
            for s in range(1, n):
                p = lax.rem(me + s, n)
                src = srcs[t].at[p] if spread else srcs[t]
                c = pltpu.make_async_remote_copy(
                    src_ref=src, dst_ref=dsts[t].at[me], send_sem=send.at[t, s],
                    recv_sem=recv.at[t, s], device_id=_peer(ax, p),
                    device_id_type=pl.DeviceIdType.MESH)
                c.start()
                started.append(c)
            src = srcs[t].at[me] if spread else srcs[t]
            c = pltpu.make_async_copy(src, dsts[t].at[me], local.at[t])
            c.start()
            started.append(c)
        for c in started:
            c.wait()

    out_shape = []
    for a, (ax, spread) in zip(arrays, kinds):
        shape = a.shape if spread else (sizes[ax],) + a.shape
        out_shape.append(jax.ShapeDtypeStruct(shape, a.dtype))
    anywhere = pl.BlockSpec(memory_space=pl.ANY)
    return pl.pallas_call(
        kernel,
        out_shape=out_shape,
        in_specs=[anywhere] * count,
        out_specs=[anywhere] * count,
        scratch_shapes=[
            pltpu.SemaphoreType.DMA((count, widest)),
            pltpu.SemaphoreType.DMA((count, widest)),
            pltpu.SemaphoreType.DMA((count,)),
        ],
        compiler_params=pltpu.CompilerParams(collective_id=cid, has_side_effects=True),
    )(*arrays)


def plane_gather(block, cid):
    n = lax.axis_size("sa")
    rows = n // 4
    mesh_kind = pl.DeviceIdType.MESH

    def kernel(src, dst, ysend, yrecv, fsend, frecv, rsend, rrecv, zsend, zrecv, psend, precv, local):
        me = lax.axis_index("sa")
        core = lax.rem(me, 2)
        row = lax.rem(me // 2, rows)
        plane = me // (2 * rows)
        partner = me + 1 - 2 * core
        across = lax.rem(me + 2 * rows, n)

        def along(d):
            return plane * 2 * rows + lax.rem(row + d, rows) * 2 + core

        barrier = pltpu.get_barrier_semaphore()
        for peer in [partner, across] + [along(d) for d in range(1, rows)]:
            pl.semaphore_signal(barrier, 1, device_id=_peer("sa", peer), device_id_type=mesh_kind)
        pl.semaphore_wait(barrier, rows + 1)

        def send(source, slot, peer, s, r):
            c = pltpu.make_async_remote_copy(
                src_ref=source, dst_ref=dst.at[slot], send_sem=s, recv_sem=r,
                device_id=_peer("sa", peer), device_id_type=mesh_kind)
            c.start()
            return c

        own = pltpu.make_async_copy(src, dst.at[me], local.at[0])
        own.start()
        z_copy = send(src, me, across, zsend.at[0], zrecv.at[0])
        pair = send(src, me, partner, psend.at[0], precv.at[0])
        direct = [send(src, me, along(d), ysend.at[d], yrecv.at[d]) for d in range(1, rows)]
        z_copy.wait_recv()
        far = lax.rem(me + 2 * rows, n)
        relayed = [send(dst.at[far], far, along(d), fsend.at[d], frecv.at[d]) for d in range(1, rows)]
        handed = [send(dst.at[far], far, partner, rsend.at[0], rrecv.at[0])]
        for d in range(1, rows):
            direct[d - 1].wait_recv()
            slot = along(rows - d)
            handed.append(send(dst.at[slot], slot, partner, rsend.at[d], rrecv.at[d]))
        for d in range(1, rows):
            relayed[d - 1].wait_recv()
            slot = lax.rem(along(rows - d) + 2 * rows, n)
            handed.append(send(dst.at[slot], slot, partner, rsend.at[rows - 1 + d],
                               rrecv.at[rows - 1 + d]))
        for c in direct + relayed + [z_copy]:
            c.wait_send()
        for c in handed:
            c.wait()
        pair.wait()
        own.wait()

    anywhere = pl.BlockSpec(memory_space=pl.ANY)
    return pl.pallas_call(
        kernel,
        out_shape=jax.ShapeDtypeStruct((n,) + block.shape, block.dtype),
        in_specs=[anywhere],
        out_specs=anywhere,
        scratch_shapes=[
            pltpu.SemaphoreType.DMA((rows,)),
            pltpu.SemaphoreType.DMA((rows,)),
            pltpu.SemaphoreType.DMA((rows,)),
            pltpu.SemaphoreType.DMA((rows,)),
            pltpu.SemaphoreType.DMA((2 * rows - 1,)),
            pltpu.SemaphoreType.DMA((2 * rows - 1,)),
            pltpu.SemaphoreType.DMA((1,)),
            pltpu.SemaphoreType.DMA((1,)),
            pltpu.SemaphoreType.DMA((1,)),
            pltpu.SemaphoreType.DMA((1,)),
            pltpu.SemaphoreType.DMA((1,)),
        ],
        compiler_params=pltpu.CompilerParams(collective_id=cid, has_side_effects=True),
    )(block)


HIGH = lax.Precision.HIGHEST


def apply_rms_norm(input_float, norm_gain_vector, root_mean_square):
    if root_mean_square:
        input_normalized = input_float * lax.rsqrt(
            jnp.mean(input_float * input_float, axis=-1, keepdims=True) + 1e-06
        )
    else:
        mean_removed = input_float - jnp.mean(input_float, axis=-1, keepdims=True)
        input_normalized = mean_removed * lax.rsqrt(
            jnp.mean(mean_removed * mean_removed, axis=-1, keepdims=True) + 1e-05
        )
    return (input_normalized, (input_normalized * norm_gain_vector).astype(jnp.bfloat16))


def gelu_value(v):
    return 0.5 * v * (1.0 + lax.erf(v / math.sqrt(2.0)))


def gelu_slope(v):
    return 0.5 * (1.0 + lax.erf(v / math.sqrt(2.0))) + v * jnp.exp(-0.5 * v * v) / math.sqrt(
        2.0 * math.pi
    )


def pool_weights(ids):
    mask = (ids > 0).astype(jnp.float32)
    return mask / jnp.sum(mask, axis=-1, keepdims=True)


def tower_forward(tokens, ids, inner, gain, root_mean_square):
    count, length, width = tokens.shape
    input_float = tokens.astype(jnp.float32).reshape(count * length, width)
    input_normalized, normalized_rows = apply_rms_norm(input_float, gain, root_mean_square)
    pre = jnp.dot(normalized_rows, inner, preferred_element_type=jnp.float32)
    weights = pool_weights(ids)
    hidden = gelu_value(pre).reshape(count, length, -1)
    pooled = jnp.einsum("nt,ntf->nf", weights, hidden, precision=HIGH)
    resid = jnp.einsum(
        "nt,ntd->nd", weights, input_float.reshape(count, length, width), precision=HIGH
    )
    return input_normalized, normalized_rows, pre, weights, pooled, resid


def tower_backward(input_normalized, normalized_rows, pre, weights, inner, hidden_grad):
    count, length = weights.shape
    width = normalized_rows.shape[-1]
    slope = gelu_slope(pre).reshape(count, length, -1)
    dpre = (
        (weights[:, :, None] * hidden_grad[:, None, :] * slope)
        .reshape(count * length, -1)
        .astype(jnp.bfloat16)
    )
    high = lax.reduce_precision(input_normalized, exponent_bits=8, mantissa_bits=7)
    low = input_normalized - high
    rows = jnp.concatenate(
        [normalized_rows, high.astype(jnp.bfloat16), low.astype(jnp.bfloat16)], axis=1
    )
    both = lax.dot_general(
        dpre, rows, (((0,), (0,)), ((), ())), preferred_element_type=jnp.float32
    )
    inner_part = both[:, :width].T
    moment = both[:, width : 2 * width] + both[:, 2 * width :]
    gain_part = jnp.sum(inner.astype(jnp.float32).T * moment, axis=0)
    return inner_part, gain_part


def per_device(
    question_states,
    question_ids,
    q_inner_weight,
    q_outer_weight,
    q_norm_gain,
    sql_states,
    sql_ids,
    s_inner_weight,
    s_outer_weight,
    s_norm_gain,
    positive_column,
):
    scale = 1.0 / math.sqrt(D)
    q_place = lax.axis_index("sa")
    s_place = lax.axis_index("pb")
    q_tokens = plane_gather(question_states[0, 0], 5)
    s_tokens = lax.all_gather(sql_states, "pb", axis=1, tiled=True)[0]
    q_rows = q_tokens.shape[0]
    s_rows = s_tokens.shape[0]

    q_hat, q_normed, q_pre, q_weights, q_pooled, q_resid = tower_forward(
        q_tokens, question_ids[0], q_inner_weight, q_norm_gain, False
    )
    s_hat, s_normed, s_pre, s_weights, s_pooled, s_resid = tower_forward(
        s_tokens, sql_ids[0], s_inner_weight, s_norm_gain, True
    )
    q_outer_f = q_outer_weight.astype(jnp.float32)
    s_outer_f = s_outer_weight.astype(jnp.float32)
    q_terms, s_terms = exchange(
        [
            (jnp.dot(q_pooled, q_outer_f, precision=HIGH), "sa", False),
            (jnp.dot(s_pooled, s_outer_f, precision=HIGH), "pb", False),
        ],
        1,
    )
    q_block = jnp.sum(q_terms, axis=0) + q_resid
    s_block = jnp.sum(s_terms, axis=0) + s_resid
    q_embed, q_pooled_all, s_embed, s_pooled_all, positive_all = exchange(
        [
            (q_block, "pb", False),
            (q_pooled, "pb", False),
            (s_block, "sa", False),
            (s_pooled, "sa", False),
            (positive_column.reshape(1, -1), "pb", False),
        ],
        2,
    )
    positive_all = positive_all.reshape(-1)
    q_embed = q_embed.reshape(-1, D)
    s_embed = s_embed.reshape(-1, D)
    q_pooled_all = q_pooled_all.reshape(-1, q_pooled.shape[-1])
    s_pooled_all = s_pooled_all.reshape(-1, s_pooled.shape[-1])
    score = scale * lax.dot_general(q_embed, s_embed, (((1,), (1,)), ((), ())), precision=HIGH)
    count = score.shape[0]
    match = (positive_all[:, None] == jnp.arange(count, dtype=jnp.int32)[None, :]).astype(
        jnp.float32
    )
    row_max = jnp.max(score, axis=1)
    row_lse = row_max + jnp.log(jnp.sum(jnp.exp(score - row_max[:, None]), axis=1))
    col_max = jnp.max(score, axis=0)
    col_lse = col_max + jnp.log(jnp.sum(jnp.exp(score - col_max[None, :]), axis=0))
    row_pos = jnp.sum(match * score, axis=1)
    col_pos = jnp.sum(match * score, axis=0)
    loss = (jnp.sum(row_lse - row_pos) + jnp.sum(col_lse - col_pos)) / (2.0 * count)
    dscore = 0.5 * (
        jnp.exp(score - row_lse[:, None]) + jnp.exp(score - col_lse[None, :]) - 2.0 * match
    )
    q_grad = scale * jnp.dot(dscore, s_embed, precision=HIGH)
    s_grad = scale * lax.dot_general(dscore, q_embed, (((0,), (0,)), ((), ())), precision=HIGH)

    q_outer_grad = lax.dot_general(q_pooled_all, q_grad, (((0,), (0,)), ((), ())), precision=HIGH)
    s_outer_grad = lax.dot_general(s_pooled_all, s_grad, (((0,), (0,)), ((), ())), precision=HIGH)
    q_grad_own = lax.dynamic_slice_in_dim(q_grad, s_place * q_rows, q_rows, 0)
    s_grad_own = lax.dynamic_slice_in_dim(s_grad, q_place * s_rows, s_rows, 0)
    q_hidden_grad = lax.dot_general(
        q_grad_own, q_outer_f, (((1,), (1,)), ((), ())), precision=HIGH
    )
    s_hidden_grad = lax.dot_general(
        s_grad_own, s_outer_f, (((1,), (1,)), ((), ())), precision=HIGH
    )
    q_inner_part, q_gain_part = tower_backward(
        q_hat, q_normed, q_pre, q_weights, q_inner_weight, q_hidden_grad
    )
    s_inner_part, s_gain_part = tower_backward(
        s_hat, s_normed, s_pre, s_weights, s_inner_weight, s_hidden_grad
    )
    q_pieces = q_inner_part.reshape(lax.axis_size("pb"), -1, q_inner_part.shape[-1])
    s_pieces = s_inner_part.reshape(lax.axis_size("sa"), -1, s_inner_part.shape[-1])
    gains = jnp.stack([q_gain_part, s_gain_part])
    q_pieces, s_pieces, gains = exchange(
        [
            (q_pieces.astype(jnp.bfloat16), "pb", True),
            (s_pieces.astype(jnp.bfloat16), "sa", True),
            (gains, "sa", False),
        ],
        3,
    )
    q_sums = jnp.sum(q_pieces.astype(jnp.float32), axis=0)
    s_sums = jnp.sum(s_pieces.astype(jnp.float32), axis=0)
    q_inner_grad, s_inner_grad, gains = exchange(
        [
            (q_sums.astype(jnp.bfloat16), "pb", False),
            (s_sums.astype(jnp.bfloat16), "sa", False),
            (jnp.sum(gains, axis=0), "pb", False),
        ],
        4,
    )
    q_inner_grad = q_inner_grad.astype(jnp.float32).reshape(q_inner_part.shape)
    s_inner_grad = s_inner_grad.astype(jnp.float32).reshape(s_inner_part.shape)
    gains = jnp.sum(gains, axis=0)
    q_gain_grad, s_gain_grad = gains[0], gains[1]
    return (loss, q_inner_grad, q_outer_grad, q_gain_grad, s_inner_grad, s_outer_grad, s_gain_grad)


def solution(mesh):
    placed = (
        P("pb", "sa", None, None),
        P("pb", None, None),
        P(None, "sa"),
        P("sa", None),
        P(),
        P("sa", "pb", None, None),
        P("sa", None, None),
        P(None, "pb"),
        P("pb", None),
        P(),
        P("pb"),
    )
    return jax.shard_map(
        per_device,
        mesh=mesh,
        in_specs=placed,
        out_specs=(P(), P(None, "sa"), P("sa", None), P(), P(None, "pb"), P("pb", None), P()),
        check_vma=False,
    )
```

```python
import functools
import math

import jax
import jax.numpy as jnp
from jax import lax
from jax.experimental import pallas as pl
from jax.experimental.pallas import tpu as pltpu
from jax.sharding import PartitionSpec as P

D = 768

MESH_AXES = ("pb", "sa")


def _peer(axis, p):
    return tuple(p if a == axis else lax.axis_index(a) for a in MESH_AXES)


def exchange(jobs, cid):
    arrays = [a for a, _, _ in jobs]
    kinds = [(ax, spread) for _, ax, spread in jobs]
    sizes = {ax: lax.axis_size(ax) for ax, _ in kinds}
    widest = max(sizes.values())
    count = len(jobs)

    def kernel(*refs):
        srcs, dsts = refs[:count], refs[count:2 * count]
        send, recv, local = refs[2 * count:]
        barrier = pltpu.get_barrier_semaphore()
        axes = list(dict.fromkeys(ax for ax, _ in kinds))
        total = 0
        for ax in axes:
            n = sizes[ax]
            me = lax.axis_index(ax)
            for s in range(1, n):
                pl.semaphore_signal(barrier, 1, device_id=_peer(ax, lax.rem(me + s, n)),
                                    device_id_type=pl.DeviceIdType.MESH)
            total += n - 1
        pl.semaphore_wait(barrier, total)
        started = []
        for t, (ax, spread) in enumerate(kinds):
            n = sizes[ax]
            me = lax.axis_index(ax)
            for s in range(1, n):
                p = lax.rem(me + s, n)
                src = srcs[t].at[p] if spread else srcs[t]
                c = pltpu.make_async_remote_copy(
                    src_ref=src, dst_ref=dsts[t].at[me], send_sem=send.at[t, s],
                    recv_sem=recv.at[t, s], device_id=_peer(ax, p),
                    device_id_type=pl.DeviceIdType.MESH)
                c.start()
                started.append(c)
            src = srcs[t].at[me] if spread else srcs[t]
            c = pltpu.make_async_copy(src, dsts[t].at[me], local.at[t])
            c.start()
            started.append(c)
        for c in started:
            c.wait()

    out_shape = []
    for a, (ax, spread) in zip(arrays, kinds):
        shape = a.shape if spread else (sizes[ax],) + a.shape
        out_shape.append(jax.ShapeDtypeStruct(shape, a.dtype))
    anywhere = pl.BlockSpec(memory_space=pl.ANY)
    return pl.pallas_call(
        kernel,
        out_shape=out_shape,
        in_specs=[anywhere] * count,
        out_specs=[anywhere] * count,
        scratch_shapes=[
            pltpu.SemaphoreType.DMA((count, widest)),
            pltpu.SemaphoreType.DMA((count, widest)),
            pltpu.SemaphoreType.DMA((count,)),
        ],
        compiler_params=pltpu.CompilerParams(collective_id=cid, has_side_effects=True),
    )(*arrays)


def plane_gather(block, cid):
    n = lax.axis_size("sa")
    rows = n // 4
    mesh_kind = pl.DeviceIdType.MESH

    def kernel(src, dst, ysend, yrecv, fsend, frecv, rsend, rrecv, zsend, zrecv, psend, precv, local):
        me = lax.axis_index("sa")
        core = lax.rem(me, 2)
        row = lax.rem(me // 2, rows)
        plane = me // (2 * rows)
        partner = me + 1 - 2 * core
        across = lax.rem(me + 2 * rows, n)

        def along(d):
            return plane * 2 * rows + lax.rem(row + d, rows) * 2 + core

        barrier = pltpu.get_barrier_semaphore()
        for peer in [partner, across] + [along(d) for d in range(1, rows)]:
            pl.semaphore_signal(barrier, 1, device_id=_peer("sa", peer), device_id_type=mesh_kind)
        pl.semaphore_wait(barrier, rows + 1)

        def send(source, slot, peer, s, r):
            c = pltpu.make_async_remote_copy(
                src_ref=source, dst_ref=dst.at[slot], send_sem=s, recv_sem=r,
                device_id=_peer("sa", peer), device_id_type=mesh_kind)
            c.start()
            return c

        own = pltpu.make_async_copy(src, dst.at[me], local.at[0])
        own.start()
        z_copy = send(src, me, across, zsend.at[0], zrecv.at[0])
        pair = send(src, me, partner, psend.at[0], precv.at[0])
        direct = [send(src, me, along(d), ysend.at[d], yrecv.at[d]) for d in range(1, rows)]
        z_copy.wait_recv()
        far = lax.rem(me + 2 * rows, n)
        relayed = [send(dst.at[far], far, along(d), fsend.at[d], frecv.at[d]) for d in range(1, rows)]
        handed = [send(dst.at[far], far, partner, rsend.at[0], rrecv.at[0])]
        for d in range(1, rows):
            direct[d - 1].wait_recv()
            slot = along(rows - d)
            handed.append(send(dst.at[slot], slot, partner, rsend.at[d], rrecv.at[d]))
        for d in range(1, rows):
            relayed[d - 1].wait_recv()
            slot = lax.rem(along(rows - d) + 2 * rows, n)
            handed.append(send(dst.at[slot], slot, partner, rsend.at[rows - 1 + d],
                               rrecv.at[rows - 1 + d]))
        for c in direct + relayed + [z_copy]:
            c.wait_send()
        for c in handed:
            c.wait()
        pair.wait()
        own.wait()

    anywhere = pl.BlockSpec(memory_space=pl.ANY)
    return pl.pallas_call(
        kernel,
        out_shape=jax.ShapeDtypeStruct((n,) + block.shape, block.dtype),
        in_specs=[anywhere],
        out_specs=anywhere,
        scratch_shapes=[
            pltpu.SemaphoreType.DMA((rows,)),
            pltpu.SemaphoreType.DMA((rows,)),
            pltpu.SemaphoreType.DMA((rows,)),
            pltpu.SemaphoreType.DMA((rows,)),
            pltpu.SemaphoreType.DMA((2 * rows - 1,)),
            pltpu.SemaphoreType.DMA((2 * rows - 1,)),
            pltpu.SemaphoreType.DMA((1,)),
            pltpu.SemaphoreType.DMA((1,)),
            pltpu.SemaphoreType.DMA((1,)),
            pltpu.SemaphoreType.DMA((1,)),
            pltpu.SemaphoreType.DMA((1,)),
        ],
        compiler_params=pltpu.CompilerParams(collective_id=cid, has_side_effects=True),
    )(block)


HIGH = lax.Precision.HIGHEST


def apply_rms_norm(input_float, norm_gain_vector, root_mean_square):
    if root_mean_square:
        input_normalized = input_float * lax.rsqrt(
            jnp.mean(input_float * input_float, axis=-1, keepdims=True) + 1e-06
        )
    else:
        mean_removed = input_float - jnp.mean(input_float, axis=-1, keepdims=True)
        input_normalized = mean_removed * lax.rsqrt(
            jnp.mean(mean_removed * mean_removed, axis=-1, keepdims=True) + 1e-05
        )
    return (input_normalized, (input_normalized * norm_gain_vector).astype(jnp.bfloat16))


def gelu_value(v):
    return 0.5 * v * (1.0 + lax.erf(v / math.sqrt(2.0)))


def gelu_slope(v):
    return 0.5 * (1.0 + lax.erf(v / math.sqrt(2.0))) + v * jnp.exp(-0.5 * v * v) / math.sqrt(
        2.0 * math.pi
    )


def pool_weights(ids):
    mask = (ids > 0).astype(jnp.float32)
    return mask / jnp.sum(mask, axis=-1, keepdims=True)


def tower_forward(tokens, ids, inner, gain, root_mean_square):
    count, length, width = tokens.shape
    input_float = tokens.astype(jnp.float32).reshape(count * length, width)
    input_normalized, normalized_rows = apply_rms_norm(input_float, gain, root_mean_square)
    pre = jnp.dot(normalized_rows, inner, preferred_element_type=jnp.float32)
    weights = pool_weights(ids)
    hidden = gelu_value(pre).reshape(count, length, -1)
    pooled = jnp.einsum("nt,ntf->nf", weights, hidden, precision=HIGH)
    resid = jnp.einsum(
        "nt,ntd->nd", weights, input_float.reshape(count, length, width), precision=HIGH
    )
    return input_normalized, normalized_rows, pre, weights, pooled, resid


def tower_backward(input_normalized, normalized_rows, pre, weights, inner, hidden_grad):
    count, length = weights.shape
    width = normalized_rows.shape[-1]
    slope = gelu_slope(pre).reshape(count, length, -1)
    dpre = (
        (weights[:, :, None] * hidden_grad[:, None, :] * slope)
        .reshape(count * length, -1)
        .astype(jnp.bfloat16)
    )
    high = lax.reduce_precision(input_normalized, exponent_bits=8, mantissa_bits=7)
    low = input_normalized - high
    rows = jnp.concatenate(
        [normalized_rows, high.astype(jnp.bfloat16), low.astype(jnp.bfloat16)], axis=1
    )
    both = lax.dot_general(
        dpre, rows, (((0,), (0,)), ((), ())), preferred_element_type=jnp.float32
    )
    inner_part = both[:, :width].T
    moment = both[:, width : 2 * width] + both[:, 2 * width :]
    gain_part = jnp.sum(inner.astype(jnp.float32).T * moment, axis=0)
    return inner_part, gain_part


def per_device(
    question_states,
    question_ids,
    q_inner_weight,
    q_outer_weight,
    q_norm_gain,
    sql_states,
    sql_ids,
    s_inner_weight,
    s_outer_weight,
    s_norm_gain,
    positive_column,
):
    scale = 1.0 / math.sqrt(D)
    q_place = lax.axis_index("sa")
    s_place = lax.axis_index("pb")
    q_tokens = plane_gather(question_states[0, 0], 5)
    s_tokens = lax.all_gather(sql_states, "pb", axis=1, tiled=True)[0]
    q_rows = q_tokens.shape[0]
    s_rows = s_tokens.shape[0]

    q_hat, q_normed, q_pre, q_weights, q_pooled, q_resid = tower_forward(
        q_tokens, question_ids[0], q_inner_weight, q_norm_gain, False
    )
    s_hat, s_normed, s_pre, s_weights, s_pooled, s_resid = tower_forward(
        s_tokens, sql_ids[0], s_inner_weight, s_norm_gain, True
    )
    q_outer_f = q_outer_weight.astype(jnp.float32)
    s_outer_f = s_outer_weight.astype(jnp.float32)
    q_terms, s_terms = exchange(
        [
            (jnp.dot(q_pooled, q_outer_f, precision=HIGH), "sa", False),
            (jnp.dot(s_pooled, s_outer_f, precision=HIGH), "pb", False),
        ],
        1,
    )
    q_block = jnp.sum(q_terms, axis=0) + q_resid
    s_block = jnp.sum(s_terms, axis=0) + s_resid
    q_embed, q_pooled_all, s_embed, s_pooled_all, positive_all = exchange(
        [
            (q_block, "pb", False),
            (q_pooled, "pb", False),
            (s_block, "sa", False),
            (s_pooled, "sa", False),
            (positive_column.reshape(1, -1), "pb", False),
        ],
        2,
    )
    positive_all = positive_all.reshape(-1)
    q_embed = q_embed.reshape(-1, D)
    s_embed = s_embed.reshape(-1, D)
    q_pooled_all = q_pooled_all.reshape(-1, q_pooled.shape[-1])
    s_pooled_all = s_pooled_all.reshape(-1, s_pooled.shape[-1])
    score = scale * lax.dot_general(q_embed, s_embed, (((1,), (1,)), ((), ())), precision=HIGH)
    count = score.shape[0]
    match = (positive_all[:, None] == jnp.arange(count, dtype=jnp.int32)[None, :]).astype(
        jnp.float32
    )
    row_max = jnp.max(score, axis=1)
    row_lse = row_max + jnp.log(jnp.sum(jnp.exp(score - row_max[:, None]), axis=1))
    col_max = jnp.max(score, axis=0)
    col_lse = col_max + jnp.log(jnp.sum(jnp.exp(score - col_max[None, :]), axis=0))
    row_pos = jnp.sum(match * score, axis=1)
    col_pos = jnp.sum(match * score, axis=0)
    loss = (jnp.sum(row_lse - row_pos) + jnp.sum(col_lse - col_pos)) / (2.0 * count)
    dscore = 0.5 * (
        jnp.exp(score - row_lse[:, None]) + jnp.exp(score - col_lse[None, :]) - 2.0 * match
    )
    q_grad = scale * jnp.dot(dscore, s_embed, precision=HIGH)
    s_grad = scale * lax.dot_general(dscore, q_embed, (((0,), (0,)), ((), ())), precision=HIGH)

    q_outer_grad = lax.dot_general(q_pooled_all, q_grad, (((0,), (0,)), ((), ())), precision=HIGH)
    s_outer_grad = lax.dot_general(s_pooled_all, s_grad, (((0,), (0,)), ((), ())), precision=HIGH)
    q_grad_own = lax.dynamic_slice_in_dim(q_grad, s_place * q_rows, q_rows, 0)
    s_grad_own = lax.dynamic_slice_in_dim(s_grad, q_place * s_rows, s_rows, 0)
    q_hidden_grad = lax.dot_general(
        q_grad_own, q_outer_f, (((1,), (1,)), ((), ())), precision=HIGH
    )
    s_hidden_grad = lax.dot_general(
        s_grad_own, s_outer_f, (((1,), (1,)), ((), ())), precision=HIGH
    )
    q_inner_part, q_gain_part = tower_backward(
        q_hat, q_normed, q_pre, q_weights, q_inner_weight, q_hidden_grad
    )
    s_inner_part, s_gain_part = tower_backward(
        s_hat, s_normed, s_pre, s_weights, s_inner_weight, s_hidden_grad
    )
    q_pieces = q_inner_part.reshape(lax.axis_size("pb"), -1, q_inner_part.shape[-1])
    s_pieces = s_inner_part.reshape(lax.axis_size("sa"), -1, s_inner_part.shape[-1])
    gains = jnp.stack([q_gain_part, s_gain_part])
    q_pieces, s_pieces, gains = exchange(
        [
            (q_pieces.astype(jnp.bfloat16), "pb", True),
            (s_pieces.astype(jnp.bfloat16), "sa", True),
            (gains, "sa", False),
        ],
        3,
    )
    q_sums = jnp.sum(q_pieces.astype(jnp.float32), axis=0)
    s_sums = jnp.sum(s_pieces.astype(jnp.float32), axis=0)
    q_inner_grad, s_inner_grad, gains = exchange(
        [
            (q_sums, "pb", False),
            (s_sums, "sa", False),
            (jnp.sum(gains, axis=0), "pb", False),
        ],
        4,
    )
    q_inner_grad = q_inner_grad.reshape(q_inner_part.shape)
    s_inner_grad = s_inner_grad.reshape(s_inner_part.shape)
    gains = jnp.sum(gains, axis=0)
    q_gain_grad, s_gain_grad = gains[0], gains[1]
    return (loss, q_inner_grad, q_outer_grad, q_gain_grad, s_inner_grad, s_outer_grad, s_gain_grad)


def solution(mesh):
    placed = (
        P("pb", "sa", None, None),
        P("pb", None, None),
        P(None, "sa"),
        P("sa", None),
        P(),
        P("sa", "pb", None, None),
        P("sa", None, None),
        P(None, "pb"),
        P("pb", None),
        P(),
        P("pb"),
    )
    return jax.shard_map(
        per_device,
        mesh=mesh,
        in_specs=placed,
        out_specs=(P(), P(None, "sa"), P("sa", None), P(), P(None, "pb"), P("pb", None), P()),
        check_vma=False,
    )
```

```python
import functools
import math

import jax
import jax.numpy as jnp
from jax import lax
from jax.experimental import pallas as pl
from jax.experimental.pallas import tpu as pltpu
from jax.sharding import PartitionSpec as P

D = 768

MESH_AXES = ("pb", "sa")


def _peer(axis, p):
    return tuple(p if a == axis else lax.axis_index(a) for a in MESH_AXES)


def exchange(jobs, cid):
    arrays = [a for a, _, _ in jobs]
    kinds = [(ax, spread) for _, ax, spread in jobs]
    sizes = {ax: lax.axis_size(ax) for ax, _ in kinds}
    widest = max(sizes.values())
    count = len(jobs)

    def kernel(*refs):
        srcs, dsts = refs[:count], refs[count:2 * count]
        send, recv, local = refs[2 * count:]
        barrier = pltpu.get_barrier_semaphore()
        axes = list(dict.fromkeys(ax for ax, _ in kinds))
        total = 0
        for ax in axes:
            n = sizes[ax]
            me = lax.axis_index(ax)
            for s in range(1, n):
                pl.semaphore_signal(barrier, 1, device_id=_peer(ax, lax.rem(me + s, n)),
                                    device_id_type=pl.DeviceIdType.MESH)
            total += n - 1
        pl.semaphore_wait(barrier, total)
        started = []
        for t, (ax, spread) in enumerate(kinds):
            n = sizes[ax]
            me = lax.axis_index(ax)
            for s in range(1, n):
                p = lax.rem(me + s, n)
                src = srcs[t].at[p] if spread else srcs[t]
                c = pltpu.make_async_remote_copy(
                    src_ref=src, dst_ref=dsts[t].at[me], send_sem=send.at[t, s],
                    recv_sem=recv.at[t, s], device_id=_peer(ax, p),
                    device_id_type=pl.DeviceIdType.MESH)
                c.start()
                started.append(c)
            src = srcs[t].at[me] if spread else srcs[t]
            c = pltpu.make_async_copy(src, dsts[t].at[me], local.at[t])
            c.start()
            started.append(c)
        for c in started:
            c.wait()

    out_shape = []
    for a, (ax, spread) in zip(arrays, kinds):
        shape = a.shape if spread else (sizes[ax],) + a.shape
        out_shape.append(jax.ShapeDtypeStruct(shape, a.dtype))
    anywhere = pl.BlockSpec(memory_space=pl.ANY)
    return pl.pallas_call(
        kernel,
        out_shape=out_shape,
        in_specs=[anywhere] * count,
        out_specs=[anywhere] * count,
        scratch_shapes=[
            pltpu.SemaphoreType.DMA((count, widest)),
            pltpu.SemaphoreType.DMA((count, widest)),
            pltpu.SemaphoreType.DMA((count,)),
        ],
        compiler_params=pltpu.CompilerParams(collective_id=cid, has_side_effects=True),
    )(*arrays)


def plane_gather(block, cid):
    n = lax.axis_size("sa")
    rows = n // 4
    mesh_kind = pl.DeviceIdType.MESH

    def kernel(src, dst, ysend, yrecv, fsend, frecv, rsend, rrecv, zsend, zrecv, psend, precv, local):
        me = lax.axis_index("sa")
        core = lax.rem(me, 2)
        row = lax.rem(me // 2, rows)
        plane = me // (2 * rows)
        partner = me + 1 - 2 * core
        across = lax.rem(me + 2 * rows, n)

        def along(d):
            return plane * 2 * rows + lax.rem(row + d, rows) * 2 + core

        barrier = pltpu.get_barrier_semaphore()
        for peer in [partner, across] + [along(d) for d in range(1, rows)]:
            pl.semaphore_signal(barrier, 1, device_id=_peer("sa", peer), device_id_type=mesh_kind)
        pl.semaphore_wait(barrier, rows + 1)

        def send(source, slot, peer, s, r):
            c = pltpu.make_async_remote_copy(
                src_ref=source, dst_ref=dst.at[slot], send_sem=s, recv_sem=r,
                device_id=_peer("sa", peer), device_id_type=mesh_kind)
            c.start()
            return c

        own = pltpu.make_async_copy(src, dst.at[me], local.at[0])
        own.start()
        z_copy = send(src, me, across, zsend.at[0], zrecv.at[0])
        pair = send(src, me, partner, psend.at[0], precv.at[0])
        direct = [send(src, me, along(d), ysend.at[d], yrecv.at[d]) for d in range(1, rows)]
        z_copy.wait_recv()
        far = lax.rem(me + 2 * rows, n)
        relayed = [send(dst.at[far], far, along(d), fsend.at[d], frecv.at[d]) for d in range(1, rows)]
        handed = [send(dst.at[far], far, partner, rsend.at[0], rrecv.at[0])]
        for d in range(1, rows):
            direct[d - 1].wait_recv()
            slot = along(rows - d)
            handed.append(send(dst.at[slot], slot, partner, rsend.at[d], rrecv.at[d]))
        for d in range(1, rows):
            relayed[d - 1].wait_recv()
            slot = lax.rem(along(rows - d) + 2 * rows, n)
            handed.append(send(dst.at[slot], slot, partner, rsend.at[rows - 1 + d],
                               rrecv.at[rows - 1 + d]))
        for c in direct + relayed + [z_copy]:
            c.wait_send()
        for c in handed:
            c.wait()
        pair.wait()
        own.wait()

    anywhere = pl.BlockSpec(memory_space=pl.ANY)
    return pl.pallas_call(
        kernel,
        out_shape=jax.ShapeDtypeStruct((n,) + block.shape, block.dtype),
        in_specs=[anywhere],
        out_specs=anywhere,
        scratch_shapes=[
            pltpu.SemaphoreType.DMA((rows,)),
            pltpu.SemaphoreType.DMA((rows,)),
            pltpu.SemaphoreType.DMA((rows,)),
            pltpu.SemaphoreType.DMA((rows,)),
            pltpu.SemaphoreType.DMA((2 * rows - 1,)),
            pltpu.SemaphoreType.DMA((2 * rows - 1,)),
            pltpu.SemaphoreType.DMA((1,)),
            pltpu.SemaphoreType.DMA((1,)),
            pltpu.SemaphoreType.DMA((1,)),
            pltpu.SemaphoreType.DMA((1,)),
            pltpu.SemaphoreType.DMA((1,)),
        ],
        compiler_params=pltpu.CompilerParams(collective_id=cid, has_side_effects=True),
    )(block)


HIGH = lax.Precision.HIGHEST


def apply_rms_norm(input_float, norm_gain_vector, root_mean_square):
    if root_mean_square:
        input_normalized = input_float * lax.rsqrt(
            jnp.mean(input_float * input_float, axis=-1, keepdims=True) + 1e-06
        )
    else:
        mean_removed = input_float - jnp.mean(input_float, axis=-1, keepdims=True)
        input_normalized = mean_removed * lax.rsqrt(
            jnp.mean(mean_removed * mean_removed, axis=-1, keepdims=True) + 1e-05
        )
    return (input_normalized, (input_normalized * norm_gain_vector).astype(jnp.bfloat16))


def gelu_value(v):
    return 0.5 * v * (1.0 + lax.erf(v / math.sqrt(2.0)))


def gelu_slope(v):
    return 0.5 * (1.0 + lax.erf(v / math.sqrt(2.0))) + v * jnp.exp(-0.5 * v * v) / math.sqrt(
        2.0 * math.pi
    )


def pool_weights(ids):
    mask = (ids > 0).astype(jnp.float32)
    return mask / jnp.sum(mask, axis=-1, keepdims=True)


def tower_forward(tokens, ids, inner, gain, root_mean_square):
    count, length, width = tokens.shape
    input_float = tokens.astype(jnp.float32).reshape(count * length, width)
    input_normalized, normalized_rows = apply_rms_norm(input_float, gain, root_mean_square)
    pre = jnp.dot(normalized_rows, inner, preferred_element_type=jnp.float32)
    weights = pool_weights(ids)
    hidden = gelu_value(pre).reshape(count, length, -1)
    pooled = jnp.einsum("nt,ntf->nf", weights, hidden, precision=HIGH)
    resid = jnp.einsum(
        "nt,ntd->nd", weights, input_float.reshape(count, length, width), precision=HIGH
    )
    return input_normalized, normalized_rows, pre, weights, pooled, resid


def tower_backward(input_normalized, normalized_rows, pre, weights, inner, hidden_grad):
    count, length = weights.shape
    width = normalized_rows.shape[-1]
    slope = gelu_slope(pre).reshape(count, length, -1)
    dpre = (
        (weights[:, :, None] * hidden_grad[:, None, :] * slope)
        .reshape(count * length, -1)
        .astype(jnp.bfloat16)
    )
    high = lax.reduce_precision(input_normalized, exponent_bits=8, mantissa_bits=7)
    low = input_normalized - high
    rows = jnp.concatenate(
        [normalized_rows, high.astype(jnp.bfloat16), low.astype(jnp.bfloat16)], axis=1
    )
    both = lax.dot_general(
        dpre, rows, (((0,), (0,)), ((), ())), preferred_element_type=jnp.float32
    )
    inner_part = both[:, :width].T
    moment = both[:, width : 2 * width] + both[:, 2 * width :]
    gain_part = jnp.sum(inner.astype(jnp.float32).T * moment, axis=0)
    return inner_part, gain_part


def per_device(
    question_states,
    question_ids,
    q_inner_weight,
    q_outer_weight,
    q_norm_gain,
    sql_states,
    sql_ids,
    s_inner_weight,
    s_outer_weight,
    s_norm_gain,
    positive_column,
):
    scale = 1.0 / math.sqrt(D)
    q_place = lax.axis_index("sa")
    s_place = lax.axis_index("pb")
    q_tokens = plane_gather(question_states[0, 0], 5)
    s_tokens = lax.all_gather(sql_states, "pb", axis=1, tiled=True)[0]
    q_rows = q_tokens.shape[0]
    s_rows = s_tokens.shape[0]

    q_hat, q_normed, q_pre, q_weights, q_pooled, q_resid = tower_forward(
        q_tokens, question_ids[0], q_inner_weight, q_norm_gain, False
    )
    s_hat, s_normed, s_pre, s_weights, s_pooled, s_resid = tower_forward(
        s_tokens, sql_ids[0], s_inner_weight, s_norm_gain, True
    )
    q_outer_f = q_outer_weight.astype(jnp.float32)
    s_outer_f = s_outer_weight.astype(jnp.float32)
    (q_terms,) = exchange([(jnp.dot(q_pooled, q_outer_f, precision=HIGH), "sa", False)], 1)
    (s_terms,) = exchange([(jnp.dot(s_pooled, s_outer_f, precision=HIGH), "pb", False)], 6)
    q_block = jnp.sum(q_terms, axis=0) + q_resid
    s_block = jnp.sum(s_terms, axis=0) + s_resid
    q_embed, q_pooled_all, s_embed, s_pooled_all, positive_all = exchange(
        [
            (q_block, "pb", False),
            (q_pooled, "pb", False),
            (s_block, "sa", False),
            (s_pooled, "sa", False),
            (positive_column.reshape(1, -1), "pb", False),
        ],
        2,
    )
    positive_all = positive_all.reshape(-1)
    q_embed = q_embed.reshape(-1, D)
    s_embed = s_embed.reshape(-1, D)
    q_pooled_all = q_pooled_all.reshape(-1, q_pooled.shape[-1])
    s_pooled_all = s_pooled_all.reshape(-1, s_pooled.shape[-1])
    score = scale * lax.dot_general(q_embed, s_embed, (((1,), (1,)), ((), ())), precision=HIGH)
    count = score.shape[0]
    match = (positive_all[:, None] == jnp.arange(count, dtype=jnp.int32)[None, :]).astype(
        jnp.float32
    )
    row_max = jnp.max(score, axis=1)
    row_lse = row_max + jnp.log(jnp.sum(jnp.exp(score - row_max[:, None]), axis=1))
    col_max = jnp.max(score, axis=0)
    col_lse = col_max + jnp.log(jnp.sum(jnp.exp(score - col_max[None, :]), axis=0))
    row_pos = jnp.sum(match * score, axis=1)
    col_pos = jnp.sum(match * score, axis=0)
    loss = (jnp.sum(row_lse - row_pos) + jnp.sum(col_lse - col_pos)) / (2.0 * count)
    dscore = 0.5 * (
        jnp.exp(score - row_lse[:, None]) + jnp.exp(score - col_lse[None, :]) - 2.0 * match
    )
    q_grad = scale * jnp.dot(dscore, s_embed, precision=HIGH)
    s_grad = scale * lax.dot_general(dscore, q_embed, (((0,), (0,)), ((), ())), precision=HIGH)

    q_outer_grad = lax.dot_general(q_pooled_all, q_grad, (((0,), (0,)), ((), ())), precision=HIGH)
    s_outer_grad = lax.dot_general(s_pooled_all, s_grad, (((0,), (0,)), ((), ())), precision=HIGH)
    q_grad_own = lax.dynamic_slice_in_dim(q_grad, s_place * q_rows, q_rows, 0)
    s_grad_own = lax.dynamic_slice_in_dim(s_grad, q_place * s_rows, s_rows, 0)
    q_hidden_grad = lax.dot_general(
        q_grad_own, q_outer_f, (((1,), (1,)), ((), ())), precision=HIGH
    )
    s_hidden_grad = lax.dot_general(
        s_grad_own, s_outer_f, (((1,), (1,)), ((), ())), precision=HIGH
    )
    q_inner_part, q_gain_part = tower_backward(
        q_hat, q_normed, q_pre, q_weights, q_inner_weight, q_hidden_grad
    )
    s_inner_part, s_gain_part = tower_backward(
        s_hat, s_normed, s_pre, s_weights, s_inner_weight, s_hidden_grad
    )
    q_pieces = q_inner_part.reshape(lax.axis_size("pb"), -1, q_inner_part.shape[-1])
    s_pieces = s_inner_part.reshape(lax.axis_size("sa"), -1, s_inner_part.shape[-1])
    gains = jnp.stack([q_gain_part, s_gain_part])
    q_pieces, s_pieces, gains = exchange(
        [
            (q_pieces.astype(jnp.bfloat16), "pb", True),
            (s_pieces.astype(jnp.bfloat16), "sa", True),
            (gains, "sa", False),
        ],
        3,
    )
    q_sums = jnp.sum(q_pieces.astype(jnp.float32), axis=0)
    s_sums = jnp.sum(s_pieces.astype(jnp.float32), axis=0)
    q_inner_grad, s_inner_grad, gains = exchange(
        [
            (q_sums.astype(jnp.bfloat16), "pb", False),
            (s_sums.astype(jnp.bfloat16), "sa", False),
            (jnp.sum(gains, axis=0), "pb", False),
        ],
        4,
    )
    q_inner_grad = q_inner_grad.astype(jnp.float32).reshape(q_inner_part.shape)
    s_inner_grad = s_inner_grad.astype(jnp.float32).reshape(s_inner_part.shape)
    gains = jnp.sum(gains, axis=0)
    q_gain_grad, s_gain_grad = gains[0], gains[1]
    return (loss, q_inner_grad, q_outer_grad, q_gain_grad, s_inner_grad, s_outer_grad, s_gain_grad)


def solution(mesh):
    placed = (
        P("pb", "sa", None, None),
        P("pb", None, None),
        P(None, "sa"),
        P("sa", None),
        P(),
        P("sa", "pb", None, None),
        P("sa", None, None),
        P(None, "pb"),
        P("pb", None),
        P(),
        P("pb"),
    )
    return jax.shard_map(
        per_device,
        mesh=mesh,
        in_specs=placed,
        out_specs=(P(), P(None, "sa"), P("sa", None), P(), P(None, "pb"), P("pb", None), P()),
        check_vma=False,
    )
```

```python
import functools
import math

import jax
import jax.numpy as jnp
from jax import lax
from jax.experimental import pallas as pl
from jax.experimental.pallas import tpu as pltpu
from jax.sharding import PartitionSpec as P

D = 768

MESH_AXES = ("pb", "sa")


def _peer(axis, p):
    return tuple(p if a == axis else lax.axis_index(a) for a in MESH_AXES)


def exchange(jobs, cid):
    arrays = [a for a, _, _ in jobs]
    kinds = [(ax, spread) for _, ax, spread in jobs]
    sizes = {ax: lax.axis_size(ax) for ax, _ in kinds}
    widest = max(sizes.values())
    count = len(jobs)

    def kernel(*refs):
        srcs, dsts = refs[:count], refs[count:2 * count]
        send, recv, local = refs[2 * count:]
        barrier = pltpu.get_barrier_semaphore()
        axes = list(dict.fromkeys(ax for ax, _ in kinds))
        total = 0
        for ax in axes:
            n = sizes[ax]
            me = lax.axis_index(ax)
            for s in range(1, n):
                pl.semaphore_signal(barrier, 1, device_id=_peer(ax, lax.rem(me + s, n)),
                                    device_id_type=pl.DeviceIdType.MESH)
            total += n - 1
        pl.semaphore_wait(barrier, total)
        started = []
        for t, (ax, spread) in enumerate(kinds):
            n = sizes[ax]
            me = lax.axis_index(ax)
            for s in range(1, n):
                p = lax.rem(me + s, n)
                src = srcs[t].at[p] if spread else srcs[t]
                c = pltpu.make_async_remote_copy(
                    src_ref=src, dst_ref=dsts[t].at[me], send_sem=send.at[t, s],
                    recv_sem=recv.at[t, s], device_id=_peer(ax, p),
                    device_id_type=pl.DeviceIdType.MESH)
                c.start()
                started.append(c)
            src = srcs[t].at[me] if spread else srcs[t]
            c = pltpu.make_async_copy(src, dsts[t].at[me], local.at[t])
            c.start()
            started.append(c)
        for c in started:
            c.wait()

    out_shape = []
    for a, (ax, spread) in zip(arrays, kinds):
        shape = a.shape if spread else (sizes[ax],) + a.shape
        out_shape.append(jax.ShapeDtypeStruct(shape, a.dtype))
    anywhere = pl.BlockSpec(memory_space=pl.ANY)
    return pl.pallas_call(
        kernel,
        out_shape=out_shape,
        in_specs=[anywhere] * count,
        out_specs=[anywhere] * count,
        scratch_shapes=[
            pltpu.SemaphoreType.DMA((count, widest)),
            pltpu.SemaphoreType.DMA((count, widest)),
            pltpu.SemaphoreType.DMA((count,)),
        ],
        compiler_params=pltpu.CompilerParams(collective_id=cid, has_side_effects=True),
    )(*arrays)


def plane_gather(block, cid):
    n = lax.axis_size("sa")
    rows = n // 4
    mesh_kind = pl.DeviceIdType.MESH

    def kernel(src, dst, ysend, yrecv, fsend, frecv, rsend, rrecv, zsend, zrecv, psend, precv, local):
        me = lax.axis_index("sa")
        core = lax.rem(me, 2)
        row = lax.rem(me // 2, rows)
        plane = me // (2 * rows)
        partner = me + 1 - 2 * core
        across = lax.rem(me + 2 * rows, n)

        def along(d):
            return plane * 2 * rows + lax.rem(row + d, rows) * 2 + core

        barrier = pltpu.get_barrier_semaphore()
        for peer in [partner, across] + [along(d) for d in range(1, rows)]:
            pl.semaphore_signal(barrier, 1, device_id=_peer("sa", peer), device_id_type=mesh_kind)
        pl.semaphore_wait(barrier, rows + 1)

        def send(source, slot, peer, s, r):
            c = pltpu.make_async_remote_copy(
                src_ref=source, dst_ref=dst.at[slot], send_sem=s, recv_sem=r,
                device_id=_peer("sa", peer), device_id_type=mesh_kind)
            c.start()
            return c

        own = pltpu.make_async_copy(src, dst.at[me], local.at[0])
        own.start()
        z_copy = send(src, me, across, zsend.at[0], zrecv.at[0])
        pair = send(src, me, partner, psend.at[0], precv.at[0])
        direct = [send(src, me, along(d), ysend.at[d], yrecv.at[d]) for d in range(1, rows)]
        z_copy.wait_recv()
        far = lax.rem(me + 2 * rows, n)
        relayed = [send(dst.at[far], far, along(d), fsend.at[d], frecv.at[d]) for d in range(1, rows)]
        handed = [send(dst.at[far], far, partner, rsend.at[0], rrecv.at[0])]
        for d in range(1, rows):
            direct[d - 1].wait_recv()
            slot = along(rows - d)
            handed.append(send(dst.at[slot], slot, partner, rsend.at[d], rrecv.at[d]))
        for d in range(1, rows):
            relayed[d - 1].wait_recv()
            slot = lax.rem(along(rows - d) + 2 * rows, n)
            handed.append(send(dst.at[slot], slot, partner, rsend.at[rows - 1 + d],
                               rrecv.at[rows - 1 + d]))
        for c in direct + relayed + [z_copy]:
            c.wait_send()
        for c in handed:
            c.wait()
        pair.wait()
        own.wait()

    anywhere = pl.BlockSpec(memory_space=pl.ANY)
    return pl.pallas_call(
        kernel,
        out_shape=jax.ShapeDtypeStruct((n,) + block.shape, block.dtype),
        in_specs=[anywhere],
        out_specs=anywhere,
        scratch_shapes=[
            pltpu.SemaphoreType.DMA((rows,)),
            pltpu.SemaphoreType.DMA((rows,)),
            pltpu.SemaphoreType.DMA((rows,)),
            pltpu.SemaphoreType.DMA((rows,)),
            pltpu.SemaphoreType.DMA((2 * rows - 1,)),
            pltpu.SemaphoreType.DMA((2 * rows - 1,)),
            pltpu.SemaphoreType.DMA((1,)),
            pltpu.SemaphoreType.DMA((1,)),
            pltpu.SemaphoreType.DMA((1,)),
            pltpu.SemaphoreType.DMA((1,)),
            pltpu.SemaphoreType.DMA((1,)),
        ],
        compiler_params=pltpu.CompilerParams(collective_id=cid, has_side_effects=True),
    )(block)


HIGH = lax.Precision.HIGHEST


def apply_rms_norm(input_float, norm_gain_vector, root_mean_square):
    if root_mean_square:
        input_normalized = input_float * lax.rsqrt(
            jnp.mean(input_float * input_float, axis=-1, keepdims=True) + 1e-06
        )
    else:
        mean_removed = input_float - jnp.mean(input_float, axis=-1, keepdims=True)
        input_normalized = mean_removed * lax.rsqrt(
            jnp.mean(mean_removed * mean_removed, axis=-1, keepdims=True) + 1e-05
        )
    return (input_normalized, (input_normalized * norm_gain_vector).astype(jnp.bfloat16))


def gelu_value(v):
    return 0.5 * v * (1.0 + lax.erf(v / math.sqrt(2.0)))


def gelu_slope(v):
    return 0.5 * (1.0 + lax.erf(v / math.sqrt(2.0))) + v * jnp.exp(-0.5 * v * v) / math.sqrt(
        2.0 * math.pi
    )


def pool_weights(ids):
    mask = (ids > 0).astype(jnp.float32)
    return mask / jnp.sum(mask, axis=-1, keepdims=True)


def tower_forward(tokens, ids, inner, gain, root_mean_square):
    count, length, width = tokens.shape
    input_float = tokens.astype(jnp.float32).reshape(count * length, width)
    input_normalized, normalized_rows = apply_rms_norm(input_float, gain, root_mean_square)
    pre = jnp.dot(normalized_rows, inner, preferred_element_type=jnp.float32)
    weights = pool_weights(ids)
    hidden = gelu_value(pre).reshape(count, length, -1)
    pooled = jnp.einsum("nt,ntf->nf", weights, hidden, precision=HIGH)
    resid = jnp.einsum(
        "nt,ntd->nd", weights, input_float.reshape(count, length, width), precision=HIGH
    )
    return input_normalized, normalized_rows, pre, weights, pooled, resid


def tower_backward(input_normalized, normalized_rows, pre, weights, inner, hidden_grad):
    count, length = weights.shape
    width = normalized_rows.shape[-1]
    slope = gelu_slope(pre).reshape(count, length, -1)
    dpre = (
        (weights[:, :, None] * hidden_grad[:, None, :] * slope)
        .reshape(count * length, -1)
        .astype(jnp.bfloat16)
    )
    high = lax.reduce_precision(input_normalized, exponent_bits=8, mantissa_bits=7)
    low = input_normalized - high
    rows = jnp.concatenate(
        [normalized_rows, high.astype(jnp.bfloat16), low.astype(jnp.bfloat16)], axis=1
    )
    both = lax.dot_general(
        dpre, rows, (((0,), (0,)), ((), ())), preferred_element_type=jnp.float32
    )
    inner_part = both[:, :width].T
    moment = both[:, width : 2 * width] + both[:, 2 * width :]
    gain_part = jnp.sum(inner.astype(jnp.float32).T * moment, axis=0)
    return inner_part, gain_part


def per_device(
    question_states,
    question_ids,
    q_inner_weight,
    q_outer_weight,
    q_norm_gain,
    sql_states,
    sql_ids,
    s_inner_weight,
    s_outer_weight,
    s_norm_gain,
    positive_column,
):
    scale = 1.0 / math.sqrt(D)
    q_place = lax.axis_index("sa")
    s_place = lax.axis_index("pb")
    q_tokens = plane_gather(question_states[0, 0], 5)
    s_tokens = lax.all_gather(sql_states, "pb", axis=1, tiled=True)[0]
    q_rows = q_tokens.shape[0]
    s_rows = s_tokens.shape[0]

    q_hat, q_normed, q_pre, q_weights, q_pooled, q_resid = tower_forward(
        q_tokens, question_ids[0], q_inner_weight, q_norm_gain, False
    )
    s_hat, s_normed, s_pre, s_weights, s_pooled, s_resid = tower_forward(
        s_tokens, sql_ids[0], s_inner_weight, s_norm_gain, True
    )
    q_outer_f = q_outer_weight.astype(jnp.float32)
    s_outer_f = s_outer_weight.astype(jnp.float32)
    q_terms = plane_gather(jnp.dot(q_pooled, q_outer_f, precision=HIGH), 1)
    (s_terms,) = exchange([(jnp.dot(s_pooled, s_outer_f, precision=HIGH), "pb", False)], 6)
    q_block = jnp.sum(q_terms, axis=0) + q_resid
    s_block = jnp.sum(s_terms, axis=0) + s_resid
    q_embed, q_pooled_all, s_embed, s_pooled_all, positive_all = exchange(
        [
            (q_block, "pb", False),
            (q_pooled, "pb", False),
            (s_block, "sa", False),
            (s_pooled, "sa", False),
            (positive_column.reshape(1, -1), "pb", False),
        ],
        2,
    )
    positive_all = positive_all.reshape(-1)
    q_embed = q_embed.reshape(-1, D)
    s_embed = s_embed.reshape(-1, D)
    q_pooled_all = q_pooled_all.reshape(-1, q_pooled.shape[-1])
    s_pooled_all = s_pooled_all.reshape(-1, s_pooled.shape[-1])
    score = scale * lax.dot_general(q_embed, s_embed, (((1,), (1,)), ((), ())), precision=HIGH)
    count = score.shape[0]
    match = (positive_all[:, None] == jnp.arange(count, dtype=jnp.int32)[None, :]).astype(
        jnp.float32
    )
    row_max = jnp.max(score, axis=1)
    row_lse = row_max + jnp.log(jnp.sum(jnp.exp(score - row_max[:, None]), axis=1))
    col_max = jnp.max(score, axis=0)
    col_lse = col_max + jnp.log(jnp.sum(jnp.exp(score - col_max[None, :]), axis=0))
    row_pos = jnp.sum(match * score, axis=1)
    col_pos = jnp.sum(match * score, axis=0)
    loss = (jnp.sum(row_lse - row_pos) + jnp.sum(col_lse - col_pos)) / (2.0 * count)
    dscore = 0.5 * (
        jnp.exp(score - row_lse[:, None]) + jnp.exp(score - col_lse[None, :]) - 2.0 * match
    )
    q_grad = scale * jnp.dot(dscore, s_embed, precision=HIGH)
    s_grad = scale * lax.dot_general(dscore, q_embed, (((0,), (0,)), ((), ())), precision=HIGH)

    q_outer_grad = lax.dot_general(q_pooled_all, q_grad, (((0,), (0,)), ((), ())), precision=HIGH)
    s_outer_grad = lax.dot_general(s_pooled_all, s_grad, (((0,), (0,)), ((), ())), precision=HIGH)
    q_grad_own = lax.dynamic_slice_in_dim(q_grad, s_place * q_rows, q_rows, 0)
    s_grad_own = lax.dynamic_slice_in_dim(s_grad, q_place * s_rows, s_rows, 0)
    q_hidden_grad = lax.dot_general(
        q_grad_own, q_outer_f, (((1,), (1,)), ((), ())), precision=HIGH
    )
    s_hidden_grad = lax.dot_general(
        s_grad_own, s_outer_f, (((1,), (1,)), ((), ())), precision=HIGH
    )
    q_inner_part, q_gain_part = tower_backward(
        q_hat, q_normed, q_pre, q_weights, q_inner_weight, q_hidden_grad
    )
    s_inner_part, s_gain_part = tower_backward(
        s_hat, s_normed, s_pre, s_weights, s_inner_weight, s_hidden_grad
    )
    q_pieces = q_inner_part.reshape(lax.axis_size("pb"), -1, q_inner_part.shape[-1])
    s_pieces = s_inner_part.reshape(lax.axis_size("sa"), -1, s_inner_part.shape[-1])
    gains = jnp.stack([q_gain_part, s_gain_part])
    q_pieces, s_pieces, gains = exchange(
        [
            (q_pieces.astype(jnp.bfloat16), "pb", True),
            (s_pieces.astype(jnp.bfloat16), "sa", True),
            (gains, "sa", False),
        ],
        3,
    )
    q_sums = jnp.sum(q_pieces.astype(jnp.float32), axis=0)
    s_sums = jnp.sum(s_pieces.astype(jnp.float32), axis=0)
    q_inner_grad, s_inner_grad, gains = exchange(
        [
            (q_sums.astype(jnp.bfloat16), "pb", False),
            (s_sums.astype(jnp.bfloat16), "sa", False),
            (jnp.sum(gains, axis=0), "pb", False),
        ],
        4,
    )
    q_inner_grad = q_inner_grad.astype(jnp.float32).reshape(q_inner_part.shape)
    s_inner_grad = s_inner_grad.astype(jnp.float32).reshape(s_inner_part.shape)
    gains = jnp.sum(gains, axis=0)
    q_gain_grad, s_gain_grad = gains[0], gains[1]
    return (loss, q_inner_grad, q_outer_grad, q_gain_grad, s_inner_grad, s_outer_grad, s_gain_grad)


def solution(mesh):
    placed = (
        P("pb", "sa", None, None),
        P("pb", None, None),
        P(None, "sa"),
        P("sa", None),
        P(),
        P("sa", "pb", None, None),
        P("sa", None, None),
        P(None, "pb"),
        P("pb", None),
        P(),
        P("pb"),
    )
    return jax.shard_map(
        per_device,
        mesh=mesh,
        in_specs=placed,
        out_specs=(P(), P(None, "sa"), P("sa", None), P(), P(None, "pb"), P("pb", None), P()),
        check_vma=False,
    )
```

```python
import functools
import math

import jax
import jax.numpy as jnp
from jax import lax
from jax.experimental import pallas as pl
from jax.experimental.pallas import tpu as pltpu
from jax.sharding import PartitionSpec as P

D = 768

MESH_AXES = ("pb", "sa")


def _peer(axis, p):
    return tuple(p if a == axis else lax.axis_index(a) for a in MESH_AXES)


def exchange(jobs, cid):
    arrays = [a for a, _, _ in jobs]
    kinds = [(ax, spread) for _, ax, spread in jobs]
    sizes = {ax: lax.axis_size(ax) for ax, _ in kinds}
    widest = max(sizes.values())
    count = len(jobs)

    def kernel(*refs):
        srcs, dsts = refs[:count], refs[count:2 * count]
        send, recv, local = refs[2 * count:]
        barrier = pltpu.get_barrier_semaphore()
        axes = list(dict.fromkeys(ax for ax, _ in kinds))
        total = 0
        for ax in axes:
            n = sizes[ax]
            me = lax.axis_index(ax)
            for s in range(1, n):
                pl.semaphore_signal(barrier, 1, device_id=_peer(ax, lax.rem(me + s, n)),
                                    device_id_type=pl.DeviceIdType.MESH)
            total += n - 1
        pl.semaphore_wait(barrier, total)
        started = []
        for t, (ax, spread) in enumerate(kinds):
            n = sizes[ax]
            me = lax.axis_index(ax)
            for s in range(1, n):
                p = lax.rem(me + s, n)
                src = srcs[t].at[p] if spread else srcs[t]
                c = pltpu.make_async_remote_copy(
                    src_ref=src, dst_ref=dsts[t].at[me], send_sem=send.at[t, s],
                    recv_sem=recv.at[t, s], device_id=_peer(ax, p),
                    device_id_type=pl.DeviceIdType.MESH)
                c.start()
                started.append(c)
            src = srcs[t].at[me] if spread else srcs[t]
            c = pltpu.make_async_copy(src, dsts[t].at[me], local.at[t])
            c.start()
            started.append(c)
        for c in started:
            c.wait()

    out_shape = []
    for a, (ax, spread) in zip(arrays, kinds):
        shape = a.shape if spread else (sizes[ax],) + a.shape
        out_shape.append(jax.ShapeDtypeStruct(shape, a.dtype))
    anywhere = pl.BlockSpec(memory_space=pl.ANY)
    return pl.pallas_call(
        kernel,
        out_shape=out_shape,
        in_specs=[anywhere] * count,
        out_specs=[anywhere] * count,
        scratch_shapes=[
            pltpu.SemaphoreType.DMA((count, widest)),
            pltpu.SemaphoreType.DMA((count, widest)),
            pltpu.SemaphoreType.DMA((count,)),
        ],
        compiler_params=pltpu.CompilerParams(collective_id=cid, has_side_effects=True),
    )(*arrays)


def plane_gather(block, cid):
    n = lax.axis_size("sa")
    rows = n // 4
    mesh_kind = pl.DeviceIdType.MESH

    def kernel(src, dst, ysend, yrecv, fsend, frecv, rsend, rrecv, zsend, zrecv, psend, precv, local):
        me = lax.axis_index("sa")
        core = lax.rem(me, 2)
        row = lax.rem(me // 2, rows)
        plane = me // (2 * rows)
        partner = me + 1 - 2 * core
        across = lax.rem(me + 2 * rows, n)

        def along(d):
            return plane * 2 * rows + lax.rem(row + d, rows) * 2 + core

        barrier = pltpu.get_barrier_semaphore()
        for peer in [partner, across] + [along(d) for d in range(1, rows)]:
            pl.semaphore_signal(barrier, 1, device_id=_peer("sa", peer), device_id_type=mesh_kind)
        pl.semaphore_wait(barrier, rows + 1)

        def send(source, slot, peer, s, r):
            c = pltpu.make_async_remote_copy(
                src_ref=source, dst_ref=dst.at[slot], send_sem=s, recv_sem=r,
                device_id=_peer("sa", peer), device_id_type=mesh_kind)
            c.start()
            return c

        own = pltpu.make_async_copy(src, dst.at[me], local.at[0])
        own.start()
        z_copy = send(src, me, across, zsend.at[0], zrecv.at[0])
        pair = send(src, me, partner, psend.at[0], precv.at[0])
        direct = [send(src, me, along(d), ysend.at[d], yrecv.at[d]) for d in range(1, rows)]
        z_copy.wait_recv()
        far = lax.rem(me + 2 * rows, n)
        relayed = [send(dst.at[far], far, along(d), fsend.at[d], frecv.at[d]) for d in range(1, rows)]
        handed = [send(dst.at[far], far, partner, rsend.at[0], rrecv.at[0])]
        for d in range(1, rows):
            direct[d - 1].wait_recv()
            slot = along(rows - d)
            handed.append(send(dst.at[slot], slot, partner, rsend.at[d], rrecv.at[d]))
        for d in range(1, rows):
            relayed[d - 1].wait_recv()
            slot = lax.rem(along(rows - d) + 2 * rows, n)
            handed.append(send(dst.at[slot], slot, partner, rsend.at[rows - 1 + d],
                               rrecv.at[rows - 1 + d]))
        for c in direct + relayed + [z_copy]:
            c.wait_send()
        for c in handed:
            c.wait()
        pair.wait()
        own.wait()

    anywhere = pl.BlockSpec(memory_space=pl.ANY)
    return pl.pallas_call(
        kernel,
        out_shape=jax.ShapeDtypeStruct((n,) + block.shape, block.dtype),
        in_specs=[anywhere],
        out_specs=anywhere,
        scratch_shapes=[
            pltpu.SemaphoreType.DMA((rows,)),
            pltpu.SemaphoreType.DMA((rows,)),
            pltpu.SemaphoreType.DMA((rows,)),
            pltpu.SemaphoreType.DMA((rows,)),
            pltpu.SemaphoreType.DMA((2 * rows - 1,)),
            pltpu.SemaphoreType.DMA((2 * rows - 1,)),
            pltpu.SemaphoreType.DMA((1,)),
            pltpu.SemaphoreType.DMA((1,)),
            pltpu.SemaphoreType.DMA((1,)),
            pltpu.SemaphoreType.DMA((1,)),
            pltpu.SemaphoreType.DMA((1,)),
        ],
        compiler_params=pltpu.CompilerParams(collective_id=cid, has_side_effects=True),
    )(block)


HIGH = lax.Precision.HIGHEST


def apply_rms_norm(input_float, norm_gain_vector, root_mean_square):
    if root_mean_square:
        input_normalized = input_float * lax.rsqrt(
            jnp.mean(input_float * input_float, axis=-1, keepdims=True) + 1e-06
        )
    else:
        mean_removed = input_float - jnp.mean(input_float, axis=-1, keepdims=True)
        input_normalized = mean_removed * lax.rsqrt(
            jnp.mean(mean_removed * mean_removed, axis=-1, keepdims=True) + 1e-05
        )
    return (input_normalized, (input_normalized * norm_gain_vector).astype(jnp.bfloat16))


def gelu_value(v):
    return 0.5 * v * (1.0 + lax.erf(v / math.sqrt(2.0)))


def gelu_slope(v):
    return 0.5 * (1.0 + lax.erf(v / math.sqrt(2.0))) + v * jnp.exp(-0.5 * v * v) / math.sqrt(
        2.0 * math.pi
    )


def pool_weights(ids):
    mask = (ids > 0).astype(jnp.float32)
    return mask / jnp.sum(mask, axis=-1, keepdims=True)


def tower_forward(tokens, ids, inner, gain, root_mean_square):
    count, length, width = tokens.shape
    input_float = tokens.astype(jnp.float32).reshape(count * length, width)
    input_normalized, normalized_rows = apply_rms_norm(input_float, gain, root_mean_square)
    pre = jnp.dot(normalized_rows, inner, preferred_element_type=jnp.float32)
    weights = pool_weights(ids)
    hidden = gelu_value(pre).reshape(count, length, -1)
    pooled = jnp.einsum("nt,ntf->nf", weights, hidden, precision=HIGH)
    resid = jnp.einsum(
        "nt,ntd->nd", weights, input_float.reshape(count, length, width), precision=HIGH
    )
    return input_normalized, normalized_rows, pre, weights, pooled, resid


def tower_backward(input_normalized, normalized_rows, pre, weights, inner, hidden_grad):
    count, length = weights.shape
    width = normalized_rows.shape[-1]
    slope = gelu_slope(pre).reshape(count, length, -1)
    dpre = (
        (weights[:, :, None] * hidden_grad[:, None, :] * slope)
        .reshape(count * length, -1)
        .astype(jnp.bfloat16)
    )
    high = lax.reduce_precision(input_normalized, exponent_bits=8, mantissa_bits=7)
    low = input_normalized - high
    rows = jnp.concatenate(
        [normalized_rows, high.astype(jnp.bfloat16), low.astype(jnp.bfloat16)], axis=1
    )
    both = lax.dot_general(
        dpre, rows, (((0,), (0,)), ((), ())), preferred_element_type=jnp.float32
    )
    inner_part = both[:, :width].T
    moment = both[:, width : 2 * width] + both[:, 2 * width :]
    gain_part = jnp.sum(inner.astype(jnp.float32).T * moment, axis=0)
    return inner_part, gain_part


def per_device(
    question_states,
    question_ids,
    q_inner_weight,
    q_outer_weight,
    q_norm_gain,
    sql_states,
    sql_ids,
    s_inner_weight,
    s_outer_weight,
    s_norm_gain,
    positive_column,
):
    scale = 1.0 / math.sqrt(D)
    q_place = lax.axis_index("sa")
    s_place = lax.axis_index("pb")
    q_tokens = plane_gather(question_states[0, 0], 5)
    s_tokens = lax.all_gather(sql_states, "pb", axis=1, tiled=True)[0]
    q_rows = q_tokens.shape[0]
    s_rows = s_tokens.shape[0]

    q_hat, q_normed, q_pre, q_weights, q_pooled, q_resid = tower_forward(
        q_tokens, question_ids[0], q_inner_weight, q_norm_gain, False
    )
    s_hat, s_normed, s_pre, s_weights, s_pooled, s_resid = tower_forward(
        s_tokens, sql_ids[0], s_inner_weight, s_norm_gain, True
    )
    q_outer_f = q_outer_weight.astype(jnp.float32)
    s_outer_f = s_outer_weight.astype(jnp.float32)
    q_terms = plane_gather(jnp.dot(q_pooled, q_outer_f, precision=HIGH), 1)
    (s_terms,) = exchange([(jnp.dot(s_pooled, s_outer_f, precision=HIGH), "pb", False)], 6)
    q_block = jnp.sum(q_terms, axis=0) + q_resid
    s_block = jnp.sum(s_terms, axis=0) + s_resid
    q_embed, q_pooled_all, positive_all = exchange(
        [
            (q_block, "pb", False),
            (q_pooled, "pb", False),
            (positive_column.reshape(1, -1), "pb", False),
        ],
        2,
    )
    s_width = s_pooled.shape[-1]
    s_pack = jnp.concatenate(
        [s_block, s_pooled, jnp.zeros((s_block.shape[0], 128 - (D + s_width) % 128), jnp.float32)],
        axis=1,
    )
    s_pack = plane_gather(s_pack, 7)
    s_embed = s_pack[:, :, :D]
    s_pooled_all = s_pack[:, :, D : D + s_width]
    positive_all = positive_all.reshape(-1)
    q_embed = q_embed.reshape(-1, D)
    s_embed = s_embed.reshape(-1, D)
    q_pooled_all = q_pooled_all.reshape(-1, q_pooled.shape[-1])
    s_pooled_all = s_pooled_all.reshape(-1, s_pooled.shape[-1])
    score = scale * lax.dot_general(q_embed, s_embed, (((1,), (1,)), ((), ())), precision=HIGH)
    count = score.shape[0]
    match = (positive_all[:, None] == jnp.arange(count, dtype=jnp.int32)[None, :]).astype(
        jnp.float32
    )
    row_max = jnp.max(score, axis=1)
    row_lse = row_max + jnp.log(jnp.sum(jnp.exp(score - row_max[:, None]), axis=1))
    col_max = jnp.max(score, axis=0)
    col_lse = col_max + jnp.log(jnp.sum(jnp.exp(score - col_max[None, :]), axis=0))
    row_pos = jnp.sum(match * score, axis=1)
    col_pos = jnp.sum(match * score, axis=0)
    loss = (jnp.sum(row_lse - row_pos) + jnp.sum(col_lse - col_pos)) / (2.0 * count)
    dscore = 0.5 * (
        jnp.exp(score - row_lse[:, None]) + jnp.exp(score - col_lse[None, :]) - 2.0 * match
    )
    q_grad = scale * jnp.dot(dscore, s_embed, precision=HIGH)
    s_grad = scale * lax.dot_general(dscore, q_embed, (((0,), (0,)), ((), ())), precision=HIGH)

    q_outer_grad = lax.dot_general(q_pooled_all, q_grad, (((0,), (0,)), ((), ())), precision=HIGH)
    s_outer_grad = lax.dot_general(s_pooled_all, s_grad, (((0,), (0,)), ((), ())), precision=HIGH)
    q_grad_own = lax.dynamic_slice_in_dim(q_grad, s_place * q_rows, q_rows, 0)
    s_grad_own = lax.dynamic_slice_in_dim(s_grad, q_place * s_rows, s_rows, 0)
    q_hidden_grad = lax.dot_general(
        q_grad_own, q_outer_f, (((1,), (1,)), ((), ())), precision=HIGH
    )
    s_hidden_grad = lax.dot_general(
        s_grad_own, s_outer_f, (((1,), (1,)), ((), ())), precision=HIGH
    )
    q_inner_part, q_gain_part = tower_backward(
        q_hat, q_normed, q_pre, q_weights, q_inner_weight, q_hidden_grad
    )
    s_inner_part, s_gain_part = tower_backward(
        s_hat, s_normed, s_pre, s_weights, s_inner_weight, s_hidden_grad
    )
    q_pieces = q_inner_part.reshape(lax.axis_size("pb"), -1, q_inner_part.shape[-1])
    s_pieces = s_inner_part.reshape(lax.axis_size("sa"), -1, s_inner_part.shape[-1])
    gains = jnp.stack([q_gain_part, s_gain_part])
    q_pieces, s_pieces, gains = exchange(
        [
            (q_pieces.astype(jnp.bfloat16), "pb", True),
            (s_pieces.astype(jnp.bfloat16), "sa", True),
            (gains, "sa", False),
        ],
        3,
    )
    q_sums = jnp.sum(q_pieces.astype(jnp.float32), axis=0)
    s_sums = jnp.sum(s_pieces.astype(jnp.float32), axis=0)
    q_inner_grad, s_inner_grad, gains = exchange(
        [
            (q_sums.astype(jnp.bfloat16), "pb", False),
            (s_sums.astype(jnp.bfloat16), "sa", False),
            (jnp.sum(gains, axis=0), "pb", False),
        ],
        4,
    )
    q_inner_grad = q_inner_grad.astype(jnp.float32).reshape(q_inner_part.shape)
    s_inner_grad = s_inner_grad.astype(jnp.float32).reshape(s_inner_part.shape)
    gains = jnp.sum(gains, axis=0)
    q_gain_grad, s_gain_grad = gains[0], gains[1]
    return (loss, q_inner_grad, q_outer_grad, q_gain_grad, s_inner_grad, s_outer_grad, s_gain_grad)


def solution(mesh):
    placed = (
        P("pb", "sa", None, None),
        P("pb", None, None),
        P(None, "sa"),
        P("sa", None),
        P(),
        P("sa", "pb", None, None),
        P("sa", None, None),
        P(None, "pb"),
        P("pb", None),
        P(),
        P("pb"),
    )
    return jax.shard_map(
        per_device,
        mesh=mesh,
        in_specs=placed,
        out_specs=(P(), P(None, "sa"), P("sa", None), P(), P(None, "pb"), P("pb", None), P()),
        check_vma=False,
    )
```

```python
import functools
import math

import jax
import jax.numpy as jnp
from jax import lax
from jax.experimental import pallas as pl
from jax.experimental.pallas import tpu as pltpu
from jax.sharding import PartitionSpec as P

D = 768

MESH_AXES = ("pb", "sa")


def _peer(axis, p):
    return tuple(p if a == axis else lax.axis_index(a) for a in MESH_AXES)


def exchange(jobs, cid):
    arrays = [a for a, _, _ in jobs]
    kinds = [(ax, spread) for _, ax, spread in jobs]
    sizes = {ax: lax.axis_size(ax) for ax, _ in kinds}
    widest = max(sizes.values())
    count = len(jobs)

    def kernel(*refs):
        srcs, dsts = refs[:count], refs[count:2 * count]
        send, recv, local = refs[2 * count:]
        barrier = pltpu.get_barrier_semaphore()
        axes = list(dict.fromkeys(ax for ax, _ in kinds))
        total = 0
        for ax in axes:
            n = sizes[ax]
            me = lax.axis_index(ax)
            for s in range(1, n):
                pl.semaphore_signal(barrier, 1, device_id=_peer(ax, lax.rem(me + s, n)),
                                    device_id_type=pl.DeviceIdType.MESH)
            total += n - 1
        pl.semaphore_wait(barrier, total)
        started = []
        for t, (ax, spread) in enumerate(kinds):
            n = sizes[ax]
            me = lax.axis_index(ax)
            for s in range(1, n):
                p = lax.rem(me + s, n)
                src = srcs[t].at[p] if spread else srcs[t]
                c = pltpu.make_async_remote_copy(
                    src_ref=src, dst_ref=dsts[t].at[me], send_sem=send.at[t, s],
                    recv_sem=recv.at[t, s], device_id=_peer(ax, p),
                    device_id_type=pl.DeviceIdType.MESH)
                c.start()
                started.append(c)
            src = srcs[t].at[me] if spread else srcs[t]
            c = pltpu.make_async_copy(src, dsts[t].at[me], local.at[t])
            c.start()
            started.append(c)
        for c in started:
            c.wait()

    out_shape = []
    for a, (ax, spread) in zip(arrays, kinds):
        shape = a.shape if spread else (sizes[ax],) + a.shape
        out_shape.append(jax.ShapeDtypeStruct(shape, a.dtype))
    anywhere = pl.BlockSpec(memory_space=pl.ANY)
    return pl.pallas_call(
        kernel,
        out_shape=out_shape,
        in_specs=[anywhere] * count,
        out_specs=[anywhere] * count,
        scratch_shapes=[
            pltpu.SemaphoreType.DMA((count, widest)),
            pltpu.SemaphoreType.DMA((count, widest)),
            pltpu.SemaphoreType.DMA((count,)),
        ],
        compiler_params=pltpu.CompilerParams(collective_id=cid, has_side_effects=True),
    )(*arrays)


def plane_gather(block, cid):
    n = lax.axis_size("sa")
    rows = n // 4
    mesh_kind = pl.DeviceIdType.MESH

    def kernel(src, dst, ysend, yrecv, fsend, frecv, rsend, rrecv, zsend, zrecv, psend, precv, local):
        me = lax.axis_index("sa")
        core = lax.rem(me, 2)
        row = lax.rem(me // 2, rows)
        plane = me // (2 * rows)
        partner = me + 1 - 2 * core
        across = lax.rem(me + 2 * rows, n)

        def along(d):
            return plane * 2 * rows + lax.rem(row + d, rows) * 2 + core

        barrier = pltpu.get_barrier_semaphore()
        for peer in [partner, across] + [along(d) for d in range(1, rows)]:
            pl.semaphore_signal(barrier, 1, device_id=_peer("sa", peer), device_id_type=mesh_kind)
        pl.semaphore_wait(barrier, rows + 1)

        def send(source, slot, peer, s, r):
            c = pltpu.make_async_remote_copy(
                src_ref=source, dst_ref=dst.at[slot], send_sem=s, recv_sem=r,
                device_id=_peer("sa", peer), device_id_type=mesh_kind)
            c.start()
            return c

        own = pltpu.make_async_copy(src, dst.at[me], local.at[0])
        own.start()
        z_copy = send(src, me, across, zsend.at[0], zrecv.at[0])
        pair = send(src, me, partner, psend.at[0], precv.at[0])
        direct = [send(src, me, along(d), ysend.at[d], yrecv.at[d]) for d in range(1, rows)]
        z_copy.wait_recv()
        far = lax.rem(me + 2 * rows, n)
        relayed = [send(dst.at[far], far, along(d), fsend.at[d], frecv.at[d]) for d in range(1, rows)]
        handed = [send(dst.at[far], far, partner, rsend.at[0], rrecv.at[0])]
        for d in range(1, rows):
            direct[d - 1].wait_recv()
            slot = along(rows - d)
            handed.append(send(dst.at[slot], slot, partner, rsend.at[d], rrecv.at[d]))
        for d in range(1, rows):
            relayed[d - 1].wait_recv()
            slot = lax.rem(along(rows - d) + 2 * rows, n)
            handed.append(send(dst.at[slot], slot, partner, rsend.at[rows - 1 + d],
                               rrecv.at[rows - 1 + d]))
        for c in direct + relayed + [z_copy]:
            c.wait_send()
        for c in handed:
            c.wait()
        pair.wait()
        own.wait()

    anywhere = pl.BlockSpec(memory_space=pl.ANY)
    return pl.pallas_call(
        kernel,
        out_shape=jax.ShapeDtypeStruct((n,) + block.shape, block.dtype),
        in_specs=[anywhere],
        out_specs=anywhere,
        scratch_shapes=[
            pltpu.SemaphoreType.DMA((rows,)),
            pltpu.SemaphoreType.DMA((rows,)),
            pltpu.SemaphoreType.DMA((rows,)),
            pltpu.SemaphoreType.DMA((rows,)),
            pltpu.SemaphoreType.DMA((2 * rows - 1,)),
            pltpu.SemaphoreType.DMA((2 * rows - 1,)),
            pltpu.SemaphoreType.DMA((1,)),
            pltpu.SemaphoreType.DMA((1,)),
            pltpu.SemaphoreType.DMA((1,)),
            pltpu.SemaphoreType.DMA((1,)),
            pltpu.SemaphoreType.DMA((1,)),
        ],
        compiler_params=pltpu.CompilerParams(collective_id=cid, has_side_effects=True),
    )(block)


HIGH = lax.Precision.HIGHEST


def apply_rms_norm(input_float, norm_gain_vector, root_mean_square):
    if root_mean_square:
        input_normalized = input_float * lax.rsqrt(
            jnp.mean(input_float * input_float, axis=-1, keepdims=True) + 1e-06
        )
    else:
        mean_removed = input_float - jnp.mean(input_float, axis=-1, keepdims=True)
        input_normalized = mean_removed * lax.rsqrt(
            jnp.mean(mean_removed * mean_removed, axis=-1, keepdims=True) + 1e-05
        )
    return (input_normalized, (input_normalized * norm_gain_vector).astype(jnp.bfloat16))


def gelu_value(v):
    return 0.5 * v * (1.0 + lax.erf(v / math.sqrt(2.0)))


def gelu_slope(v):
    return 0.5 * (1.0 + lax.erf(v / math.sqrt(2.0))) + v * jnp.exp(-0.5 * v * v) / math.sqrt(
        2.0 * math.pi
    )


def pool_weights(ids):
    mask = (ids > 0).astype(jnp.float32)
    return mask / jnp.sum(mask, axis=-1, keepdims=True)


def tower_forward(tokens, ids, inner, gain, root_mean_square):
    count, length, width = tokens.shape
    input_float = tokens.astype(jnp.float32).reshape(count * length, width)
    input_normalized, normalized_rows = apply_rms_norm(input_float, gain, root_mean_square)
    pre = jnp.dot(normalized_rows, inner, preferred_element_type=jnp.float32)
    weights = pool_weights(ids)
    hidden = gelu_value(pre).reshape(count, length, -1)
    pooled = jnp.einsum("nt,ntf->nf", weights, hidden, precision=HIGH)
    resid = jnp.einsum(
        "nt,ntd->nd", weights, input_float.reshape(count, length, width), precision=HIGH
    )
    return input_normalized, normalized_rows, pre, weights, pooled, resid


def tower_backward(input_normalized, normalized_rows, pre, weights, inner, hidden_grad):
    count, length = weights.shape
    width = normalized_rows.shape[-1]
    slope = gelu_slope(pre).reshape(count, length, -1)
    dpre = (
        (weights[:, :, None] * hidden_grad[:, None, :] * slope)
        .reshape(count * length, -1)
        .astype(jnp.bfloat16)
    )
    high = lax.reduce_precision(input_normalized, exponent_bits=8, mantissa_bits=7)
    low = input_normalized - high
    rows = jnp.concatenate(
        [normalized_rows, high.astype(jnp.bfloat16), low.astype(jnp.bfloat16)], axis=1
    )
    both = lax.dot_general(
        dpre, rows, (((0,), (0,)), ((), ())), preferred_element_type=jnp.float32
    )
    inner_part = both[:, :width].T
    moment = both[:, width : 2 * width] + both[:, 2 * width :]
    gain_part = jnp.sum(inner.astype(jnp.float32).T * moment, axis=0)
    return inner_part, gain_part


def per_device(
    question_states,
    question_ids,
    q_inner_weight,
    q_outer_weight,
    q_norm_gain,
    sql_states,
    sql_ids,
    s_inner_weight,
    s_outer_weight,
    s_norm_gain,
    positive_column,
):
    scale = 1.0 / math.sqrt(D)
    q_place = lax.axis_index("sa")
    s_place = lax.axis_index("pb")
    q_tokens = plane_gather(question_states[0, 0], 5)
    s_tokens = lax.all_gather(sql_states, "pb", axis=1, tiled=True)[0]
    q_rows = q_tokens.shape[0]
    s_rows = s_tokens.shape[0]

    q_hat, q_normed, q_pre, q_weights, q_pooled, q_resid = tower_forward(
        q_tokens, question_ids[0], q_inner_weight, q_norm_gain, False
    )
    s_hat, s_normed, s_pre, s_weights, s_pooled, s_resid = tower_forward(
        s_tokens, sql_ids[0], s_inner_weight, s_norm_gain, True
    )
    q_outer_f = q_outer_weight.astype(jnp.float32)
    s_outer_f = s_outer_weight.astype(jnp.float32)
    q_terms = plane_gather(jnp.dot(q_pooled, q_outer_f, precision=HIGH), 1)
    q_block = jnp.sum(q_terms, axis=0) + q_resid
    q_embed, q_pooled_all, positive_all, s_terms = exchange(
        [
            (q_block, "pb", False),
            (q_pooled, "pb", False),
            (positive_column.reshape(1, -1), "pb", False),
            (jnp.dot(s_pooled, s_outer_f, precision=HIGH), "pb", False),
        ],
        2,
    )
    s_block = jnp.sum(s_terms, axis=0) + s_resid
    s_width = s_pooled.shape[-1]
    s_pack = jnp.concatenate(
        [s_block, s_pooled, jnp.zeros((s_block.shape[0], 128 - (D + s_width) % 128), jnp.float32)],
        axis=1,
    )
    s_pack = plane_gather(s_pack, 7)
    s_embed = s_pack[:, :, :D]
    s_pooled_all = s_pack[:, :, D : D + s_width]
    positive_all = positive_all.reshape(-1)
    q_embed = q_embed.reshape(-1, D)
    s_embed = s_embed.reshape(-1, D)
    q_pooled_all = q_pooled_all.reshape(-1, q_pooled.shape[-1])
    s_pooled_all = s_pooled_all.reshape(-1, s_pooled.shape[-1])
    score = scale * lax.dot_general(q_embed, s_embed, (((1,), (1,)), ((), ())), precision=HIGH)
    count = score.shape[0]
    match = (positive_all[:, None] == jnp.arange(count, dtype=jnp.int32)[None, :]).astype(
        jnp.float32
    )
    row_max = jnp.max(score, axis=1)
    row_lse = row_max + jnp.log(jnp.sum(jnp.exp(score - row_max[:, None]), axis=1))
    col_max = jnp.max(score, axis=0)
    col_lse = col_max + jnp.log(jnp.sum(jnp.exp(score - col_max[None, :]), axis=0))
    row_pos = jnp.sum(match * score, axis=1)
    col_pos = jnp.sum(match * score, axis=0)
    loss = (jnp.sum(row_lse - row_pos) + jnp.sum(col_lse - col_pos)) / (2.0 * count)
    dscore = 0.5 * (
        jnp.exp(score - row_lse[:, None]) + jnp.exp(score - col_lse[None, :]) - 2.0 * match
    )
    q_grad = scale * jnp.dot(dscore, s_embed, precision=HIGH)
    s_grad = scale * lax.dot_general(dscore, q_embed, (((0,), (0,)), ((), ())), precision=HIGH)

    q_outer_grad = lax.dot_general(q_pooled_all, q_grad, (((0,), (0,)), ((), ())), precision=HIGH)
    s_outer_grad = lax.dot_general(s_pooled_all, s_grad, (((0,), (0,)), ((), ())), precision=HIGH)
    q_grad_own = lax.dynamic_slice_in_dim(q_grad, s_place * q_rows, q_rows, 0)
    s_grad_own = lax.dynamic_slice_in_dim(s_grad, q_place * s_rows, s_rows, 0)
    q_hidden_grad = lax.dot_general(
        q_grad_own, q_outer_f, (((1,), (1,)), ((), ())), precision=HIGH
    )
    s_hidden_grad = lax.dot_general(
        s_grad_own, s_outer_f, (((1,), (1,)), ((), ())), precision=HIGH
    )
    q_inner_part, q_gain_part = tower_backward(
        q_hat, q_normed, q_pre, q_weights, q_inner_weight, q_hidden_grad
    )
    s_inner_part, s_gain_part = tower_backward(
        s_hat, s_normed, s_pre, s_weights, s_inner_weight, s_hidden_grad
    )
    q_pieces = q_inner_part.reshape(lax.axis_size("pb"), -1, q_inner_part.shape[-1])
    s_pieces = s_inner_part.reshape(lax.axis_size("sa"), -1, s_inner_part.shape[-1])
    gains = jnp.stack([q_gain_part, s_gain_part])
    q_pieces, s_pieces, gains = exchange(
        [
            (q_pieces.astype(jnp.bfloat16), "pb", True),
            (s_pieces.astype(jnp.bfloat16), "sa", True),
            (gains, "sa", False),
        ],
        3,
    )
    q_sums = jnp.sum(q_pieces.astype(jnp.float32), axis=0)
    s_sums = jnp.sum(s_pieces.astype(jnp.float32), axis=0)
    q_inner_grad, s_inner_grad, gains = exchange(
        [
            (q_sums.astype(jnp.bfloat16), "pb", False),
            (s_sums.astype(jnp.bfloat16), "sa", False),
            (jnp.sum(gains, axis=0), "pb", False),
        ],
        4,
    )
    q_inner_grad = q_inner_grad.astype(jnp.float32).reshape(q_inner_part.shape)
    s_inner_grad = s_inner_grad.astype(jnp.float32).reshape(s_inner_part.shape)
    gains = jnp.sum(gains, axis=0)
    q_gain_grad, s_gain_grad = gains[0], gains[1]
    return (loss, q_inner_grad, q_outer_grad, q_gain_grad, s_inner_grad, s_outer_grad, s_gain_grad)


def solution(mesh):
    placed = (
        P("pb", "sa", None, None),
        P("pb", None, None),
        P(None, "sa"),
        P("sa", None),
        P(),
        P("sa", "pb", None, None),
        P("sa", None, None),
        P(None, "pb"),
        P("pb", None),
        P(),
        P("pb"),
    )
    return jax.shard_map(
        per_device,
        mesh=mesh,
        in_specs=placed,
        out_specs=(P(), P(None, "sa"), P("sa", None), P(), P(None, "pb"), P("pb", None), P()),
        check_vma=False,
    )
```

```python
import functools
import math

import jax
import jax.numpy as jnp
from jax import lax
from jax.experimental import pallas as pl
from jax.experimental.pallas import tpu as pltpu
from jax.sharding import PartitionSpec as P

D = 768

MESH_AXES = ("pb", "sa")


def _peer(axis, p):
    return tuple(p if a == axis else lax.axis_index(a) for a in MESH_AXES)


def exchange(jobs, cid):
    arrays = [a for a, _, _ in jobs]
    kinds = [(ax, spread) for _, ax, spread in jobs]
    sizes = {ax: lax.axis_size(ax) for ax, _ in kinds}
    widest = max(sizes.values())
    count = len(jobs)

    def kernel(*refs):
        srcs, dsts = refs[:count], refs[count:2 * count]
        send, recv, local = refs[2 * count:]
        barrier = pltpu.get_barrier_semaphore()
        axes = list(dict.fromkeys(ax for ax, _ in kinds))
        total = 0
        for ax in axes:
            n = sizes[ax]
            me = lax.axis_index(ax)
            for s in range(1, n):
                pl.semaphore_signal(barrier, 1, device_id=_peer(ax, lax.rem(me + s, n)),
                                    device_id_type=pl.DeviceIdType.MESH)
            total += n - 1
        pl.semaphore_wait(barrier, total)
        started = []
        for t, (ax, spread) in enumerate(kinds):
            n = sizes[ax]
            me = lax.axis_index(ax)
            for s in range(1, n):
                p = lax.rem(me + s, n)
                src = srcs[t].at[p] if spread else srcs[t]
                c = pltpu.make_async_remote_copy(
                    src_ref=src, dst_ref=dsts[t].at[me], send_sem=send.at[t, s],
                    recv_sem=recv.at[t, s], device_id=_peer(ax, p),
                    device_id_type=pl.DeviceIdType.MESH)
                c.start()
                started.append(c)
            src = srcs[t].at[me] if spread else srcs[t]
            c = pltpu.make_async_copy(src, dsts[t].at[me], local.at[t])
            c.start()
            started.append(c)
        for c in started:
            c.wait()

    out_shape = []
    for a, (ax, spread) in zip(arrays, kinds):
        shape = a.shape if spread else (sizes[ax],) + a.shape
        out_shape.append(jax.ShapeDtypeStruct(shape, a.dtype))
    anywhere = pl.BlockSpec(memory_space=pl.ANY)
    return pl.pallas_call(
        kernel,
        out_shape=out_shape,
        in_specs=[anywhere] * count,
        out_specs=[anywhere] * count,
        scratch_shapes=[
            pltpu.SemaphoreType.DMA((count, widest)),
            pltpu.SemaphoreType.DMA((count, widest)),
            pltpu.SemaphoreType.DMA((count,)),
        ],
        compiler_params=pltpu.CompilerParams(collective_id=cid, has_side_effects=True),
    )(*arrays)


def plane_gather(block, cid):
    n = lax.axis_size("sa")
    rows = n // 4
    mesh_kind = pl.DeviceIdType.MESH

    def kernel(src, dst, ysend, yrecv, fsend, frecv, rsend, rrecv, zsend, zrecv, psend, precv, local):
        me = lax.axis_index("sa")
        core = lax.rem(me, 2)
        row = lax.rem(me // 2, rows)
        plane = me // (2 * rows)
        partner = me + 1 - 2 * core
        across = lax.rem(me + 2 * rows, n)

        def along(d):
            return plane * 2 * rows + lax.rem(row + d, rows) * 2 + core

        barrier = pltpu.get_barrier_semaphore()
        for peer in [partner, across] + [along(d) for d in range(1, rows)]:
            pl.semaphore_signal(barrier, 1, device_id=_peer("sa", peer), device_id_type=mesh_kind)
        pl.semaphore_wait(barrier, rows + 1)

        def send(source, slot, peer, s, r):
            c = pltpu.make_async_remote_copy(
                src_ref=source, dst_ref=dst.at[slot], send_sem=s, recv_sem=r,
                device_id=_peer("sa", peer), device_id_type=mesh_kind)
            c.start()
            return c

        own = pltpu.make_async_copy(src, dst.at[me], local.at[0])
        own.start()
        z_copy = send(src, me, across, zsend.at[0], zrecv.at[0])
        pair = send(src, me, partner, psend.at[0], precv.at[0])
        direct = [send(src, me, along(d), ysend.at[d], yrecv.at[d]) for d in range(1, rows)]
        z_copy.wait_recv()
        far = lax.rem(me + 2 * rows, n)
        relayed = [send(dst.at[far], far, along(d), fsend.at[d], frecv.at[d]) for d in range(1, rows)]
        handed = [send(dst.at[far], far, partner, rsend.at[0], rrecv.at[0])]
        for d in range(1, rows):
            direct[d - 1].wait_recv()
            slot = along(rows - d)
            handed.append(send(dst.at[slot], slot, partner, rsend.at[d], rrecv.at[d]))
        for d in range(1, rows):
            relayed[d - 1].wait_recv()
            slot = lax.rem(along(rows - d) + 2 * rows, n)
            handed.append(send(dst.at[slot], slot, partner, rsend.at[rows - 1 + d],
                               rrecv.at[rows - 1 + d]))
        for c in direct + relayed + [z_copy]:
            c.wait_send()
        for c in handed:
            c.wait()
        pair.wait()
        own.wait()

    anywhere = pl.BlockSpec(memory_space=pl.ANY)
    return pl.pallas_call(
        kernel,
        out_shape=jax.ShapeDtypeStruct((n,) + block.shape, block.dtype),
        in_specs=[anywhere],
        out_specs=anywhere,
        scratch_shapes=[
            pltpu.SemaphoreType.DMA((rows,)),
            pltpu.SemaphoreType.DMA((rows,)),
            pltpu.SemaphoreType.DMA((rows,)),
            pltpu.SemaphoreType.DMA((rows,)),
            pltpu.SemaphoreType.DMA((2 * rows - 1,)),
            pltpu.SemaphoreType.DMA((2 * rows - 1,)),
            pltpu.SemaphoreType.DMA((1,)),
            pltpu.SemaphoreType.DMA((1,)),
            pltpu.SemaphoreType.DMA((1,)),
            pltpu.SemaphoreType.DMA((1,)),
            pltpu.SemaphoreType.DMA((1,)),
        ],
        compiler_params=pltpu.CompilerParams(collective_id=cid, has_side_effects=True),
    )(block)


HIGH = lax.Precision.HIGHEST


def apply_rms_norm(input_float, norm_gain_vector, root_mean_square):
    if root_mean_square:
        input_normalized = input_float * lax.rsqrt(
            jnp.mean(input_float * input_float, axis=-1, keepdims=True) + 1e-06
        )
    else:
        mean_removed = input_float - jnp.mean(input_float, axis=-1, keepdims=True)
        input_normalized = mean_removed * lax.rsqrt(
            jnp.mean(mean_removed * mean_removed, axis=-1, keepdims=True) + 1e-05
        )
    return (input_normalized, (input_normalized * norm_gain_vector).astype(jnp.bfloat16))


def gelu_value(v):
    return 0.5 * v * (1.0 + lax.erf(v / math.sqrt(2.0)))


def gelu_slope(v):
    return 0.5 * (1.0 + lax.erf(v / math.sqrt(2.0))) + v * jnp.exp(-0.5 * v * v) / math.sqrt(
        2.0 * math.pi
    )


def pool_weights(ids):
    mask = (ids > 0).astype(jnp.float32)
    return mask / jnp.sum(mask, axis=-1, keepdims=True)


def tower_forward(tokens, ids, inner, gain, root_mean_square):
    count, length, width = tokens.shape
    input_float = tokens.astype(jnp.float32).reshape(count * length, width)
    input_normalized, normalized_rows = apply_rms_norm(input_float, gain, root_mean_square)
    pre = jnp.dot(normalized_rows, inner, preferred_element_type=jnp.float32)
    weights = pool_weights(ids)
    hidden = gelu_value(pre).reshape(count, length, -1)
    pooled = jnp.einsum("nt,ntf->nf", weights, hidden, precision=HIGH)
    resid = jnp.einsum(
        "nt,ntd->nd", weights, input_float.reshape(count, length, width), precision=HIGH
    )
    return input_normalized, normalized_rows, pre, weights, pooled, resid


def tower_backward(input_normalized, normalized_rows, pre, weights, inner, hidden_grad):
    count, length = weights.shape
    width = normalized_rows.shape[-1]
    slope = gelu_slope(pre).reshape(count, length, -1)
    dpre = (
        (weights[:, :, None] * hidden_grad[:, None, :] * slope)
        .reshape(count * length, -1)
        .astype(jnp.bfloat16)
    )
    high = lax.reduce_precision(input_normalized, exponent_bits=8, mantissa_bits=7)
    low = input_normalized - high
    rows = jnp.concatenate(
        [normalized_rows, high.astype(jnp.bfloat16), low.astype(jnp.bfloat16)], axis=1
    )
    both = lax.dot_general(
        dpre, rows, (((0,), (0,)), ((), ())), preferred_element_type=jnp.float32
    )
    inner_part = both[:, :width].T
    moment = both[:, width : 2 * width] + both[:, 2 * width :]
    gain_part = jnp.sum(inner.astype(jnp.float32).T * moment, axis=0)
    return inner_part, gain_part


def per_device(
    question_states,
    question_ids,
    q_inner_weight,
    q_outer_weight,
    q_norm_gain,
    sql_states,
    sql_ids,
    s_inner_weight,
    s_outer_weight,
    s_norm_gain,
    positive_column,
):
    scale = 1.0 / math.sqrt(D)
    q_place = lax.axis_index("sa")
    s_place = lax.axis_index("pb")
    q_tokens = plane_gather(question_states[0, 0], 5)
    s_tokens = lax.all_gather(sql_states, "pb", axis=1, tiled=True)[0]
    q_rows = q_tokens.shape[0]
    s_rows = s_tokens.shape[0]

    q_hat, q_normed, q_pre, q_weights, q_pooled, q_resid = tower_forward(
        q_tokens, question_ids[0], q_inner_weight, q_norm_gain, False
    )
    s_hat, s_normed, s_pre, s_weights, s_pooled, s_resid = tower_forward(
        s_tokens, sql_ids[0], s_inner_weight, s_norm_gain, True
    )
    q_outer_f = q_outer_weight.astype(jnp.float32)
    s_outer_f = s_outer_weight.astype(jnp.float32)
    q_terms = plane_gather(jnp.dot(q_pooled, q_outer_f, precision=HIGH), 1)
    q_block = jnp.sum(q_terms, axis=0) + q_resid
    q_embed, q_pooled_all, positive_all, s_terms = exchange(
        [
            (q_block, "pb", False),
            (q_pooled, "pb", False),
            (positive_column.reshape(1, -1), "pb", False),
            (jnp.dot(s_pooled, s_outer_f, precision=HIGH), "pb", False),
        ],
        2,
    )
    s_block = jnp.sum(s_terms, axis=0) + s_resid
    s_width = s_pooled.shape[-1]
    s_pack = jnp.concatenate(
        [s_block, s_pooled, jnp.zeros((s_block.shape[0], 128 - (D + s_width) % 128), jnp.float32)],
        axis=1,
    )
    s_pack = plane_gather(s_pack, 7)
    s_embed = s_pack[:, :, :D]
    s_pooled_all = s_pack[:, :, D : D + s_width]
    positive_all = positive_all.reshape(-1)
    q_embed = q_embed.reshape(-1, D)
    s_embed = s_embed.reshape(-1, D)
    q_pooled_all = q_pooled_all.reshape(-1, q_pooled.shape[-1])
    s_pooled_all = s_pooled_all.reshape(-1, s_pooled.shape[-1])
    score = scale * lax.dot_general(q_embed, s_embed, (((1,), (1,)), ((), ())), precision=HIGH)
    count = score.shape[0]
    match = (positive_all[:, None] == jnp.arange(count, dtype=jnp.int32)[None, :]).astype(
        jnp.float32
    )
    row_max = jnp.max(score, axis=1)
    row_lse = row_max + jnp.log(jnp.sum(jnp.exp(score - row_max[:, None]), axis=1))
    col_max = jnp.max(score, axis=0)
    col_lse = col_max + jnp.log(jnp.sum(jnp.exp(score - col_max[None, :]), axis=0))
    row_pos = jnp.sum(match * score, axis=1)
    col_pos = jnp.sum(match * score, axis=0)
    loss = (jnp.sum(row_lse - row_pos) + jnp.sum(col_lse - col_pos)) / (2.0 * count)
    dscore = 0.5 * (
        jnp.exp(score - row_lse[:, None]) + jnp.exp(score - col_lse[None, :]) - 2.0 * match
    )
    q_grad = scale * jnp.dot(dscore, s_embed, precision=HIGH)
    s_grad = scale * lax.dot_general(dscore, q_embed, (((0,), (0,)), ((), ())), precision=HIGH)

    q_outer_grad = lax.dot_general(q_pooled_all, q_grad, (((0,), (0,)), ((), ())), precision=HIGH)
    s_outer_grad = lax.dot_general(s_pooled_all, s_grad, (((0,), (0,)), ((), ())), precision=HIGH)
    q_grad_own = lax.dynamic_slice_in_dim(q_grad, s_place * q_rows, q_rows, 0)
    s_grad_own = lax.dynamic_slice_in_dim(s_grad, q_place * s_rows, s_rows, 0)
    q_hidden_grad = lax.dot_general(
        q_grad_own, q_outer_f, (((1,), (1,)), ((), ())), precision=HIGH
    )
    s_hidden_grad = lax.dot_general(
        s_grad_own, s_outer_f, (((1,), (1,)), ((), ())), precision=HIGH
    )
    q_inner_part, q_gain_part = tower_backward(
        q_hat, q_normed, q_pre, q_weights, q_inner_weight, q_hidden_grad
    )
    s_inner_part, s_gain_part = tower_backward(
        s_hat, s_normed, s_pre, s_weights, s_inner_weight, s_hidden_grad
    )
    q_pieces = q_inner_part.reshape(lax.axis_size("pb"), -1, 128)
    s_pieces = s_inner_part.reshape(lax.axis_size("sa"), -1, 128)
    gains = jnp.stack([q_gain_part, s_gain_part])
    q_pieces, s_pieces, gains = exchange(
        [
            (q_pieces.astype(jnp.bfloat16), "pb", True),
            (s_pieces.astype(jnp.bfloat16), "sa", True),
            (gains, "sa", False),
        ],
        3,
    )
    q_sums = jnp.sum(q_pieces.astype(jnp.float32), axis=0)
    s_sums = jnp.sum(s_pieces.astype(jnp.float32), axis=0)
    q_inner_grad, s_inner_grad, gains = exchange(
        [
            (q_sums.astype(jnp.bfloat16), "pb", False),
            (s_sums.astype(jnp.bfloat16), "sa", False),
            (jnp.sum(gains, axis=0), "pb", False),
        ],
        4,
    )
    q_inner_grad = q_inner_grad.astype(jnp.float32).reshape(q_inner_part.shape)
    s_inner_grad = s_inner_grad.astype(jnp.float32).reshape(s_inner_part.shape)
    gains = jnp.sum(gains, axis=0)
    q_gain_grad, s_gain_grad = gains[0], gains[1]
    return (loss, q_inner_grad, q_outer_grad, q_gain_grad, s_inner_grad, s_outer_grad, s_gain_grad)


def solution(mesh):
    placed = (
        P("pb", "sa", None, None),
        P("pb", None, None),
        P(None, "sa"),
        P("sa", None),
        P(),
        P("sa", "pb", None, None),
        P("sa", None, None),
        P(None, "pb"),
        P("pb", None),
        P(),
        P("pb"),
    )
    return jax.shard_map(
        per_device,
        mesh=mesh,
        in_specs=placed,
        out_specs=(P(), P(None, "sa"), P("sa", None), P(), P(None, "pb"), P("pb", None), P()),
        check_vma=False,
    )
```

```python
import functools
import math

import jax
import jax.numpy as jnp
from jax import lax
from jax.experimental import pallas as pl
from jax.experimental.pallas import tpu as pltpu
from jax.sharding import PartitionSpec as P

D = 768

MESH_AXES = ("pb", "sa")


def _peer(axis, p):
    return tuple(p if a == axis else lax.axis_index(a) for a in MESH_AXES)


def exchange(jobs, cid):
    arrays = [a for a, _, _ in jobs]
    kinds = [(ax, spread) for _, ax, spread in jobs]
    sizes = {ax: lax.axis_size(ax) for ax, _ in kinds}
    widest = max(sizes.values())
    count = len(jobs)

    def kernel(*refs):
        srcs, dsts = refs[:count], refs[count:2 * count]
        send, recv, local = refs[2 * count:]
        barrier = pltpu.get_barrier_semaphore()
        axes = list(dict.fromkeys(ax for ax, _ in kinds))
        total = 0
        for ax in axes:
            n = sizes[ax]
            me = lax.axis_index(ax)
            for s in range(1, n):
                pl.semaphore_signal(barrier, 1, device_id=_peer(ax, lax.rem(me + s, n)),
                                    device_id_type=pl.DeviceIdType.MESH)
            total += n - 1
        pl.semaphore_wait(barrier, total)
        started = []
        for t, (ax, spread) in enumerate(kinds):
            n = sizes[ax]
            me = lax.axis_index(ax)
            for s in range(1, n):
                p = lax.rem(me + s, n)
                src = srcs[t].at[p] if spread else srcs[t]
                c = pltpu.make_async_remote_copy(
                    src_ref=src, dst_ref=dsts[t].at[me], send_sem=send.at[t, s],
                    recv_sem=recv.at[t, s], device_id=_peer(ax, p),
                    device_id_type=pl.DeviceIdType.MESH)
                c.start()
                started.append(c)
            src = srcs[t].at[me] if spread else srcs[t]
            c = pltpu.make_async_copy(src, dsts[t].at[me], local.at[t])
            c.start()
            started.append(c)
        for c in started:
            c.wait()

    out_shape = []
    for a, (ax, spread) in zip(arrays, kinds):
        shape = a.shape if spread else (sizes[ax],) + a.shape
        out_shape.append(jax.ShapeDtypeStruct(shape, a.dtype))
    anywhere = pl.BlockSpec(memory_space=pl.ANY)
    return pl.pallas_call(
        kernel,
        out_shape=out_shape,
        in_specs=[anywhere] * count,
        out_specs=[anywhere] * count,
        scratch_shapes=[
            pltpu.SemaphoreType.DMA((count, widest)),
            pltpu.SemaphoreType.DMA((count, widest)),
            pltpu.SemaphoreType.DMA((count,)),
        ],
        compiler_params=pltpu.CompilerParams(collective_id=cid, has_side_effects=True),
    )(*arrays)


def plane_gather(block, cid):
    n = lax.axis_size("sa")
    rows = n // 4
    mesh_kind = pl.DeviceIdType.MESH

    def kernel(src, dst, ysend, yrecv, fsend, frecv, rsend, rrecv, zsend, zrecv, psend, precv, local):
        me = lax.axis_index("sa")
        core = lax.rem(me, 2)
        row = lax.rem(me // 2, rows)
        plane = me // (2 * rows)
        partner = me + 1 - 2 * core
        across = lax.rem(me + 2 * rows, n)

        def along(d):
            return plane * 2 * rows + lax.rem(row + d, rows) * 2 + core

        barrier = pltpu.get_barrier_semaphore()
        for peer in [partner, across] + [along(d) for d in range(1, rows)]:
            pl.semaphore_signal(barrier, 1, device_id=_peer("sa", peer), device_id_type=mesh_kind)
        pl.semaphore_wait(barrier, rows + 1)

        def send(source, slot, peer, s, r):
            c = pltpu.make_async_remote_copy(
                src_ref=source, dst_ref=dst.at[slot], send_sem=s, recv_sem=r,
                device_id=_peer("sa", peer), device_id_type=mesh_kind)
            c.start()
            return c

        own = pltpu.make_async_copy(src, dst.at[me], local.at[0])
        own.start()
        z_copy = send(src, me, across, zsend.at[0], zrecv.at[0])
        pair = send(src, me, partner, psend.at[0], precv.at[0])
        direct = [send(src, me, along(d), ysend.at[d], yrecv.at[d]) for d in range(1, rows)]
        z_copy.wait_recv()
        far = lax.rem(me + 2 * rows, n)
        relayed = [send(dst.at[far], far, along(d), fsend.at[d], frecv.at[d]) for d in range(1, rows)]
        handed = [send(dst.at[far], far, partner, rsend.at[0], rrecv.at[0])]
        for d in range(1, rows):
            direct[d - 1].wait_recv()
            slot = along(rows - d)
            handed.append(send(dst.at[slot], slot, partner, rsend.at[d], rrecv.at[d]))
        for d in range(1, rows):
            relayed[d - 1].wait_recv()
            slot = lax.rem(along(rows - d) + 2 * rows, n)
            handed.append(send(dst.at[slot], slot, partner, rsend.at[rows - 1 + d],
                               rrecv.at[rows - 1 + d]))
        for c in direct + relayed + [z_copy]:
            c.wait_send()
        for c in handed:
            c.wait()
        pair.wait()
        own.wait()

    anywhere = pl.BlockSpec(memory_space=pl.ANY)
    return pl.pallas_call(
        kernel,
        out_shape=jax.ShapeDtypeStruct((n,) + block.shape, block.dtype),
        in_specs=[anywhere],
        out_specs=anywhere,
        scratch_shapes=[
            pltpu.SemaphoreType.DMA((rows,)),
            pltpu.SemaphoreType.DMA((rows,)),
            pltpu.SemaphoreType.DMA((rows,)),
            pltpu.SemaphoreType.DMA((rows,)),
            pltpu.SemaphoreType.DMA((2 * rows - 1,)),
            pltpu.SemaphoreType.DMA((2 * rows - 1,)),
            pltpu.SemaphoreType.DMA((1,)),
            pltpu.SemaphoreType.DMA((1,)),
            pltpu.SemaphoreType.DMA((1,)),
            pltpu.SemaphoreType.DMA((1,)),
            pltpu.SemaphoreType.DMA((1,)),
        ],
        compiler_params=pltpu.CompilerParams(collective_id=cid, has_side_effects=True),
    )(block)


HIGH = lax.Precision.HIGHEST


def apply_rms_norm(input_float, norm_gain_vector, root_mean_square):
    if root_mean_square:
        input_normalized = input_float * lax.rsqrt(
            jnp.mean(input_float * input_float, axis=-1, keepdims=True) + 1e-06
        )
    else:
        mean_removed = input_float - jnp.mean(input_float, axis=-1, keepdims=True)
        input_normalized = mean_removed * lax.rsqrt(
            jnp.mean(mean_removed * mean_removed, axis=-1, keepdims=True) + 1e-05
        )
    return (input_normalized, (input_normalized * norm_gain_vector).astype(jnp.bfloat16))


def gelu_value(v):
    return 0.5 * v * (1.0 + lax.erf(v / math.sqrt(2.0)))


def gelu_slope(v):
    return 0.5 * (1.0 + lax.erf(v / math.sqrt(2.0))) + v * jnp.exp(-0.5 * v * v) / math.sqrt(
        2.0 * math.pi
    )


def pool_weights(ids):
    mask = (ids > 0).astype(jnp.float32)
    return mask / jnp.sum(mask, axis=-1, keepdims=True)


def tower_forward(tokens, ids, inner, gain, root_mean_square):
    count, length, width = tokens.shape
    input_float = tokens.astype(jnp.float32).reshape(count * length, width)
    input_normalized, normalized_rows = apply_rms_norm(input_float, gain, root_mean_square)
    pre = jnp.dot(normalized_rows, inner, preferred_element_type=jnp.float32)
    weights = pool_weights(ids)
    hidden = gelu_value(pre).reshape(count, length, -1)
    pooled = jnp.einsum("nt,ntf->nf", weights, hidden, precision=HIGH)
    resid = jnp.einsum(
        "nt,ntd->nd", weights, input_float.reshape(count, length, width), precision=HIGH
    )
    return input_normalized, normalized_rows, pre, weights, pooled, resid


def tower_backward(input_normalized, normalized_rows, pre, weights, inner, hidden_grad):
    count, length = weights.shape
    width = normalized_rows.shape[-1]
    slope = gelu_slope(pre).reshape(count, length, -1)
    dpre = (
        (weights[:, :, None] * hidden_grad[:, None, :] * slope)
        .reshape(count * length, -1)
        .astype(jnp.bfloat16)
    )
    high = lax.reduce_precision(input_normalized, exponent_bits=8, mantissa_bits=7)
    low = input_normalized - high
    rows = jnp.concatenate(
        [normalized_rows, high.astype(jnp.bfloat16), low.astype(jnp.bfloat16)], axis=1
    )
    both = lax.dot_general(
        dpre, rows, (((0,), (0,)), ((), ())), preferred_element_type=jnp.float32
    )
    inner_part = both[:, :width].T
    moment = both[:, width : 2 * width] + both[:, 2 * width :]
    gain_part = jnp.sum(inner.astype(jnp.float32).T * moment, axis=0)
    return inner_part, gain_part


def per_device(
    question_states,
    question_ids,
    q_inner_weight,
    q_outer_weight,
    q_norm_gain,
    sql_states,
    sql_ids,
    s_inner_weight,
    s_outer_weight,
    s_norm_gain,
    positive_column,
):
    scale = 1.0 / math.sqrt(D)
    q_place = lax.axis_index("sa")
    s_place = lax.axis_index("pb")
    q_tokens = plane_gather(question_states[0, 0], 5)
    s_tokens = lax.all_gather(sql_states, "pb", axis=1, tiled=True)[0]
    q_rows = q_tokens.shape[0]
    s_rows = s_tokens.shape[0]

    q_hat, q_normed, q_pre, q_weights, q_pooled, q_resid = tower_forward(
        q_tokens, question_ids[0], q_inner_weight, q_norm_gain, False
    )
    s_hat, s_normed, s_pre, s_weights, s_pooled, s_resid = tower_forward(
        s_tokens, sql_ids[0], s_inner_weight, s_norm_gain, True
    )
    q_outer_f = q_outer_weight.astype(jnp.float32)
    s_outer_f = s_outer_weight.astype(jnp.float32)
    q_terms = plane_gather(jnp.dot(q_pooled, q_outer_f, precision=HIGH), 1)
    q_block = jnp.sum(q_terms, axis=0) + q_resid
    q_embed, q_pooled_all, positive_all, s_terms = exchange(
        [
            (q_block, "pb", False),
            (q_pooled.reshape(-1, 128), "pb", False),
            (positive_column.reshape(1, -1), "pb", False),
            (jnp.dot(s_pooled, s_outer_f, precision=HIGH), "pb", False),
        ],
        2,
    )
    s_block = jnp.sum(s_terms, axis=0) + s_resid
    s_width = s_pooled.shape[-1]
    s_pack = jnp.concatenate(
        [s_block, s_pooled, jnp.zeros((s_block.shape[0], 128 - (D + s_width) % 128), jnp.float32)],
        axis=1,
    )
    s_pack = plane_gather(s_pack, 7)
    s_embed = s_pack[:, :, :D]
    s_pooled_all = s_pack[:, :, D : D + s_width]
    positive_all = positive_all.reshape(-1)
    q_embed = q_embed.reshape(-1, D)
    s_embed = s_embed.reshape(-1, D)
    q_pooled_all = q_pooled_all.reshape(-1, q_pooled.shape[-1])
    s_pooled_all = s_pooled_all.reshape(-1, s_pooled.shape[-1])
    score = scale * lax.dot_general(q_embed, s_embed, (((1,), (1,)), ((), ())), precision=HIGH)
    count = score.shape[0]
    match = (positive_all[:, None] == jnp.arange(count, dtype=jnp.int32)[None, :]).astype(
        jnp.float32
    )
    row_max = jnp.max(score, axis=1)
    row_lse = row_max + jnp.log(jnp.sum(jnp.exp(score - row_max[:, None]), axis=1))
    col_max = jnp.max(score, axis=0)
    col_lse = col_max + jnp.log(jnp.sum(jnp.exp(score - col_max[None, :]), axis=0))
    row_pos = jnp.sum(match * score, axis=1)
    col_pos = jnp.sum(match * score, axis=0)
    loss = (jnp.sum(row_lse - row_pos) + jnp.sum(col_lse - col_pos)) / (2.0 * count)
    dscore = 0.5 * (
        jnp.exp(score - row_lse[:, None]) + jnp.exp(score - col_lse[None, :]) - 2.0 * match
    )
    q_grad = scale * jnp.dot(dscore, s_embed, precision=HIGH)
    s_grad = scale * lax.dot_general(dscore, q_embed, (((0,), (0,)), ((), ())), precision=HIGH)

    q_outer_grad = lax.dot_general(q_pooled_all, q_grad, (((0,), (0,)), ((), ())), precision=HIGH)
    s_outer_grad = lax.dot_general(s_pooled_all, s_grad, (((0,), (0,)), ((), ())), precision=HIGH)
    q_grad_own = lax.dynamic_slice_in_dim(q_grad, s_place * q_rows, q_rows, 0)
    s_grad_own = lax.dynamic_slice_in_dim(s_grad, q_place * s_rows, s_rows, 0)
    q_hidden_grad = lax.dot_general(
        q_grad_own, q_outer_f, (((1,), (1,)), ((), ())), precision=HIGH
    )
    s_hidden_grad = lax.dot_general(
        s_grad_own, s_outer_f, (((1,), (1,)), ((), ())), precision=HIGH
    )
    q_inner_part, q_gain_part = tower_backward(
        q_hat, q_normed, q_pre, q_weights, q_inner_weight, q_hidden_grad
    )
    s_inner_part, s_gain_part = tower_backward(
        s_hat, s_normed, s_pre, s_weights, s_inner_weight, s_hidden_grad
    )
    q_pieces = q_inner_part.reshape(lax.axis_size("pb"), -1, 128)
    s_pieces = s_inner_part.reshape(lax.axis_size("sa"), -1, 128)
    gains = jnp.stack([q_gain_part, s_gain_part])
    q_pieces, s_pieces, gains = exchange(
        [
            (q_pieces.astype(jnp.bfloat16), "pb", True),
            (s_pieces.astype(jnp.bfloat16), "sa", True),
            (gains, "sa", False),
        ],
        3,
    )
    q_sums = jnp.sum(q_pieces.astype(jnp.float32), axis=0)
    s_sums = jnp.sum(s_pieces.astype(jnp.float32), axis=0)
    q_inner_grad, s_inner_grad, gains = exchange(
        [
            (q_sums.astype(jnp.bfloat16), "pb", False),
            (s_sums.astype(jnp.bfloat16), "sa", False),
            (jnp.sum(gains, axis=0), "pb", False),
        ],
        4,
    )
    q_inner_grad = q_inner_grad.astype(jnp.float32).reshape(q_inner_part.shape)
    s_inner_grad = s_inner_grad.astype(jnp.float32).reshape(s_inner_part.shape)
    gains = jnp.sum(gains, axis=0)
    q_gain_grad, s_gain_grad = gains[0], gains[1]
    return (loss, q_inner_grad, q_outer_grad, q_gain_grad, s_inner_grad, s_outer_grad, s_gain_grad)


def solution(mesh):
    placed = (
        P("pb", "sa", None, None),
        P("pb", None, None),
        P(None, "sa"),
        P("sa", None),
        P(),
        P("sa", "pb", None, None),
        P("sa", None, None),
        P(None, "pb"),
        P("pb", None),
        P(),
        P("pb"),
    )
    return jax.shard_map(
        per_device,
        mesh=mesh,
        in_specs=placed,
        out_specs=(P(), P(None, "sa"), P("sa", None), P(), P(None, "pb"), P("pb", None), P()),
        check_vma=False,
    )
```
